256 devices in a mesh: gx: 16 (over y, z_lo), gy: 16 (over z_hi, x, core).
Axes of the slice: x: 4, y: 4, z: 8 (z_hi: 2, z_lo: 4; z = z_hi * 4 + z_lo), core: 2. Of those that a mesh axis runs over, the one named last changes fastest.
Arguments:
- object_field: float32 [2, 8192, 8192], P(None, 'gy', 'gx'), may hold values from -6 to 6
- probe_field: float32 [2, 256, 256], replicated, may hold values from -5 to 5
- measured: float32 [16, 16, 4, 256, 256], P('gy', 'gx'), may hold values from 0 to 2.5
- offsets: int32 [16, 16, 4, 2], P('gy', 'gx'), may hold values from 0 to 512
- counts: int32 [16, 16], P('gy', 'gx'), may hold values from 1 to 4
Outputs:
- updated_object: float32 [2, 8192, 8192], P(None, 'gy', 'gx')
The draws below stay inside these ranges and needn't reach their ends.
Inputs may be any that keep to these rules, and one draw needn't show every extreme that they name: `offsets`: A window lies within its tile and the 128 cells around it. Windows 0 to counts - 1 of a tile are live, the others unused.
All inputs are finite; a program needn't handle non-finite values.
Results may differ from the reference program's by a relative error of at most 0.0055.
Values sent between devices are 32-bit elements; how exact they have to be, the bound alone decides.
No kernel may reach another device: no remote copies, remote signals or barrier semaphores. Data moves between devices by JAX's collectives and lax.ppermute only.
A program may use at most 128 MiB of HBM per device.

```python
import math
import jax
import jax.numpy as jnp
from jax import lax

P_SIZE = 256
TILE = 512
WIN = 4
ITERS = 2
MARGIN = 128
NROWS = 8192
NCOLS = 8192
N_GX = 16
N_GY = 16


def plant(drawn, key, least, high):
    place = [jax.random.randint(jax.random.fold_in(key, axis), (), 0, length) for axis, length in enumerate(drawn.shape)]
    widest = drawn.shape.index(max(drawn.shape))
    beside = place[:widest] + [(place[widest] + 1) % drawn.shape[widest]] + place[widest + 1:]
    return drawn.at[tuple(place)].set(least).at[tuple(beside)].set(high)


def level_of(own_key, shape, cuts, low, high):
    gain = 1.0
    for dim, parts in cuts:
        draws = jax.random.uniform(jax.random.fold_in(jax.random.fold_in(own_key, 6), dim), (parts,), jnp.float32, low / len(cuts), high / len(cuts))
        gain = gain * jnp.repeat(jnp.exp(draws), shape[dim] // parts).reshape((-1,) + (1,) * (len(shape) - 1 - dim))
    return gain


def gaussian(own_key, dims, spread, bound, cuts=(), kind=jnp.bfloat16):
    values = jax.random.normal(own_key, dims, jnp.float32) * spread
    if len(cuts) > 0:
        values = level_of(own_key, dims, cuts, -0.22, 0.18) * values
    return jnp.clip(values, min=-bound, max=bound).astype(kind)


def setup_inputs(seed: int = 0) -> dict:
    key_of = jax.random.split(jax.random.key(seed), 6)
    object_field = gaussian(key_of[0], (2, NROWS, NCOLS), 1.0, 6.0, ((1, 16), (2, 16)), jnp.float32)
    probe_field = gaussian(key_of[1], (2, P_SIZE, P_SIZE), 1.0, 5.0, (), jnp.float32)
    measured = jnp.clip(2.5 * jax.random.uniform(key_of[2], (N_GY, N_GX, WIN, P_SIZE, P_SIZE), jnp.float32) ** level_of(key_of[2], (N_GY, N_GX, WIN, P_SIZE, P_SIZE), ((0, 16), (1, 16)), -0.2, 0.2), 0.0, 2.5)
    offsets = plant(jax.random.randint(key_of[3], (N_GY, N_GX, WIN, 2), 0, TILE + 1), jax.random.fold_in(key_of[3], 1), 0, TILE).astype(jnp.int32)
    counts = plant(jax.random.randint(key_of[4], (N_GY, N_GX), 1, WIN + 1), jax.random.fold_in(key_of[4], 1), 1, WIN).astype(jnp.int32)
    return dict(object_field=object_field, probe_field=probe_field, measured=measured, offsets=offsets, counts=counts)


step_size = 0.25
amplitude_floor = 0.5

def tables(window_side):
    indices = jnp.arange(window_side, dtype=jnp.int32)
    phases = (indices[:, None] * indices[None, :] % window_side).astype(jnp.float32) * (2.0 * math.pi / window_side)
    norm_scale = 1.0 / math.sqrt(window_side)
    return ((jnp.cos(phases) * norm_scale).astype(jnp.bfloat16), (jnp.sin(phases) * norm_scale).astype(jnp.bfloat16))

def left_product(matrix, stacked):
    return jnp.einsum('ik,wkj->wij', matrix.astype(jnp.float32), stacked.astype(jnp.float32))

def right_product(stacked, matrix):
    return jnp.einsum('wik,kj->wij', stacked.astype(jnp.float32), matrix.astype(jnp.float32))

def transform(real_part, imag_part, cosine_table, sines_signed):
    half_real = (left_product(cosine_table, real_part) - left_product(sines_signed, imag_part)).astype(jnp.bfloat16)
    half_imag = (left_product(cosine_table, imag_part) + left_product(sines_signed, real_part)).astype(jnp.bfloat16)
    far_real = right_product(half_real, cosine_table) - right_product(half_imag, sines_signed)
    far_imag = right_product(half_real, sines_signed) + right_product(half_imag, cosine_table)
    return (far_real, far_imag)

def window_gradient(patches, probe_field, amplitudes, cosine_table, sine_table):
    probe_real, probe_imag = (probe_field[0], probe_field[1])
    patch_real, patch_imag = (patches[:, 0], patches[:, 1])
    exit_real = (probe_real * patch_real - probe_imag * patch_imag).astype(jnp.bfloat16)
    exit_imag = (probe_real * patch_imag + probe_imag * patch_real).astype(jnp.bfloat16)
    far_real, far_imag = transform(exit_real, exit_imag, cosine_table, -sine_table)
    modulus = jnp.sqrt(far_real * far_real + far_imag * far_imag)
    factor = 1.0 - amplitudes / jnp.maximum(modulus, amplitude_floor)
    back_real, back_imag = transform((far_real * factor).astype(jnp.bfloat16), (far_imag * factor).astype(jnp.bfloat16), cosine_table, sine_table)
    return jnp.stack((probe_real * back_real + probe_imag * back_imag, probe_real * back_imag - probe_imag * back_real), axis=1)

def reference(object_field, probe_field, measured, offsets, counts):
    cosine_table, sine_table = tables(P_SIZE)
    amplitudes = measured.reshape(N_GY * N_GX, WIN, P_SIZE, P_SIZE)
    starts = offsets.reshape(N_GY * N_GX, WIN, 2)
    live_counts = counts.reshape(N_GY * N_GX)
    for iteration in range(ITERS):
        padded = jnp.pad(object_field, ((0, 0), (MARGIN, MARGIN), (MARGIN, MARGIN)))

        def tile_step(gradient, tile_index):
            tile_row = tile_index // N_GX * TILE
            tile_col = tile_index % N_GX * TILE
            corner = starts[tile_index]
            patches = jax.vmap(lambda window_start: lax.dynamic_slice(padded, (jnp.int32(0), tile_row + window_start[0], tile_col + window_start[1]), (2, P_SIZE, P_SIZE)))(corner)
            live_mask = (jnp.arange(WIN, dtype=jnp.int32) < live_counts[tile_index]).astype(jnp.float32)
            contributions = window_gradient(patches, probe_field, amplitudes[tile_index], cosine_table, sine_table) * live_mask[:, None, None, None]

            def deposit(window, total):
                row_start = tile_row + corner[window, 0]
                col_start = tile_col + corner[window, 1]
                current = lax.dynamic_slice(total, (jnp.int32(0), row_start, col_start), (2, P_SIZE, P_SIZE))
                return lax.dynamic_update_slice(total, current + contributions[window], (jnp.int32(0), row_start, col_start))
            return (lax.fori_loop(0, WIN, deposit, gradient), None)
        gradient, _ = lax.scan(tile_step, jnp.zeros_like(padded), jnp.arange(N_GY * N_GX, dtype=jnp.int32))
        object_field = object_field - step_size * gradient[:, MARGIN:MARGIN + NROWS, MARGIN:MARGIN + NCOLS]
    return object_field
```

```python
import functools
import math

import jax
import jax.numpy as jnp
from jax import lax
from jax.experimental import pallas as pl
from jax.experimental.pallas import tpu as pltpu
from jax.sharding import PartitionSpec as P

ITERS = 2
step_size = 0.25
amplitude_floor = 0.5

MIB = 1 << 20

GX_ODD, GY_ODD, EDGE, LIVE, OFFS = 0, 1, 2, 3, 4


def pairs(count, first):
    ups = [(i, i + 1) for i in range(first, count - 1, 2)]
    return ups + [(b, a) for a, b in ups]


def swap(odd_cells, even_cells, axis):
    count = lax.axis_size(axis)
    from_odd = lax.ppermute(odd_cells, axis, pairs(count, 1))
    from_even = lax.ppermute(even_cells, axis, pairs(count, 0))
    return from_odd, from_even


def dot(a, b):
    return jnp.dot(a, b, preferred_element_type=jnp.float32)


def table_blocks(shift, half, side):
    rows = lax.broadcasted_iota(jnp.int32, (half, half), 0)
    cols = lax.broadcasted_iota(jnp.int32, (half, half), 1)
    scale = 2.0 * math.pi / side
    norm = 1.0 / math.sqrt(side)

    def entries(freq, cell):
        phase = (freq * (cell - shift + side)) & (side - 1)
        angle = phase.astype(jnp.float32) * scale
        return jnp.cos(angle) * norm, jnp.sin(angle) * norm

    out = []
    for odd in (0, 1):
        c, s = entries(2 * rows + odd, cols)
        ct, st = entries(2 * cols + odd, rows)
        out.append((c, s, ct, st))
    return out


def prepare_kernel(side, windows, meta, probe, measured, probes, tables, amps):
    half = side // 2
    bf = jnp.bfloat16
    rows = lax.broadcasted_iota(jnp.int32, (side, side), 0)
    cols = lax.broadcasted_iota(jnp.int32, (side, side), 1)
    place = jnp.where(cols < half, 2 * cols, 2 * (cols - half) + 1)
    picks = (rows == place).astype(jnp.float32).astype(bf)
    place_t = jnp.where(rows < half, 2 * rows, 2 * (rows - half) + 1)
    picks_t = (cols == place_t).astype(jnp.float32).astype(bf)

    def parts(x):
        high = x.astype(bf)
        rest = x - high.astype(jnp.float32)
        mid = rest.astype(bf)
        low = (rest - mid.astype(jnp.float32)).astype(bf)
        return high, mid, low

    def body(w, _):
        row = meta[OFFS + 2 * w] & (side - 1)
        col = meta[OFFS + 2 * w + 1] & (side - 1)
        for part in (0, 1):
            turned = pltpu.roll(probe[part], row, 0)
            probes[w, part] = pltpu.roll(turned, col, 1)
        for axis, shift in ((0, row), (1, col)):
            for odd, (c, s, ct, st) in enumerate(table_blocks(shift, half, side)):
                at = 4 * axis + 2 * odd
                tables[w, at, :half, :half] = c.astype(bf)
                tables[w, at, :half, half:] = s.astype(bf)
                tables[w, at, half:, :half] = (-s).astype(bf)
                tables[w, at, half:, half:] = c.astype(bf)
                tables[w, at + 1, :half, :half] = ct.astype(bf)
                tables[w, at + 1, :half, half:] = (-st).astype(bf)
                tables[w, at + 1, half:, :half] = st.astype(bf)
                tables[w, at + 1, half:, half:] = ct.astype(bf)
        a = [dot(x, picks) for x in parts(measured[w])]
        b = [dot(picks_t, x) for x in parts(a[0] + (a[1] + a[2]))]
        amps[w] = b[0] + (b[1] + b[2])
        return 0

    lax.fori_loop(0, windows, body, 0)


def gradient_kernel(
    side,
    windows,
    meta,
    centre,
    halo_odd,
    halo_even,
    probes,
    tables,
    amps,
    grad,
    rim_odd,
    rim_even,
    field,
    total,
    mixed,
):
    half = side // 2
    tile = centre.shape[1]
    bf = jnp.bfloat16
    odd_row = meta[GY_ODD]
    top, bottom = 0, half + tile
    at_odd = pl.multiple_of(odd_row * bottom, half)
    at_even = pl.multiple_of((1 - odd_row) * bottom, half)
    field[:, pl.ds(half, tile), :] = centre[...]
    field[:, pl.ds(at_odd, half), :] = halo_odd[...]
    field[:, pl.ds(at_even, half), :] = halo_even[...]
    total[...] = jnp.zeros_like(total)
    chunk = 32
    zero = jnp.float32(0)

    for w in range(windows):
        a, b = meta[OFFS + 2 * w], meta[OFFS + 2 * w + 1]
        live = w < meta[LIVE]
        hi_a, hi_b = (a >= side).astype(jnp.int32), (b >= side).astype(jnp.int32)
        row0, col0 = pl.multiple_of(hi_a * side, side), pl.multiple_of(hi_b * side, side)
        row_in, col_in = a - row0, b - col0
        near = lax.broadcasted_iota(jnp.int32, (chunk, side), 1) >= col_in

        def below(start):
            return (lax.broadcasted_iota(jnp.int32, (chunk, side), 0) + start) >= row_in

        def patch(part, start):
            def at(i, j):
                return field[
                    part,
                    pl.ds(pl.multiple_of(row0 + i * side + start, chunk), chunk),
                    pl.ds(pl.multiple_of(col0 + j * side, side), side),
                ]

            return jnp.where(
                below(start),
                jnp.where(near, at(0, 0), at(0, 1)),
                jnp.where(near, at(1, 0), at(1, 1)),
            )

        def exits(start):
            real, imag = patch(0, start), patch(1, start)
            p_real = probes[w, 0, pl.ds(start, chunk), :]
            p_imag = probes[w, 1, pl.ds(start, chunk), :]
            return p_real * real - p_imag * imag, p_real * imag + p_imag * real

        for i in range(0, half, chunk):
            r0, i0 = exits(i)
            r1, i1 = exits(half + i)
            mixed[0, i : i + chunk, :] = (r0 + r1).astype(bf)
            mixed[0, half + i : half + i + chunk, :] = (i0 + i1).astype(bf)
            mixed[1, i : i + chunk, :] = (r0 - r1).astype(bf)
            mixed[1, half + i : half + i + chunk, :] = (i0 - i1).astype(bf)

        plus, minus = [], []
        for odd in (0, 1):
            h = dot(tables[w, 2 * odd], mixed[odd])
            re0, re1 = h[:half, :half], h[:half, half:]
            im0, im1 = h[half:, :half], h[half:, half:]
            plus.append(jnp.concatenate([re0 + re1, im0 + im1], axis=1).astype(bf))
            minus.append(jnp.concatenate([re0 - re1, im0 - im1], axis=1).astype(bf))

        backs = []
        for odd, sides in ((0, plus), (1, minus)):
            far = dot(jnp.concatenate(sides, axis=0), tables[w, 4 + 2 * odd + 1])
            re, im = far[:, :half], far[:, half:]
            power = jnp.maximum(re * re + im * im, amplitude_floor * amplitude_floor)
            factor = 1.0 - amps[w, :, odd * half : (odd + 1) * half] * lax.rsqrt(power)
            chi = jnp.concatenate([re * factor, im * factor], axis=1).astype(bf)
            backs.append(dot(chi, tables[w, 4 + 2 * odd]))
        left, right = backs[0] + backs[1], backs[0] - backs[1]

        outs = []
        for odd in (0, 1):
            at = slice(odd * half, (odd + 1) * half)
            real = jnp.concatenate([left[at, :half], right[at, :half]], axis=1)
            imag = jnp.concatenate([left[at, half:], right[at, half:]], axis=1)
            stacked = jnp.concatenate([real, imag], axis=0).astype(bf)
            outs.append(dot(tables[w, 2 * odd + 1], stacked))
        upper, lower = outs[0] + outs[1], outs[0] - outs[1]

        for start in range(0, side, chunk):
            back = upper if start < half else lower
            at = start % half
            b_real, b_imag = back[at : at + chunk], back[half + at : half + at + chunk]
            p_real = probes[w, 0, pl.ds(start, chunk), :]
            p_imag = probes[w, 1, pl.ds(start, chunk), :]
            terms = (p_real * b_real + p_imag * b_imag, p_real * b_imag - p_imag * b_real)
            rows_in = below(start)
            for part in (0, 1):
                for i, j in ((0, 0), (0, 1), (1, 0), (1, 1)):
                    keep = (rows_in if i == 0 else ~rows_in) & (near if j == 0 else ~near)
                    place = (
                        part,
                        pl.ds(pl.multiple_of(row0 + i * side + start, chunk), chunk),
                        pl.ds(pl.multiple_of(col0 + j * side, side), side),
                    )
                    total[place] = total[place] + jnp.where(keep & live, terms[part], zero)

    grad[...] = total[:, pl.ds(half, tile), :]
    rim_odd[...] = total[:, pl.ds(at_odd, half), :]
    rim_even[...] = total[:, pl.ds(at_even, half), :]


def row_places(meta, half, tile):
    odd_row = meta[GY_ODD]
    far = tile - half
    return pl.multiple_of(odd_row * far, half), pl.multiple_of((1 - odd_row) * far, half)


def assemble_kernel(meta, own, halo_odd, halo_even, centre, rim_odd, rim_even):
    tile, half = own.shape[1], halo_odd.shape[2]
    odd_col = meta[GX_ODD]
    beyond = half + tile
    centre[:, :, half : half + tile] = own[...]
    centre[:, :, pl.ds(pl.multiple_of(odd_col * beyond, half), half)] = halo_odd[...]
    centre[:, :, pl.ds(pl.multiple_of((1 - odd_col) * beyond, half), half)] = halo_even[...]
    at_odd, at_even = row_places(meta, half, tile)
    rim_odd[...] = centre[:, pl.ds(at_odd, half), :]
    rim_even[...] = centre[:, pl.ds(at_even, half), :]


def bands_kernel(width, meta, grad, rim_odd, rim_even, band_odd, band_even):
    tile, half = grad.shape[1], rim_odd.shape[1]
    odd_col = meta[GX_ODD]
    last = grad.shape[2] - width
    at_odd, at_even = row_places(meta, half, tile)
    for band, place in ((band_odd, odd_col * last), (band_even, (1 - odd_col) * last)):
        cols = pl.ds(pl.multiple_of(place, 128), width)
        band[...] = grad[:, :, cols]
        for at, rim in ((at_odd, rim_odd), (at_even, rim_even)):
            rows = pl.ds(at, half)
            band[:, rows, :] = band[:, rows, :] + rim[:, :, cols]


def update_kernel(meta, centre, grad, rim_odd, rim_even, band_odd, band_even, fresh, out_odd, out_even):
    tile, half = grad.shape[1], rim_odd.shape[1]
    odd_col = meta[GX_ODD]
    width = band_odd.shape[2]
    last = grad.shape[2] - width
    at_odd, at_even = row_places(meta, half, tile)
    fresh[...] = centre[...] - step_size * grad[...]
    for at, rim in ((at_odd, rim_odd), (at_even, rim_even)):
        rows = pl.ds(at, half)
        fresh[:, rows, :] = fresh[:, rows, :] - step_size * rim[...]
    for place, band in ((odd_col * last, band_odd), ((1 - odd_col) * last, band_even)):
        cols = pl.ds(pl.multiple_of(place, 128), width)
        fresh[:, :, cols] = fresh[:, :, cols] - step_size * band[...]

    @pl.when(meta[EDGE] == 1)
    def _():
        outside = pl.ds(pl.multiple_of(odd_col * (half + tile), half), half)
        fresh[:, :, outside] = jnp.zeros((2, tile, half), jnp.float32)

    out_odd[...] = fresh[:, pl.ds(at_odd, half), :]
    out_even[...] = fresh[:, pl.ds(at_even, half), :]


def final_kernel(meta, centre, grad, rim_odd, rim_even, band_odd, band_even, out):
    tile, half = grad.shape[1], rim_odd.shape[1]
    odd_col = meta[GX_ODD]
    last = tile - half
    at_odd, at_even = row_places(meta, half, tile)
    own = slice(half, half + tile)
    out[...] = centre[:, :, own] - step_size * grad[:, :, own]
    for at, rim in ((at_odd, rim_odd), (at_even, rim_even)):
        rows = pl.ds(at, half)
        out[:, rows, :] = out[:, rows, :] - step_size * rim[:, :, own]
    for place, band in ((odd_col * last, band_odd), ((1 - odd_col) * last, band_even)):
        cols = pl.ds(pl.multiple_of(place, 128), half)
        out[:, :, cols] = out[:, :, cols] - step_size * band[...]


def call(kernel, meta, arrays, outs, scratch=(), flops=0, room=0):
    f32 = jnp.float32
    shapes = [jax.ShapeDtypeStruct(*o) if isinstance(o[0], tuple) else jax.ShapeDtypeStruct(o, f32) for o in outs]
    shapes_in = [jax.ShapeDtypeStruct(x.shape, x.dtype) for x in arrays]
    moved = sum(math.prod(x.shape) * x.dtype.itemsize for x in [*shapes_in, *shapes])
    smem = pl.BlockSpec(memory_space=pltpu.SMEM)
    vmem = pl.BlockSpec(memory_space=pltpu.VMEM)
    return pl.pallas_call(
        kernel,
        out_shape=shapes,
        in_specs=[smem] + [vmem] * len(arrays),
        out_specs=[vmem] * len(shapes),
        scratch_shapes=list(scratch),
        compiler_params=pltpu.CompilerParams(vmem_limit_bytes=moved + room + MIB),
        cost_estimate=pl.CostEstimate(flops=flops, bytes_accessed=moved, transcendentals=0),
    )(meta, *arrays)


def local(object_field, probe_field, measured, offsets, counts):
    tile = object_field.shape[1]
    side = probe_field.shape[1]
    half = side // 2
    windows = offsets.shape[2]
    wide = tile + side
    bf = jnp.bfloat16
    place_col, columns_of_tiles = lax.axis_index("gx"), lax.axis_size("gx")
    odd_col = place_col % 2
    edge = (place_col == 0) | (place_col == columns_of_tiles - 1)
    odd_row = lax.axis_index("gy") % 2
    meta = jnp.concatenate(
        [jnp.stack([odd_col, odd_row, edge.astype(jnp.int32), counts[0, 0]]), offsets[0, 0].reshape(-1)]
    ).astype(jnp.int32)

    def columns(start):
        return lax.dynamic_slice(object_field, (0, 0, start), (2, tile, half))

    sides = swap(columns(odd_col * (tile - half)), columns((1 - odd_col) * (tile - half)), "gx")
    rim, column = (2, half, wide), (2, tile, half)
    middle, band = (2, tile, wide), (2, tile, side)
    probes, tables, amps = call(
        functools.partial(prepare_kernel, side, windows),
        meta,
        (probe_field, measured[0, 0]),
        ((windows, 2, side, side), ((windows, 8, side, side), bf), (windows, side, side)),
        flops=10**9,
        room=8 * MIB,
    )
    centre, *rims = call(assemble_kernel, meta, (object_field, *sides), (middle, rim, rim))
    for iteration in range(ITERS):
        halos = swap(*rims, "gy")
        grad, *rims = call(
            functools.partial(gradient_kernel, side, windows),
            meta,
            (centre, *halos, probes, tables, amps),
            (middle, rim, rim),
            scratch=(
                pltpu.VMEM((2, wide, wide), jnp.float32),
                pltpu.VMEM((2, wide, wide), jnp.float32),
                pltpu.VMEM((2, side, side), bf),
            ),
            flops=windows * 16 * side**3,
            room=20 * MIB,
        )
        rims = swap(*rims, "gy")
        width = side if iteration + 1 < ITERS else half
        shape = band if iteration + 1 < ITERS else column
        bands = call(functools.partial(bands_kernel, width), meta, (grad, *rims), (shape, shape))
        bands = swap(*bands, "gx")
        if iteration + 1 < ITERS:
            centre, *rims = call(
                update_kernel, meta, (centre, grad, *rims, *bands), (middle, rim, rim)
            )
    (updated,) = call(
        final_kernel, meta, (centre, grad, *rims, *bands), (object_field.shape,)
    )
    return updated


def solution(mesh):
    return jax.shard_map(
        local,
        mesh=mesh,
        in_specs=(
            P(None, "gy", "gx"),
            P(),
            P("gy", "gx", None, None, None),
            P("gy", "gx", None, None),
            P("gy", "gx"),
        ),
        out_specs=P(None, "gy", "gx"),
        check_vma=False,
    )
```

```python
import functools
import math

import jax
import jax.numpy as jnp
from jax import lax
from jax.experimental import pallas as pl
from jax.experimental.pallas import tpu as pltpu
from jax.sharding import PartitionSpec as P


ITERS = 2
step_size = 0.25
amplitude_floor = 0.5

MIB = 1 << 20

GX_ODD, GY_ODD, EDGE, RELAY, LIVE, OFFS = 0, 1, 2, 3, 4, 5


def pairs(count, first):
    ups = [(i, i + 1) for i in range(first, count - 1, 2)]
    return ups + [(b, a) for a, b in ups]


def swap_rows(odd_real, odd_imag, even_cells):
    count = lax.axis_size("gy")
    low = count // 2 - 1
    far = [(low, low + 1), (low + 1, low)]
    near = [p for p in pairs(count, 1) if p not in far]
    imag = lax.ppermute(odd_imag, "gy", near + [(low, 0), (low + 1, count - 1)])
    real = lax.ppermute(odd_real, "gy", near + far)
    even = lax.ppermute(even_cells, "gy", pairs(count, 0))
    relayed = lax.ppermute(imag, "gy", [(0, low + 1), (count - 1, low)])
    return real, imag, relayed, even


def swap_columns(odd_cells, even_cells):
    count = lax.axis_size("gx")
    from_odd = lax.ppermute(odd_cells, "gx", pairs(count, 1))
    from_even = lax.ppermute(even_cells, "gx", pairs(count, 0))
    return from_odd, from_even


def odd_terms(meta, real, imag, relayed):
    own = meta[RELAY] == 0
    return real[...], jnp.where(own, imag[...], jnp.zeros_like(imag)) + relayed[...]


def dot(a, b):
    return jnp.dot(a, b, preferred_element_type=jnp.float32)


def table_blocks(shift, half, side):
    rows = lax.broadcasted_iota(jnp.int32, (half, half), 0)
    cols = lax.broadcasted_iota(jnp.int32, (half, half), 1)
    scale = 2.0 * math.pi / side
    norm = 1.0 / math.sqrt(side)

    def entries(freq, cell):
        phase = (freq * (cell - shift + side)) & (side - 1)
        angle = phase.astype(jnp.float32) * scale
        return jnp.cos(angle) * norm, jnp.sin(angle) * norm

    out = []
    for odd in (0, 1):
        c, s = entries(2 * rows + odd, cols)
        ct, st = entries(2 * cols + odd, rows)
        out.append((c, s, ct, st))
    return out


def prepare_kernel(side, windows, meta, probe, measured, probes, tables, amps):
    half = side // 2
    bf = jnp.bfloat16
    rows = lax.broadcasted_iota(jnp.int32, (side, side), 0)
    cols = lax.broadcasted_iota(jnp.int32, (side, side), 1)
    place = jnp.where(cols < half, 2 * cols, 2 * (cols - half) + 1)
    picks = (rows == place).astype(jnp.float32).astype(bf)
    place_t = jnp.where(rows < half, 2 * rows, 2 * (rows - half) + 1)
    picks_t = (cols == place_t).astype(jnp.float32).astype(bf)

    def parts(x):
        high = x.astype(bf)
        rest = x - high.astype(jnp.float32)
        mid = rest.astype(bf)
        low = (rest - mid.astype(jnp.float32)).astype(bf)
        return high, mid, low

    def body(w, _):
        row = meta[OFFS + 2 * w] & (side - 1)
        col = meta[OFFS + 2 * w + 1] & (side - 1)
        for part in (0, 1):
            turned = pltpu.roll(probe[part], row, 0)
            probes[w, part] = pltpu.roll(turned, col, 1)
        for axis, shift in ((0, row), (1, col)):
            for odd, (c, s, ct, st) in enumerate(table_blocks(shift, half, side)):
                at = 4 * axis + 2 * odd
                tables[w, at, :half, :half] = c.astype(bf)
                tables[w, at, :half, half:] = s.astype(bf)
                tables[w, at, half:, :half] = (-s).astype(bf)
                tables[w, at, half:, half:] = c.astype(bf)
                tables[w, at + 1, :half, :half] = ct.astype(bf)
                tables[w, at + 1, :half, half:] = (-st).astype(bf)
                tables[w, at + 1, half:, :half] = st.astype(bf)
                tables[w, at + 1, half:, half:] = ct.astype(bf)
        a = [dot(x, picks) for x in parts(measured[w])]
        b = [dot(picks_t, x) for x in parts(a[0] + (a[1] + a[2]))]
        amps[w] = b[0] + (b[1] + b[2])
        return 0

    lax.fori_loop(0, windows, body, 0)


def gradient_kernel(
    side,
    windows,
    meta,
    centre,
    halo_real,
    halo_imag,
    halo_relayed,
    halo_even,
    probes,
    tables,
    amps,
    grad,
    rim_real,
    rim_imag,
    rim_even,
    field,
    total,
    mixed,
):
    half = side // 2
    tile = centre.shape[1]
    bf = jnp.bfloat16
    odd_row = meta[GY_ODD]
    bottom = half + tile
    at_odd = pl.multiple_of(odd_row * bottom, half)
    at_even = pl.multiple_of((1 - odd_row) * bottom, half)
    field[:, pl.ds(half, tile), :] = centre[...]
    for part, cells in enumerate(odd_terms(meta, halo_real, halo_imag, halo_relayed)):
        field[part, pl.ds(at_odd, half), :] = cells
    field[:, pl.ds(at_even, half), :] = halo_even[...]
    total[...] = jnp.zeros_like(total)
    chunk = 32
    zero = jnp.float32(0)

    for w in range(windows):
        a, b = meta[OFFS + 2 * w], meta[OFFS + 2 * w + 1]
        live = w < meta[LIVE]
        hi_a, hi_b = (a >= side).astype(jnp.int32), (b >= side).astype(jnp.int32)
        row0, col0 = pl.multiple_of(hi_a * side, side), pl.multiple_of(hi_b * side, side)
        row_in, col_in = a - row0, b - col0
        near = lax.broadcasted_iota(jnp.int32, (chunk, side), 1) >= col_in

        def below(start):
            return (lax.broadcasted_iota(jnp.int32, (chunk, side), 0) + start) >= row_in

        def patch(part, start):
            def at(i, j):
                return field[
                    part,
                    pl.ds(pl.multiple_of(row0 + i * side + start, chunk), chunk),
                    pl.ds(pl.multiple_of(col0 + j * side, side), side),
                ]

            return jnp.where(
                below(start),
                jnp.where(near, at(0, 0), at(0, 1)),
                jnp.where(near, at(1, 0), at(1, 1)),
            )

        def exits(start):
            real, imag = patch(0, start), patch(1, start)
            p_real = probes[w, 0, pl.ds(start, chunk), :]
            p_imag = probes[w, 1, pl.ds(start, chunk), :]
            return p_real * real - p_imag * imag, p_real * imag + p_imag * real

        for i in range(0, half, chunk):
            r0, i0 = exits(i)
            r1, i1 = exits(half + i)
            mixed[0, i : i + chunk, :] = (r0 + r1).astype(bf)
            mixed[0, half + i : half + i + chunk, :] = (i0 + i1).astype(bf)
            mixed[1, i : i + chunk, :] = (r0 - r1).astype(bf)
            mixed[1, half + i : half + i + chunk, :] = (i0 - i1).astype(bf)

        plus, minus = [], []
        for odd in (0, 1):
            h = dot(tables[w, 2 * odd], mixed[odd])
            re0, re1 = h[:half, :half], h[:half, half:]
            im0, im1 = h[half:, :half], h[half:, half:]
            plus.append(jnp.concatenate([re0 + re1, im0 + im1], axis=1).astype(bf))
            minus.append(jnp.concatenate([re0 - re1, im0 - im1], axis=1).astype(bf))

        backs = []
        for odd, sides in ((0, plus), (1, minus)):
            far = dot(jnp.concatenate(sides, axis=0), tables[w, 4 + 2 * odd + 1])
            re, im = far[:, :half], far[:, half:]
            power = jnp.maximum(re * re + im * im, amplitude_floor * amplitude_floor)
            factor = 1.0 - amps[w, :, odd * half : (odd + 1) * half] * lax.rsqrt(power)
            chi = jnp.concatenate([re * factor, im * factor], axis=1).astype(bf)
            backs.append(dot(chi, tables[w, 4 + 2 * odd]))
        left, right = backs[0] + backs[1], backs[0] - backs[1]

        outs = []
        for odd in (0, 1):
            at = slice(odd * half, (odd + 1) * half)
            real = jnp.concatenate([left[at, :half], right[at, :half]], axis=1)
            imag = jnp.concatenate([left[at, half:], right[at, half:]], axis=1)
            stacked = jnp.concatenate([real, imag], axis=0).astype(bf)
            outs.append(dot(tables[w, 2 * odd + 1], stacked))
        upper, lower = outs[0] + outs[1], outs[0] - outs[1]

        for start in range(0, side, chunk):
            back = upper if start < half else lower
            at = start % half
            b_real, b_imag = back[at : at + chunk], back[half + at : half + at + chunk]
            p_real = probes[w, 0, pl.ds(start, chunk), :]
            p_imag = probes[w, 1, pl.ds(start, chunk), :]
            terms = (p_real * b_real + p_imag * b_imag, p_real * b_imag - p_imag * b_real)
            rows_in = below(start)
            for part in (0, 1):
                for i, j in ((0, 0), (0, 1), (1, 0), (1, 1)):
                    keep = (rows_in if i == 0 else ~rows_in) & (near if j == 0 else ~near)
                    place = (
                        part,
                        pl.ds(pl.multiple_of(row0 + i * side + start, chunk), chunk),
                        pl.ds(pl.multiple_of(col0 + j * side, side), side),
                    )
                    total[place] = total[place] + jnp.where(keep & live, terms[part], zero)

    grad[...] = total[:, pl.ds(half, tile), :]
    rim_real[...] = total[0, pl.ds(at_odd, half), :]
    rim_imag[...] = total[1, pl.ds(at_odd, half), :]
    rim_even[...] = total[:, pl.ds(at_even, half), :]


def row_places(meta, half, tile):
    odd_row = meta[GY_ODD]
    far = tile - half
    return pl.multiple_of(odd_row * far, half), pl.multiple_of((1 - odd_row) * far, half)


def assemble_kernel(meta, own, halo_odd, halo_even, _, centre, rim_real, rim_imag, rim_even):
    tile, half = own.shape[1], halo_odd.shape[2]
    odd_col = meta[GX_ODD]
    beyond = half + tile
    centre[:, :, half : half + tile] = own[...]
    centre[:, :, pl.ds(pl.multiple_of(odd_col * beyond, half), half)] = halo_odd[...]
    centre[:, :, pl.ds(pl.multiple_of((1 - odd_col) * beyond, half), half)] = halo_even[...]
    at_odd, at_even = row_places(meta, half, tile)
    rim_real[...] = centre[0, pl.ds(at_odd, half), :]
    rim_imag[...] = centre[1, pl.ds(at_odd, half), :]
    rim_even[...] = centre[:, pl.ds(at_even, half), :]


def bands_kernel(width, meta, grad, rim_real, rim_imag, rim_relayed, rim_even, band_odd, band_even):
    tile, half = grad.shape[1], rim_even.shape[1]
    odd_col = meta[GX_ODD]
    last = grad.shape[2] - width
    at_odd, at_even = row_places(meta, half, tile)
    for band, place in ((band_odd, odd_col * last), (band_even, (1 - odd_col) * last)):
        cols = pl.ds(pl.multiple_of(place, 128), width)
        band[...] = grad[:, :, cols]
        own = meta[RELAY] == 0
        real, imag = rim_real[:, cols], rim_imag[:, cols]
        imag = jnp.where(own, imag, jnp.zeros_like(imag)) + rim_relayed[:, cols]
        rows = pl.ds(at_odd, half)
        for part, cells in ((0, real), (1, imag)):
            band[part, rows, :] = band[part, rows, :] + cells
        rows = pl.ds(at_even, half)
        band[:, rows, :] = band[:, rows, :] + rim_even[:, :, cols]


def update_kernel(
    meta,
    centre,
    grad,
    rim_real,
    rim_imag,
    rim_relayed,
    rim_even,
    band_odd,
    band_even,
    fresh,
    out_real,
    out_imag,
    out_even,
):
    tile, half = grad.shape[1], rim_even.shape[1]
    odd_col = meta[GX_ODD]
    width = band_odd.shape[2]
    last = grad.shape[2] - width
    at_odd, at_even = row_places(meta, half, tile)
    fresh[...] = centre[...] - step_size * grad[...]
    rows = pl.ds(at_odd, half)
    for part, cells in enumerate(odd_terms(meta, rim_real, rim_imag, rim_relayed)):
        fresh[part, rows, :] = fresh[part, rows, :] - step_size * cells
    rows = pl.ds(at_even, half)
    fresh[:, rows, :] = fresh[:, rows, :] - step_size * rim_even[...]
    for place, band in ((odd_col * last, band_odd), ((1 - odd_col) * last, band_even)):
        cols = pl.ds(pl.multiple_of(place, 128), width)
        fresh[:, :, cols] = fresh[:, :, cols] - step_size * band[...]

    @pl.when(meta[EDGE] == 1)
    def _():
        outside = pl.ds(pl.multiple_of(odd_col * (half + tile), half), half)
        fresh[:, :, outside] = jnp.zeros((2, tile, half), jnp.float32)

    out_real[...] = fresh[0, pl.ds(at_odd, half), :]
    out_imag[...] = fresh[1, pl.ds(at_odd, half), :]
    out_even[...] = fresh[:, pl.ds(at_even, half), :]


def final_kernel(
    meta, centre, grad, rim_real, rim_imag, rim_relayed, rim_even, band_odd, band_even, out
):
    tile, half = grad.shape[1], rim_even.shape[1]
    odd_col = meta[GX_ODD]
    last = tile - half
    at_odd, at_even = row_places(meta, half, tile)
    own = slice(half, half + tile)
    out[...] = centre[:, :, own] - step_size * grad[:, :, own]
    rows = pl.ds(at_odd, half)
    for part, cells in enumerate(odd_terms(meta, rim_real, rim_imag, rim_relayed)):
        out[part, rows, :] = out[part, rows, :] - step_size * cells[:, own]
    rows = pl.ds(at_even, half)
    out[:, rows, :] = out[:, rows, :] - step_size * rim_even[:, :, own]
    for place, band in ((odd_col * last, band_odd), ((1 - odd_col) * last, band_even)):
        cols = pl.ds(pl.multiple_of(place, 128), half)
        out[:, :, cols] = out[:, :, cols] - step_size * band[...]


def call(kernel, meta, arrays, outs, scratch=(), flops=0, room=0, after=None):
    f32 = jnp.float32
    shapes = [jax.ShapeDtypeStruct(*o) if isinstance(o[0], tuple) else jax.ShapeDtypeStruct(o, f32) for o in outs]
    shapes_in = [jax.ShapeDtypeStruct(x.shape, x.dtype) for x in arrays]
    moved = sum(math.prod(x.shape) * x.dtype.itemsize for x in [*shapes_in, *shapes])
    late = [] if after is None else [after]
    smem = pl.BlockSpec(memory_space=pltpu.SMEM)
    vmem = pl.BlockSpec(memory_space=pltpu.VMEM)
    return pl.pallas_call(
        kernel,
        out_shape=shapes,
        in_specs=[smem] + [vmem] * len(arrays) + [pl.BlockSpec(memory_space=pl.ANY)] * len(late),
        out_specs=[vmem] * len(shapes),
        scratch_shapes=list(scratch),
        compiler_params=pltpu.CompilerParams(vmem_limit_bytes=moved + room + MIB),
        cost_estimate=pl.CostEstimate(flops=flops, bytes_accessed=moved, transcendentals=0),
    )(meta, *arrays, *late)


def local(object_field, probe_field, measured, offsets, counts):
    tile = object_field.shape[1]
    side = probe_field.shape[1]
    half = side // 2
    windows = offsets.shape[2]
    wide = tile + side
    bf = jnp.bfloat16
    place_col, columns_of_tiles = lax.axis_index("gx"), lax.axis_size("gx")
    odd_col = place_col % 2
    edge = (place_col == 0) | (place_col == columns_of_tiles - 1)
    place_row, rows_of_tiles = lax.axis_index("gy"), lax.axis_size("gy")
    odd_row = place_row % 2
    relay = (place_row == 0) | (place_row == rows_of_tiles - 1)
    meta = jnp.concatenate(
        [jnp.stack([odd_col, odd_row, edge.astype(jnp.int32), relay.astype(jnp.int32), counts[0, 0]]), offsets[0, 0].reshape(-1)]
    ).astype(jnp.int32)

    def columns(start):
        return lax.dynamic_slice(object_field, (0, 0, start), (2, tile, half))

    sides = swap_columns(columns(odd_col * (tile - half)), columns((1 - odd_col) * (tile - half)))
    line, rim, column = (half, wide), (2, half, wide), (2, tile, half)
    middle, band = (2, tile, wide), (2, tile, side)
    probes, tables, amps = call(
        functools.partial(prepare_kernel, side, windows),
        meta,
        (probe_field, measured[0, 0]),
        ((windows, 2, side, side), ((windows, 8, side, side), bf), (windows, side, side)),
        flops=10**9,
        room=8 * MIB,
    )
    centre, *rims = call(
        assemble_kernel, meta, (object_field, *sides), (middle, line, line, rim), after=amps
    )
    for iteration in range(ITERS):
        halos = swap_rows(*rims)
        grad, *rims = call(
            functools.partial(gradient_kernel, side, windows),
            meta,
            (centre, *halos, probes, tables, amps),
            (middle, line, line, rim),
            scratch=(
                pltpu.VMEM((2, wide, wide), jnp.float32),
                pltpu.VMEM((2, wide, wide), jnp.float32),
                pltpu.VMEM((2, side, side), bf),
            ),
            flops=windows * 16 * side**3,
            room=20 * MIB,
        )
        rims = swap_rows(*rims)
        width = side if iteration + 1 < ITERS else half
        shape = band if iteration + 1 < ITERS else column
        bands = call(functools.partial(bands_kernel, width), meta, (grad, *rims), (shape, shape))
        bands = swap_columns(*bands)
        if iteration + 1 < ITERS:
            centre, *rims = call(
                update_kernel, meta, (centre, grad, *rims, *bands), (middle, line, line, rim)
            )
    (updated,) = call(
        final_kernel, meta, (centre, grad, *rims, *bands), (object_field.shape,)
    )
    return updated


def solution(mesh):
    return jax.shard_map(
        local,
        mesh=mesh,
        in_specs=(
            P(None, "gy", "gx"),
            P(),
            P("gy", "gx", None, None, None),
            P("gy", "gx", None, None),
            P("gy", "gx"),
        ),
        out_specs=P(None, "gy", "gx"),
        check_vma=False,
    )
```

```python
import functools
import math

import jax
import jax.numpy as jnp
from jax import lax
from jax.experimental import pallas as pl
from jax.experimental.pallas import tpu as pltpu
from jax.sharding import PartitionSpec as P


ITERS = 2
step_size = 0.25
amplitude_floor = 0.5

MIB = 1 << 20

GX_ODD, GY_ODD, EDGE, RELAY, LIVE, OFFS = 0, 1, 2, 3, 4, 5


def pairs(count, first):
    ups = [(i, i + 1) for i in range(first, count - 1, 2)]
    return ups + [(b, a) for a, b in ups]


def swap_rows(direct, detour, even_cells):
    count = lax.axis_size("gy")
    low = count // 2 - 1
    far = [(low, low + 1), (low + 1, low)]
    near = [p for p in pairs(count, 1) if p not in far]
    first = lax.ppermute(detour, "gy", near + [(low, 0), (low + 1, count - 1)])
    straight = lax.ppermute(direct, "gy", near + far)
    even = lax.ppermute(even_cells, "gy", pairs(count, 0))
    second = lax.ppermute(first, "gy", [(0, low + 1), (count - 1, low)])
    return straight, first, second, even


def swap_columns(odd_cells, even_cells):
    count = lax.axis_size("gx")
    from_odd = lax.ppermute(odd_cells, "gx", pairs(count, 1))
    from_even = lax.ppermute(even_cells, "gx", pairs(count, 0))
    return from_odd, from_even


CUT = 128


def pack(real, imag, direct, detour):
    wide = real.shape[1]
    direct[:, :wide] = real
    direct[:, wide:] = imag[:, :CUT]
    detour[...] = imag[:, CUT:]


def unpack(meta, direct, detour, relayed, line):
    wide = line.shape[2]
    own = meta[RELAY] == 0
    line[0] = direct[:, :wide]
    line[1, :, :CUT] = direct[:, wide:]
    line[1, :, CUT:] = jnp.where(own, detour[...], jnp.zeros_like(detour)) + relayed[...]


def dot(a, b):
    return jnp.dot(a, b, preferred_element_type=jnp.float32)


def table_blocks(shift, half, side):
    rows = lax.broadcasted_iota(jnp.int32, (half, half), 0)
    cols = lax.broadcasted_iota(jnp.int32, (half, half), 1)
    scale = 2.0 * math.pi / side
    norm = 1.0 / math.sqrt(side)

    def entries(freq, cell):
        phase = (freq * (cell - shift + side)) & (side - 1)
        angle = phase.astype(jnp.float32) * scale
        return jnp.cos(angle) * norm, jnp.sin(angle) * norm

    out = []
    for odd in (0, 1):
        c, s = entries(2 * rows + odd, cols)
        ct, st = entries(2 * cols + odd, rows)
        out.append((c, s, ct, st))
    return out


def prepare_kernel(side, windows, meta, probe, measured, probes, tables, amps):
    half = side // 2
    bf = jnp.bfloat16
    rows = lax.broadcasted_iota(jnp.int32, (side, side), 0)
    cols = lax.broadcasted_iota(jnp.int32, (side, side), 1)
    place = jnp.where(cols < half, 2 * cols, 2 * (cols - half) + 1)
    picks = (rows == place).astype(jnp.float32).astype(bf)
    place_t = jnp.where(rows < half, 2 * rows, 2 * (rows - half) + 1)
    picks_t = (cols == place_t).astype(jnp.float32).astype(bf)

    def parts(x):
        high = x.astype(bf)
        rest = x - high.astype(jnp.float32)
        mid = rest.astype(bf)
        low = (rest - mid.astype(jnp.float32)).astype(bf)
        return high, mid, low

    def body(w, _):
        row = meta[OFFS + 2 * w] & (side - 1)
        col = meta[OFFS + 2 * w + 1] & (side - 1)
        for part in (0, 1):
            turned = pltpu.roll(probe[part], row, 0)
            probes[w, part] = pltpu.roll(turned, col, 1)
        for axis, shift in ((0, row), (1, col)):
            for odd, (c, s, ct, st) in enumerate(table_blocks(shift, half, side)):
                at = 4 * axis + 2 * odd
                tables[w, at, :half, :half] = c.astype(bf)
                tables[w, at, :half, half:] = s.astype(bf)
                tables[w, at, half:, :half] = (-s).astype(bf)
                tables[w, at, half:, half:] = c.astype(bf)
                tables[w, at + 1, :half, :half] = ct.astype(bf)
                tables[w, at + 1, :half, half:] = (-st).astype(bf)
                tables[w, at + 1, half:, :half] = st.astype(bf)
                tables[w, at + 1, half:, half:] = ct.astype(bf)
        a = [dot(x, picks) for x in parts(measured[w])]
        b = [dot(picks_t, x) for x in parts(a[0] + (a[1] + a[2]))]
        amps[w] = b[0] + (b[1] + b[2])
        return 0

    lax.fori_loop(0, windows, body, 0)


def gradient_kernel(
    side,
    windows,
    meta,
    centre,
    halo_direct,
    halo_detour,
    halo_relayed,
    halo_even,
    probes,
    tables,
    amps,
    grad,
    rim_direct,
    rim_detour,
    rim_even,
    band_odd,
    band_even,
    field,
    total,
    mixed,
    line,
):
    half = side // 2
    tile, wide = centre.shape[1:]
    bf = jnp.bfloat16
    odd_row = meta[GY_ODD]
    bottom = half + tile
    at_odd = pl.multiple_of(odd_row * bottom, half)
    at_even = pl.multiple_of((1 - odd_row) * bottom, half)
    field[:, pl.ds(half, tile), :] = centre[...]
    unpack(meta, halo_direct, halo_detour, halo_relayed, line)
    field[:, pl.ds(at_odd, half), :] = line[...]
    field[:, pl.ds(at_even, half), :] = halo_even[...]
    total[...] = jnp.zeros_like(total)
    chunk = 32
    zero = jnp.float32(0)

    for w in range(windows):
        a, b = meta[OFFS + 2 * w], meta[OFFS + 2 * w + 1]
        live = w < meta[LIVE]
        hi_a, hi_b = (a >= side).astype(jnp.int32), (b >= side).astype(jnp.int32)
        row0, col0 = pl.multiple_of(hi_a * side, side), pl.multiple_of(hi_b * side, side)
        row_in, col_in = a - row0, b - col0
        near = lax.broadcasted_iota(jnp.int32, (chunk, side), 1) >= col_in

        def below(start):
            return (lax.broadcasted_iota(jnp.int32, (chunk, side), 0) + start) >= row_in

        def patch(part, start):
            def at(i, j):
                return field[
                    part,
                    pl.ds(pl.multiple_of(row0 + i * side + start, chunk), chunk),
                    pl.ds(pl.multiple_of(col0 + j * side, side), side),
                ]

            return jnp.where(
                below(start),
                jnp.where(near, at(0, 0), at(0, 1)),
                jnp.where(near, at(1, 0), at(1, 1)),
            )

        def exits(start):
            real, imag = patch(0, start), patch(1, start)
            p_real = probes[w, 0, pl.ds(start, chunk), :]
            p_imag = probes[w, 1, pl.ds(start, chunk), :]
            return p_real * real - p_imag * imag, p_real * imag + p_imag * real

        for i in range(0, half, chunk):
            r0, i0 = exits(i)
            r1, i1 = exits(half + i)
            mixed[0, i : i + chunk, :] = (r0 + r1).astype(bf)
            mixed[0, half + i : half + i + chunk, :] = (i0 + i1).astype(bf)
            mixed[1, i : i + chunk, :] = (r0 - r1).astype(bf)
            mixed[1, half + i : half + i + chunk, :] = (i0 - i1).astype(bf)

        plus, minus = [], []
        for odd in (0, 1):
            h = dot(tables[w, 2 * odd], mixed[odd])
            re0, re1 = h[:half, :half], h[:half, half:]
            im0, im1 = h[half:, :half], h[half:, half:]
            plus.append(jnp.concatenate([re0 + re1, im0 + im1], axis=1).astype(bf))
            minus.append(jnp.concatenate([re0 - re1, im0 - im1], axis=1).astype(bf))

        backs = []
        for odd, sides in ((0, plus), (1, minus)):
            far = dot(jnp.concatenate(sides, axis=0), tables[w, 4 + 2 * odd + 1])
            re, im = far[:, :half], far[:, half:]
            power = jnp.maximum(re * re + im * im, amplitude_floor * amplitude_floor)
            factor = 1.0 - amps[w, :, odd * half : (odd + 1) * half] * lax.rsqrt(power)
            chi = jnp.concatenate([re * factor, im * factor], axis=1).astype(bf)
            backs.append(dot(chi, tables[w, 4 + 2 * odd]))
        left, right = backs[0] + backs[1], backs[0] - backs[1]

        outs = []
        for odd in (0, 1):
            at = slice(odd * half, (odd + 1) * half)
            real = jnp.concatenate([left[at, :half], right[at, :half]], axis=1)
            imag = jnp.concatenate([left[at, half:], right[at, half:]], axis=1)
            stacked = jnp.concatenate([real, imag], axis=0).astype(bf)
            outs.append(dot(tables[w, 2 * odd + 1], stacked))
        upper, lower = outs[0] + outs[1], outs[0] - outs[1]

        for start in range(0, side, chunk):
            back = upper if start < half else lower
            at = start % half
            b_real, b_imag = back[at : at + chunk], back[half + at : half + at + chunk]
            p_real = probes[w, 0, pl.ds(start, chunk), :]
            p_imag = probes[w, 1, pl.ds(start, chunk), :]
            terms = (p_real * b_real + p_imag * b_imag, p_real * b_imag - p_imag * b_real)
            rows_in = below(start)
            for part in (0, 1):
                for i, j in ((0, 0), (0, 1), (1, 0), (1, 1)):
                    keep = (rows_in if i == 0 else ~rows_in) & (near if j == 0 else ~near)
                    place = (
                        part,
                        pl.ds(pl.multiple_of(row0 + i * side + start, chunk), chunk),
                        pl.ds(pl.multiple_of(col0 + j * side, side), side),
                    )
                    total[place] = total[place] + jnp.where(keep & live, terms[part], zero)

    grad[...] = total[:, pl.ds(half, tile), :]
    odd_rows = pl.ds(at_odd, half)
    pack(total[0, odd_rows, :], total[1, odd_rows, :], rim_direct, rim_detour)
    rim_even[...] = total[:, pl.ds(at_even, half), :]
    for band, cols in (
        (band_odd, odd_side(meta, band_odd, wide)),
        (band_even, even_side(meta, band_even, wide)),
    ):
        band[...] = total[:, side:tile, cols]


def odd_side(meta, band, wide):
    return pl.ds(pl.multiple_of(meta[GX_ODD] * (wide - band.shape[2]), 128), band.shape[2])


def even_side(meta, band, wide):
    return pl.ds(pl.multiple_of((1 - meta[GX_ODD]) * (wide - band.shape[2]), 128), band.shape[2])


def rim_rows(meta, half):
    odd_row = meta[GY_ODD]
    return (
        pl.ds(pl.multiple_of(odd_row * half, half), half),
        pl.ds(pl.multiple_of((1 - odd_row) * half, half), half),
    )


def sides_kernel(meta, own, rim_odd, rim_even, mid_odd, mid_even, sems):
    tile, half = own.shape[1], rim_odd.shape[2]
    copies = []
    for rim, mid, cols in (
        (rim_odd, mid_odd, odd_side(meta, rim_odd, tile)),
        (rim_even, mid_even, even_side(meta, rim_even, tile)),
    ):
        for src, dst in (
            (own.at[:, pl.ds(0, half), cols], rim.at[:, pl.ds(0, half), :]),
            (own.at[:, pl.ds(tile - half, half), cols], rim.at[:, pl.ds(half, half), :]),
            (own.at[:, pl.ds(half, tile - 2 * half), cols], mid),
        ):
            copies.append(pltpu.make_async_copy(src, dst, sems.at[len(copies)]))
    for copy in copies:
        copy.start()
    for copy in copies:
        copy.wait()


def edges_kernel(meta, own, side_odd, side_even, _, direct, detour, even, lines):
    tile, half = own.shape[1], side_odd.shape[2]
    wide = lines.shape[2]
    for at, rows in ((0, slice(0, half)), (half, slice(tile - half, tile))):
        lines[:, at : at + half, half : half + tile] = own[:, rows, :]
    lines[:, :, odd_side(meta, side_odd, wide)] = side_odd[...]
    lines[:, :, even_side(meta, side_even, wide)] = side_even[...]
    odd_rows, even_rows = rim_rows(meta, half)
    pack(lines[0, odd_rows, :], lines[1, odd_rows, :], direct, detour)
    even[...] = lines[:, even_rows, :]


def centre_kernel(meta, own, lines, side_odd, side_even, centre):
    tile, half = own.shape[1], side_odd.shape[2]
    wide = lines.shape[2]
    mid = slice(half, tile - half)
    centre[:, :half, :] = lines[:, :half, :]
    centre[:, tile - half :, :] = lines[:, half:, :]
    centre[:, mid, half : half + tile] = own[:, mid, :]
    centre[:, mid, odd_side(meta, side_odd, wide)] = side_odd[...]
    centre[:, mid, even_side(meta, side_even, wide)] = side_even[...]


def bands_kernel(meta, grad, direct, detour, relayed, even, band_odd, band_even, line):
    (tile, wide), half = grad.shape[1:], even.shape[1]
    unpack(meta, direct, detour, relayed, line)
    odd_rows, even_rows = rim_rows(meta, half)
    for band, cols in ((band_odd, odd_side(meta, band_odd, wide)), (band_even, even_side(meta, band_even, wide))):
        band[:, :half, :] = grad[:, :half, cols]
        band[:, half:, :] = grad[:, tile - half :, cols]
        band[:, odd_rows, :] = band[:, odd_rows, :] + line[:, :, cols]
        band[:, even_rows, :] = band[:, even_rows, :] + even[:, :, cols]


def clear_outside(meta, cells, half):
    wide = cells.shape[2]

    @pl.when(meta[EDGE] == 1)
    def _():
        outside = pl.ds(pl.multiple_of(meta[GX_ODD] * (wide - half), half), half)
        cells[:, :, outside] = jnp.zeros((*cells.shape[:2], half), jnp.float32)


def update_edges_kernel(
    meta, centre, grad, line, even, band_odd, band_even, direct, detour, out_even, lines
):
    (tile, wide), half = grad.shape[1:], even.shape[1]
    odd_rows, even_rows = rim_rows(meta, half)
    for at, rows in ((0, slice(0, half)), (half, slice(tile - half, tile))):
        lines[:, at : at + half, :] = centre[:, rows, :] - step_size * grad[:, rows, :]
    lines[:, odd_rows, :] = lines[:, odd_rows, :] - step_size * line[...]
    lines[:, even_rows, :] = lines[:, even_rows, :] - step_size * even[...]
    for band, cols in ((band_odd, odd_side(meta, band_odd, wide)), (band_even, even_side(meta, band_even, wide))):
        lines[:, :, cols] = lines[:, :, cols] - step_size * band[...]
    clear_outside(meta, lines, half)
    pack(lines[0, odd_rows, :], lines[1, odd_rows, :], direct, detour)
    out_even[...] = lines[:, even_rows, :]


def update_centre_kernel(meta, centre, grad, lines, band_odd, band_even, fresh):
    tile, wide = grad.shape[1:]
    half = lines.shape[1] // 2
    mid = slice(half, tile - half)
    fresh[:, mid, :] = centre[:, mid, :] - step_size * grad[:, mid, :]
    for band, cols in ((band_odd, odd_side(meta, band_odd, wide)), (band_even, even_side(meta, band_even, wide))):
        fresh[:, mid, cols] = fresh[:, mid, cols] - step_size * band[...]
    clear_outside(meta, fresh, half)
    fresh[:, :half, :] = lines[:, :half, :]
    fresh[:, tile - half :, :] = lines[:, half:, :]


def final_kernel(meta, centre, grad, line, even, mid_odd, mid_even, rim_odd, rim_even, out):
    tile, half = grad.shape[1], even.shape[1]
    own = slice(half, half + tile)
    odd_row = meta[GY_ODD]
    far = tile - half
    out[...] = centre[:, :, own] - step_size * grad[:, :, own]
    for at, rim in ((odd_row * far, line), ((1 - odd_row) * far, even)):
        rows = pl.ds(pl.multiple_of(at, half), half)
        out[:, rows, :] = out[:, rows, :] - step_size * rim[:, :, own]
    for mid, rim, cols in (
        (mid_odd, rim_odd, odd_side(meta, mid_odd, tile)),
        (mid_even, rim_even, even_side(meta, mid_even, tile)),
    ):
        out[:, :half, cols] = out[:, :half, cols] - step_size * rim[:, :half, :]
        out[:, half:far, cols] = out[:, half:far, cols] - step_size * mid[...]
        out[:, far:, cols] = out[:, far:, cols] - step_size * rim[:, half:, :]


def call(kernel, meta, arrays, outs, scratch=(), flops=0, room=0, after=None, hbm=False):
    f32 = jnp.float32
    shapes = [
        jax.ShapeDtypeStruct(*o) if isinstance(o[0], tuple) else jax.ShapeDtypeStruct(o, f32)
        for o in outs
    ]
    shapes_in = [jax.ShapeDtypeStruct(x.shape, x.dtype) for x in arrays]
    moved = sum(math.prod(x.shape) * x.dtype.itemsize for x in [*shapes_in, *shapes])
    late = [] if after is None else [after]
    smem = pl.BlockSpec(memory_space=pltpu.SMEM)
    vmem = pl.BlockSpec(memory_space=pltpu.VMEM)
    anywhere = pl.BlockSpec(memory_space=pl.ANY)
    return pl.pallas_call(
        kernel,
        out_shape=shapes,
        in_specs=[smem] + [pl.BlockSpec(memory_space=pltpu.HBM) if hbm else vmem] * len(arrays) + [anywhere] * len(late),
        out_specs=[vmem] * len(shapes),
        scratch_shapes=list(scratch),
        compiler_params=pltpu.CompilerParams(vmem_limit_bytes=room or moved + MIB),
        cost_estimate=pl.CostEstimate(flops=flops, bytes_accessed=moved, transcendentals=0),
    )(meta, *arrays, *late)


def local(object_field, probe_field, measured, offsets, counts):
    tile = object_field.shape[1]
    side = probe_field.shape[1]
    half = side // 2
    windows = offsets.shape[2]
    wide = tile + side
    bf, f32 = jnp.bfloat16, jnp.float32
    place_col, columns_of_tiles = lax.axis_index("gx"), lax.axis_size("gx")
    odd_col = place_col % 2
    edge = (place_col == 0) | (place_col == columns_of_tiles - 1)
    place_row, rows_of_tiles = lax.axis_index("gy"), lax.axis_size("gy")
    odd_row = place_row % 2
    relay = (place_row == 0) | (place_row == rows_of_tiles - 1)
    places = jnp.stack([odd_col, odd_row, edge.astype(jnp.int32), relay.astype(jnp.int32)])
    meta = jnp.concatenate([places, counts[0], offsets[0, 0].reshape(-1)]).astype(jnp.int32)

    column, band = (2, 2 * half, half), (2, 2 * half, side)
    mid_column, mid_band = (2, tile - 2 * half, half), (2, tile - 2 * half, side)
    middle, lines = (2, tile, wide), (2, 2 * half, wide)
    line = (2, half, wide)
    sends = ((half, wide + CUT), (half, wide - CUT), line)

    *rims, mid_odd, mid_even = call(
        sides_kernel,
        places,
        (object_field,),
        (column, column, mid_column, mid_column),
        scratch=(pltpu.SemaphoreType.DMA((6,)),),
        hbm=True,
    )
    rims = swap_columns(*rims)
    mids = swap_columns(mid_odd, mid_even)
    probes, tables, amps = call(
        functools.partial(prepare_kernel, side, windows),
        meta,
        (probe_field, measured[0, 0]),
        ((windows, 2, side, side), ((windows, 8, side, side), bf), (windows, side, side)),
        flops=10**9,
        room=20 * MIB,
    )
    *edges, rows = call(edges_kernel, meta, (object_field, *rims), (*sends, lines), after=amps)
    halos = swap_rows(*edges)
    (centre,) = call(centre_kernel, meta, (object_field, rows, *mids), (middle,))
    for iteration in range(ITERS):
        last = iteration + 1 == ITERS
        grad, *rims, mid_odd, mid_even = call(
            functools.partial(gradient_kernel, side, windows),
            meta,
            (centre, *halos, probes, tables, amps),
            (middle, *sends, *((mid_column if last else mid_band),) * 2),
            scratch=(
                pltpu.VMEM((2, wide, wide), f32),
                pltpu.VMEM((2, wide, wide), f32),
                pltpu.VMEM((2, side, side), bf),
                pltpu.VMEM(line, f32),
            ),
            flops=windows * 16 * side**3,
            room=24 * MIB,
        )
        rims = swap_rows(*rims)
        shape = column if last else band
        *bands, odd_line = call(bands_kernel, meta, (grad, *rims), (shape, shape, line))
        bands = swap_columns(*bands)
        mids = swap_columns(mid_odd, mid_even)
        if last:
            break
        *edges, rows = call(
            update_edges_kernel,
            meta,
            (centre, grad, odd_line, rims[3], *bands),
            (*sends, lines),
        )
        halos = swap_rows(*edges)
        (centre,) = call(update_centre_kernel, meta, (centre, grad, rows, *mids), (middle,))
    (updated,) = call(
        final_kernel,
        meta,
        (centre, grad, odd_line, rims[3], *mids, *bands),
        (object_field.shape,),
    )
    return updated


def solution(mesh):
    return jax.shard_map(
        local,
        mesh=mesh,
        in_specs=(
            P(None, "gy", "gx"),
            P(),
            P("gy", "gx", None, None, None),
            P("gy", "gx", None, None),
            P("gy", "gx"),
        ),
        out_specs=P(None, "gy", "gx"),
        check_vma=False,
    )
```

```python
import functools
import math

import jax
import jax.numpy as jnp
from jax import lax
from jax.experimental import pallas as pl
from jax.experimental.pallas import tpu as pltpu
from jax.sharding import PartitionSpec as P


ITERS = 2
step_size = 0.25
amplitude_floor = 0.5

MIB = 1 << 20

GX_ODD, GY_ODD, EDGE, RELAY, LIVE, OFFS = 0, 1, 2, 3, 4, 5


def pairs(count, first):
    ups = [(i, i + 1) for i in range(first, count - 1, 2)]
    return ups + [(b, a) for a, b in ups]


def swap_rows(direct, detour, even_cells):
    count = lax.axis_size("gy")
    low = count // 2 - 1
    far = [(low, low + 1), (low + 1, low)]
    near = [p for p in pairs(count, 1) if p not in far]
    first = lax.ppermute(detour, "gy", near + [(low, 0), (low + 1, count - 1)])
    straight = lax.ppermute(direct, "gy", near + far)
    even = lax.ppermute(even_cells, "gy", pairs(count, 0))
    second = lax.ppermute(first, "gy", [(0, low + 1), (count - 1, low)])
    return straight, first, second, even


def swap_columns(odd_cells, even_cells):
    count = lax.axis_size("gx")
    from_odd = lax.ppermute(odd_cells, "gx", pairs(count, 1))
    from_even = lax.ppermute(even_cells, "gx", pairs(count, 0))
    return from_odd, from_even


CUT = 128


def pack(real, imag, direct, detour):
    wide = real.shape[1]
    direct[:, :wide] = real
    direct[:, wide:] = imag[:, :CUT]
    detour[...] = imag[:, CUT:]


def unpack(meta, direct, detour, relayed, line):
    wide = line.shape[2]
    own = meta[RELAY] == 0
    line[0] = direct[:, :wide]
    line[1, :, :CUT] = direct[:, wide:]
    line[1, :, CUT:] = jnp.where(own, detour[...], jnp.zeros_like(detour)) + relayed[...]


def dot(a, b):
    return jnp.dot(a, b, preferred_element_type=jnp.float32)


def waves(turn, side):
    quarter = side // 4
    moved = turn + quarter // 2
    rest = (moved & (quarter - 1)) - quarter // 2
    which = (moved >> (quarter.bit_length() - 1)) & 3
    x = rest.astype(jnp.float32) * (2.0 * math.pi / side)
    y = x * x
    c = 1.0 + y * (-1 / 2 + y * (1 / 24 + y * (-1 / 720 + y * (1 / 40320))))
    s = x * (1.0 + y * (-1 / 6 + y * (1 / 120 + y * (-1 / 5040 + y * (1 / 362880)))))
    swapped = (which & 1) == 1
    first, second = jnp.where(swapped, s, c), jnp.where(swapped, c, s)
    cos = jnp.where((which == 1) | (which == 2), -first, first)
    sin = jnp.where(which >= 2, -second, second)
    return cos, sin


def table_blocks(shift, half, side):
    freq = 2 * lax.broadcasted_iota(jnp.int32, (half, half), 0)
    cell = lax.broadcasted_iota(jnp.int32, (half, half), 1) - shift
    norm = 1.0 / math.sqrt(side)
    out = []
    for odd in (0, 1):
        c, s = waves((freq + odd) * cell, side)
        c, s = c * norm, s * norm
        out.append((c, s, c.T, s.T))
    return out


def prepare_kernel(side, windows, meta, probe, measured, probes, tables, amps):
    half = side // 2
    bf = jnp.bfloat16
    rows = lax.broadcasted_iota(jnp.int32, (side, side), 0)
    cols = lax.broadcasted_iota(jnp.int32, (side, side), 1)
    place = jnp.where(cols < half, 2 * cols, 2 * (cols - half) + 1)
    picks = (rows == place).astype(jnp.float32).astype(bf)
    place_t = jnp.where(rows < half, 2 * rows, 2 * (rows - half) + 1)
    picks_t = (cols == place_t).astype(jnp.float32).astype(bf)

    def parts(x):
        high = x.astype(bf)
        rest = x - high.astype(jnp.float32)
        mid = rest.astype(bf)
        low = (rest - mid.astype(jnp.float32)).astype(bf)
        return high, mid, low

    def body(w, _):
        row = meta[OFFS + 2 * w] & (side - 1)
        col = meta[OFFS + 2 * w + 1] & (side - 1)
        for part in (0, 1):
            turned = pltpu.roll(probe[part], row, 0)
            probes[w, part] = pltpu.roll(turned, col, 1)
        for axis, shift in ((0, row), (1, col)):
            for odd, (c, s, ct, st) in enumerate(table_blocks(shift, half, side)):
                at = 4 * axis + 2 * odd
                tables[w, at, :half, :half] = c.astype(bf)
                tables[w, at, :half, half:] = s.astype(bf)
                tables[w, at, half:, :half] = (-s).astype(bf)
                tables[w, at, half:, half:] = c.astype(bf)
                tables[w, at + 1, :half, :half] = ct.astype(bf)
                tables[w, at + 1, :half, half:] = (-st).astype(bf)
                tables[w, at + 1, half:, :half] = st.astype(bf)
                tables[w, at + 1, half:, half:] = ct.astype(bf)
        a = [dot(x, picks) for x in parts(measured[w])]
        b = [dot(picks_t, x) for x in parts(a[0] + (a[1] + a[2]))]
        amps[w] = b[0] + (b[1] + b[2])
        return 0

    lax.fori_loop(0, windows, body, 0)


def gradient_kernel(
    side,
    windows,
    meta,
    centre,
    halo_direct,
    halo_detour,
    halo_relayed,
    halo_even,
    probes,
    tables,
    amps,
    grad,
    rim_direct,
    rim_detour,
    rim_even,
    band_odd,
    band_even,
    field,
    total,
    mixed,
    line,
):
    half = side // 2
    tile, wide = centre.shape[1:]
    bf = jnp.bfloat16
    odd_row = meta[GY_ODD]
    bottom = half + tile
    at_odd = pl.multiple_of(odd_row * bottom, half)
    at_even = pl.multiple_of((1 - odd_row) * bottom, half)
    field[:, pl.ds(half, tile), :] = centre[...]
    unpack(meta, halo_direct, halo_detour, halo_relayed, line)
    field[:, pl.ds(at_odd, half), :] = line[...]
    field[:, pl.ds(at_even, half), :] = halo_even[...]
    total[...] = jnp.zeros_like(total)
    chunk = 32
    zero = jnp.float32(0)

    for w in range(windows):
        a, b = meta[OFFS + 2 * w], meta[OFFS + 2 * w + 1]
        live = w < meta[LIVE]
        hi_a, hi_b = (a >= side).astype(jnp.int32), (b >= side).astype(jnp.int32)
        row0, col0 = pl.multiple_of(hi_a * side, side), pl.multiple_of(hi_b * side, side)
        row_in, col_in = a - row0, b - col0
        near = lax.broadcasted_iota(jnp.int32, (chunk, side), 1) >= col_in

        def below(start):
            return (lax.broadcasted_iota(jnp.int32, (chunk, side), 0) + start) >= row_in

        def patch(part, start):
            def at(i, j):
                return field[
                    part,
                    pl.ds(pl.multiple_of(row0 + i * side + start, chunk), chunk),
                    pl.ds(pl.multiple_of(col0 + j * side, side), side),
                ]

            return jnp.where(
                below(start),
                jnp.where(near, at(0, 0), at(0, 1)),
                jnp.where(near, at(1, 0), at(1, 1)),
            )

        def exits(start):
            real, imag = patch(0, start), patch(1, start)
            p_real = probes[w, 0, pl.ds(start, chunk), :]
            p_imag = probes[w, 1, pl.ds(start, chunk), :]
            return p_real * real - p_imag * imag, p_real * imag + p_imag * real

        for i in range(0, half, chunk):
            r0, i0 = exits(i)
            r1, i1 = exits(half + i)
            mixed[0, i : i + chunk, :] = (r0 + r1).astype(bf)
            mixed[0, half + i : half + i + chunk, :] = (i0 + i1).astype(bf)
            mixed[1, i : i + chunk, :] = (r0 - r1).astype(bf)
            mixed[1, half + i : half + i + chunk, :] = (i0 - i1).astype(bf)

        plus, minus = [], []
        for odd in (0, 1):
            h = dot(tables[w, 2 * odd], mixed[odd])
            re0, re1 = h[:half, :half], h[:half, half:]
            im0, im1 = h[half:, :half], h[half:, half:]
            plus.append(jnp.concatenate([re0 + re1, im0 + im1], axis=1).astype(bf))
            minus.append(jnp.concatenate([re0 - re1, im0 - im1], axis=1).astype(bf))

        backs = []
        for odd, sides in ((0, plus), (1, minus)):
            far = dot(jnp.concatenate(sides, axis=0), tables[w, 4 + 2 * odd + 1])
            re, im = far[:, :half], far[:, half:]
            power = jnp.maximum(re * re + im * im, amplitude_floor * amplitude_floor)
            factor = 1.0 - amps[w, :, odd * half : (odd + 1) * half] * lax.rsqrt(power)
            chi = jnp.concatenate([re * factor, im * factor], axis=1).astype(bf)
            backs.append(dot(chi, tables[w, 4 + 2 * odd]))
        left, right = backs[0] + backs[1], backs[0] - backs[1]

        outs = []
        for odd in (0, 1):
            at = slice(odd * half, (odd + 1) * half)
            real = jnp.concatenate([left[at, :half], right[at, :half]], axis=1)
            imag = jnp.concatenate([left[at, half:], right[at, half:]], axis=1)
            stacked = jnp.concatenate([real, imag], axis=0).astype(bf)
            outs.append(dot(tables[w, 2 * odd + 1], stacked))
        upper, lower = outs[0] + outs[1], outs[0] - outs[1]

        for start in range(0, side, chunk):
            back = upper if start < half else lower
            at = start % half
            b_real, b_imag = back[at : at + chunk], back[half + at : half + at + chunk]
            p_real = probes[w, 0, pl.ds(start, chunk), :]
            p_imag = probes[w, 1, pl.ds(start, chunk), :]
            terms = (p_real * b_real + p_imag * b_imag, p_real * b_imag - p_imag * b_real)
            rows_in = below(start)
            for part in (0, 1):
                for i, j in ((0, 0), (0, 1), (1, 0), (1, 1)):
                    keep = (rows_in if i == 0 else ~rows_in) & (near if j == 0 else ~near)
                    place = (
                        part,
                        pl.ds(pl.multiple_of(row0 + i * side + start, chunk), chunk),
                        pl.ds(pl.multiple_of(col0 + j * side, side), side),
                    )
                    total[place] = total[place] + jnp.where(keep & live, terms[part], zero)

    grad[...] = total[:, pl.ds(half, tile), :]
    odd_rows = pl.ds(at_odd, half)
    pack(total[0, odd_rows, :], total[1, odd_rows, :], rim_direct, rim_detour)
    rim_even[...] = total[:, pl.ds(at_even, half), :]
    for band, cols in (
        (band_odd, odd_side(meta, band_odd, wide)),
        (band_even, even_side(meta, band_even, wide)),
    ):
        band[...] = total[:, side:tile, cols]


def odd_side(meta, band, wide):
    return pl.ds(pl.multiple_of(meta[GX_ODD] * (wide - band.shape[2]), 128), band.shape[2])


def even_side(meta, band, wide):
    return pl.ds(pl.multiple_of((1 - meta[GX_ODD]) * (wide - band.shape[2]), 128), band.shape[2])


def rim_rows(meta, half):
    odd_row = meta[GY_ODD]
    return (
        pl.ds(pl.multiple_of(odd_row * half, half), half),
        pl.ds(pl.multiple_of((1 - odd_row) * half, half), half),
    )


def sides_kernel(meta, own, rim_odd, rim_even, mid_odd, mid_even):
    tile, half = own.shape[1], rim_odd.shape[2]
    far = tile - half
    for rim, mid, cols in (
        (rim_odd, mid_odd, odd_side(meta, rim_odd, tile)),
        (rim_even, mid_even, even_side(meta, rim_even, tile)),
    ):
        rim[:, :half, :] = own[:, :half, cols]
        rim[:, half:, :] = own[:, far:, cols]
        mid[...] = own[:, half:far, cols]


def edges_kernel(meta, own, side_odd, side_even, _, direct, detour, even, lines):
    tile, half = own.shape[1], side_odd.shape[2]
    wide = lines.shape[2]
    for at, rows in ((0, slice(0, half)), (half, slice(tile - half, tile))):
        lines[:, at : at + half, half : half + tile] = own[:, rows, :]
    lines[:, :, odd_side(meta, side_odd, wide)] = side_odd[...]
    lines[:, :, even_side(meta, side_even, wide)] = side_even[...]
    odd_rows, even_rows = rim_rows(meta, half)
    pack(lines[0, odd_rows, :], lines[1, odd_rows, :], direct, detour)
    even[...] = lines[:, even_rows, :]


def centre_kernel(meta, own, lines, side_odd, side_even, centre):
    tile, half = own.shape[1], side_odd.shape[2]
    wide = lines.shape[2]
    mid = slice(half, tile - half)
    centre[:, :half, :] = lines[:, :half, :]
    centre[:, tile - half :, :] = lines[:, half:, :]
    centre[:, mid, half : half + tile] = own[:, mid, :]
    centre[:, mid, odd_side(meta, side_odd, wide)] = side_odd[...]
    centre[:, mid, even_side(meta, side_even, wide)] = side_even[...]


def bands_kernel(meta, grad, direct, detour, relayed, even, band_odd, band_even, line):
    (tile, wide), half = grad.shape[1:], even.shape[1]
    unpack(meta, direct, detour, relayed, line)
    odd_rows, even_rows = rim_rows(meta, half)
    for band, cols in ((band_odd, odd_side(meta, band_odd, wide)), (band_even, even_side(meta, band_even, wide))):
        band[:, :half, :] = grad[:, :half, cols]
        band[:, half:, :] = grad[:, tile - half :, cols]
        band[:, odd_rows, :] = band[:, odd_rows, :] + line[:, :, cols]
        band[:, even_rows, :] = band[:, even_rows, :] + even[:, :, cols]


def clear_outside(meta, cells, half):
    wide = cells.shape[2]

    @pl.when(meta[EDGE] == 1)
    def _():
        outside = pl.ds(pl.multiple_of(meta[GX_ODD] * (wide - half), half), half)
        cells[:, :, outside] = jnp.zeros((*cells.shape[:2], half), jnp.float32)


def update_edges_kernel(
    meta, centre, grad, line, even, band_odd, band_even, direct, detour, out_even, lines
):
    (tile, wide), half = grad.shape[1:], even.shape[1]
    odd_rows, even_rows = rim_rows(meta, half)
    for at, rows in ((0, slice(0, half)), (half, slice(tile - half, tile))):
        lines[:, at : at + half, :] = centre[:, rows, :] - step_size * grad[:, rows, :]
    lines[:, odd_rows, :] = lines[:, odd_rows, :] - step_size * line[...]
    lines[:, even_rows, :] = lines[:, even_rows, :] - step_size * even[...]
    for band, cols in ((band_odd, odd_side(meta, band_odd, wide)), (band_even, even_side(meta, band_even, wide))):
        lines[:, :, cols] = lines[:, :, cols] - step_size * band[...]
    clear_outside(meta, lines, half)
    pack(lines[0, odd_rows, :], lines[1, odd_rows, :], direct, detour)
    out_even[...] = lines[:, even_rows, :]


def update_centre_kernel(meta, centre, grad, lines, band_odd, band_even, fresh):
    tile, wide = grad.shape[1:]
    half = lines.shape[1] // 2
    mid = slice(half, tile - half)
    fresh[:, mid, :] = centre[:, mid, :] - step_size * grad[:, mid, :]
    for band, cols in ((band_odd, odd_side(meta, band_odd, wide)), (band_even, even_side(meta, band_even, wide))):
        fresh[:, mid, cols] = fresh[:, mid, cols] - step_size * band[...]
    clear_outside(meta, fresh, half)
    fresh[:, :half, :] = lines[:, :half, :]
    fresh[:, tile - half :, :] = lines[:, half:, :]


def final_kernel(meta, centre, grad, line, even, mid_odd, mid_even, rim_odd, rim_even, out):
    tile, half = grad.shape[1], even.shape[1]
    own = slice(half, half + tile)
    odd_row = meta[GY_ODD]
    far = tile - half
    out[...] = centre[:, :, own] - step_size * grad[:, :, own]
    for at, rim in ((odd_row * far, line), ((1 - odd_row) * far, even)):
        rows = pl.ds(pl.multiple_of(at, half), half)
        out[:, rows, :] = out[:, rows, :] - step_size * rim[:, :, own]
    for mid, rim, cols in (
        (mid_odd, rim_odd, odd_side(meta, mid_odd, tile)),
        (mid_even, rim_even, even_side(meta, mid_even, tile)),
    ):
        out[:, :half, cols] = out[:, :half, cols] - step_size * rim[:, :half, :]
        out[:, half:far, cols] = out[:, half:far, cols] - step_size * mid[...]
        out[:, far:, cols] = out[:, far:, cols] - step_size * rim[:, half:, :]


def call(kernel, meta, arrays, outs, scratch=(), flops=0, room=0, after=None):
    f32 = jnp.float32
    shapes = [
        jax.ShapeDtypeStruct(*o) if isinstance(o[0], tuple) else jax.ShapeDtypeStruct(o, f32)
        for o in outs
    ]
    shapes_in = [jax.ShapeDtypeStruct(x.shape, x.dtype) for x in arrays]
    moved = sum(math.prod(x.shape) * x.dtype.itemsize for x in [*shapes_in, *shapes])
    late = [] if after is None else [after]
    smem = pl.BlockSpec(memory_space=pltpu.SMEM)
    vmem = pl.BlockSpec(memory_space=pltpu.VMEM)
    anywhere = pl.BlockSpec(memory_space=pl.ANY)
    return pl.pallas_call(
        kernel,
        out_shape=shapes,
        in_specs=[smem] + [vmem] * len(arrays) + [anywhere] * len(late),
        out_specs=[vmem] * len(shapes),
        scratch_shapes=list(scratch),
        compiler_params=pltpu.CompilerParams(vmem_limit_bytes=room or moved + MIB),
        cost_estimate=pl.CostEstimate(flops=flops, bytes_accessed=moved, transcendentals=0),
    )(meta, *arrays, *late)


def local(object_field, probe_field, measured, offsets, counts):
    tile = object_field.shape[1]
    side = probe_field.shape[1]
    half = side // 2
    windows = offsets.shape[2]
    wide = tile + side
    bf, f32 = jnp.bfloat16, jnp.float32
    place_col, columns_of_tiles = lax.axis_index("gx"), lax.axis_size("gx")
    odd_col = place_col % 2
    edge = (place_col == 0) | (place_col == columns_of_tiles - 1)
    place_row, rows_of_tiles = lax.axis_index("gy"), lax.axis_size("gy")
    odd_row = place_row % 2
    relay = (place_row == 0) | (place_row == rows_of_tiles - 1)
    places = jnp.stack([odd_col, odd_row, edge.astype(jnp.int32), relay.astype(jnp.int32)])
    meta = jnp.concatenate([places, counts[0], offsets[0, 0].reshape(-1)]).astype(jnp.int32)

    column, band = (2, 2 * half, half), (2, 2 * half, side)
    mid_column, mid_band = (2, tile - 2 * half, half), (2, tile - 2 * half, side)
    middle, lines = (2, tile, wide), (2, 2 * half, wide)
    line = (2, half, wide)
    sends = ((half, wide + CUT), (half, wide - CUT), line)

    *rims, mid_odd, mid_even = call(
        sides_kernel,
        places,
        (object_field,),
        (column, column, mid_column, mid_column),
    )
    rims = swap_columns(*rims)
    mids = swap_columns(mid_odd, mid_even)
    probes, tables, amps = call(
        functools.partial(prepare_kernel, side, windows),
        meta,
        (probe_field, measured[0, 0]),
        ((windows, 2, side, side), ((windows, 8, side, side), bf), (windows, side, side)),
        flops=10**9,
        room=20 * MIB,
    )
    *edges, rows = call(edges_kernel, meta, (object_field, *rims), (*sends, lines), after=amps)
    halos = swap_rows(*edges)
    (centre,) = call(centre_kernel, meta, (object_field, rows, *mids), (middle,))
    for iteration in range(ITERS):
        last = iteration + 1 == ITERS
        grad, *rims, mid_odd, mid_even = call(
            functools.partial(gradient_kernel, side, windows),
            meta,
            (centre, *halos, probes, tables, amps),
            (middle, *sends, *((mid_column if last else mid_band),) * 2),
            scratch=(
                pltpu.VMEM((2, wide, wide), f32),
                pltpu.VMEM((2, wide, wide), f32),
                pltpu.VMEM((2, side, side), bf),
                pltpu.VMEM(line, f32),
            ),
            flops=windows * 16 * side**3,
            room=24 * MIB,
        )
        rims = swap_rows(*rims)
        shape = column if last else band
        *bands, odd_line = call(bands_kernel, meta, (grad, *rims), (shape, shape, line))
        bands = swap_columns(*bands)
        mids = swap_columns(mid_odd, mid_even)
        if last:
            break
        *edges, rows = call(
            update_edges_kernel,
            meta,
            (centre, grad, odd_line, rims[3], *bands),
            (*sends, lines),
        )
        halos = swap_rows(*edges)
        (centre,) = call(update_centre_kernel, meta, (centre, grad, rows, *mids), (middle,))
    (updated,) = call(
        final_kernel,
        meta,
        (centre, grad, odd_line, rims[3], *mids, *bands),
        (object_field.shape,),
    )
    return updated


def solution(mesh):
    return jax.shard_map(
        local,
        mesh=mesh,
        in_specs=(
            P(None, "gy", "gx"),
            P(),
            P("gy", "gx", None, None, None),
            P("gy", "gx", None, None),
            P("gy", "gx"),
        ),
        out_specs=P(None, "gy", "gx"),
        check_vma=False,
    )
```

```python
import functools
import math

import jax
import jax.numpy as jnp
from jax import lax
from jax.experimental import pallas as pl
from jax.experimental.pallas import tpu as pltpu
from jax.sharding import PartitionSpec as P


ITERS = 2
step_size = 0.25
amplitude_floor = 0.5

MIB = 1 << 20

GX_ODD, GY_ODD, EDGE, RELAY, LIVE, OFFS = 0, 1, 2, 3, 4, 5


def pairs(count, first):
    ups = [(i, i + 1) for i in range(first, count - 1, 2)]
    return ups + [(b, a) for a, b in ups]


def swap_rows(direct, detour, even_cells):
    count = lax.axis_size("gy")
    low = count // 2 - 1
    far = [(low, low + 1), (low + 1, low)]
    near = [p for p in pairs(count, 1) if p not in far]
    first = lax.ppermute(detour, "gy", near + [(low, 0), (low + 1, count - 1)])
    straight = lax.ppermute(direct, "gy", near + far)
    even = lax.ppermute(even_cells, "gy", pairs(count, 0))
    second = lax.ppermute(first, "gy", [(0, low + 1), (count - 1, low)])
    return straight, first, second, even


def swap_columns(odd_cells, even_cells):
    count = lax.axis_size("gx")
    from_odd = lax.ppermute(odd_cells, "gx", pairs(count, 1))
    from_even = lax.ppermute(even_cells, "gx", pairs(count, 0))
    return from_odd, from_even


CUT = 128


def pack(real, imag, direct, detour):
    straight = direct.shape[1]
    direct[...] = real[:, :straight]
    detour[:, :CUT] = real[:, straight:]
    detour[:, CUT:] = imag


def unpack(meta, direct, detour, relayed, line):
    straight = direct.shape[1]
    own = meta[RELAY] == 0
    line[0, :, :straight] = direct[...]
    rest = jnp.where(own, detour[...], jnp.zeros_like(detour)) + relayed[...]
    line[0, :, straight:] = rest[:, :CUT]
    line[1] = rest[:, CUT:]


def dot(a, b):
    return jnp.dot(a, b, preferred_element_type=jnp.float32)


def waves(turn, side):
    quarter = side // 4
    moved = turn + quarter // 2
    rest = (moved & (quarter - 1)) - quarter // 2
    which = (moved >> (quarter.bit_length() - 1)) & 3
    x = rest.astype(jnp.float32) * (2.0 * math.pi / side)
    y = x * x
    c = 1.0 + y * (-1 / 2 + y * (1 / 24 + y * (-1 / 720 + y * (1 / 40320))))
    s = x * (1.0 + y * (-1 / 6 + y * (1 / 120 + y * (-1 / 5040 + y * (1 / 362880)))))
    swapped = (which & 1) == 1
    first, second = jnp.where(swapped, s, c), jnp.where(swapped, c, s)
    cos = jnp.where((which == 1) | (which == 2), -first, first)
    sin = jnp.where(which >= 2, -second, second)
    return cos, sin


def table_blocks(shift, half, side):
    freq = 2 * lax.broadcasted_iota(jnp.int32, (half, half), 0)
    cell = lax.broadcasted_iota(jnp.int32, (half, half), 1) - shift
    norm = 1.0 / math.sqrt(side)
    out = []
    for odd in (0, 1):
        c, s = waves((freq + odd) * cell, side)
        c, s = c * norm, s * norm
        out.append((c, s, c.T, s.T))
    return out


def prepare_kernel(side, windows, meta, probe, measured, probes, tables, amps):
    half = side // 2
    bf = jnp.bfloat16
    rows = lax.broadcasted_iota(jnp.int32, (side, side), 0)
    cols = lax.broadcasted_iota(jnp.int32, (side, side), 1)
    place = jnp.where(cols < half, 2 * cols, 2 * (cols - half) + 1)
    picks = (rows == place).astype(jnp.float32).astype(bf)
    place_t = jnp.where(rows < half, 2 * rows, 2 * (rows - half) + 1)
    picks_t = (cols == place_t).astype(jnp.float32).astype(bf)

    def parts(x):
        high = x.astype(bf)
        rest = x - high.astype(jnp.float32)
        mid = rest.astype(bf)
        low = (rest - mid.astype(jnp.float32)).astype(bf)
        return high, mid, low

    def body(w, _):
        row = meta[OFFS + 2 * w] & (side - 1)
        col = meta[OFFS + 2 * w + 1] & (side - 1)
        for part in (0, 1):
            turned = pltpu.roll(probe[part], row, 0)
            probes[w, part] = pltpu.roll(turned, col, 1)
        for axis, shift in ((0, row), (1, col)):
            for odd, (c, s, ct, st) in enumerate(table_blocks(shift, half, side)):
                at = 4 * axis + 2 * odd
                tables[w, at, :half, :half] = c.astype(bf)
                tables[w, at, :half, half:] = s.astype(bf)
                tables[w, at, half:, :half] = (-s).astype(bf)
                tables[w, at, half:, half:] = c.astype(bf)
                tables[w, at + 1, :half, :half] = ct.astype(bf)
                tables[w, at + 1, :half, half:] = (-st).astype(bf)
                tables[w, at + 1, half:, :half] = st.astype(bf)
                tables[w, at + 1, half:, half:] = ct.astype(bf)
        a = [dot(x, picks) for x in parts(measured[w])]
        b = [dot(picks_t, x) for x in parts(a[0] + (a[1] + a[2]))]
        amps[w] = b[0] + (b[1] + b[2])
        return 0

    lax.fori_loop(0, windows, body, 0)


def gradient_kernel(
    side,
    windows,
    meta,
    _field,
    _total,
    halo_direct,
    halo_detour,
    halo_relayed,
    halo_even,
    probes,
    tables,
    amps,
    field,
    total,
    rim_direct,
    rim_detour,
    rim_even,
    band_odd,
    band_even,
    mixed,
):
    half = side // 2
    wide = field.shape[2]
    tile = wide - side
    bf = jnp.bfloat16
    odd_row = meta[GY_ODD]
    bottom = half + tile
    odd_rows = pl.ds(pl.multiple_of(odd_row * bottom, half), half)
    even_rows = pl.ds(pl.multiple_of((1 - odd_row) * bottom, half), half)
    unpack(meta, halo_direct, halo_detour, halo_relayed, field.at[:, odd_rows, :])
    field[:, even_rows, :] = halo_even[...]
    chunk = 32
    zero = jnp.float32(0)

    for w in range(windows):
        a, b = meta[OFFS + 2 * w], meta[OFFS + 2 * w + 1]
        live = w < meta[LIVE]
        hi_a, hi_b = (a >= side).astype(jnp.int32), (b >= side).astype(jnp.int32)
        row0, col0 = pl.multiple_of(hi_a * side, side), pl.multiple_of(hi_b * side, side)
        row_in, col_in = a - row0, b - col0
        near = lax.broadcasted_iota(jnp.int32, (chunk, side), 1) >= col_in

        def below(start):
            return (lax.broadcasted_iota(jnp.int32, (chunk, side), 0) + start) >= row_in

        def patch(part, start):
            def at(i, j):
                return field[
                    part,
                    pl.ds(pl.multiple_of(row0 + i * side + start, chunk), chunk),
                    pl.ds(pl.multiple_of(col0 + j * side, side), side),
                ]

            return jnp.where(
                below(start),
                jnp.where(near, at(0, 0), at(0, 1)),
                jnp.where(near, at(1, 0), at(1, 1)),
            )

        def exits(start):
            real, imag = patch(0, start), patch(1, start)
            p_real = probes[w, 0, pl.ds(start, chunk), :]
            p_imag = probes[w, 1, pl.ds(start, chunk), :]
            return p_real * real - p_imag * imag, p_real * imag + p_imag * real

        for i in range(0, half, chunk):
            r0, i0 = exits(i)
            r1, i1 = exits(half + i)
            mixed[0, i : i + chunk, :] = (r0 + r1).astype(bf)
            mixed[0, half + i : half + i + chunk, :] = (i0 + i1).astype(bf)
            mixed[1, i : i + chunk, :] = (r0 - r1).astype(bf)
            mixed[1, half + i : half + i + chunk, :] = (i0 - i1).astype(bf)

        plus, minus = [], []
        for odd in (0, 1):
            h = dot(tables[w, 2 * odd], mixed[odd])
            re0, re1 = h[:half, :half], h[:half, half:]
            im0, im1 = h[half:, :half], h[half:, half:]
            plus.append(jnp.concatenate([re0 + re1, im0 + im1], axis=1).astype(bf))
            minus.append(jnp.concatenate([re0 - re1, im0 - im1], axis=1).astype(bf))

        backs = []
        for odd, sides in ((0, plus), (1, minus)):
            far = dot(jnp.concatenate(sides, axis=0), tables[w, 4 + 2 * odd + 1])
            re, im = far[:, :half], far[:, half:]
            power = jnp.maximum(re * re + im * im, amplitude_floor * amplitude_floor)
            factor = 1.0 - amps[w, :, odd * half : (odd + 1) * half] * lax.rsqrt(power)
            chi = jnp.concatenate([re * factor, im * factor], axis=1).astype(bf)
            backs.append(dot(chi, tables[w, 4 + 2 * odd]))
        left, right = backs[0] + backs[1], backs[0] - backs[1]

        outs = []
        for odd in (0, 1):
            at = slice(odd * half, (odd + 1) * half)
            real = jnp.concatenate([left[at, :half], right[at, :half]], axis=1)
            imag = jnp.concatenate([left[at, half:], right[at, half:]], axis=1)
            stacked = jnp.concatenate([real, imag], axis=0).astype(bf)
            outs.append(dot(tables[w, 2 * odd + 1], stacked))
        upper, lower = outs[0] + outs[1], outs[0] - outs[1]

        for start in range(0, side, chunk):
            back = upper if start < half else lower
            at = start % half
            b_real, b_imag = back[at : at + chunk], back[half + at : half + at + chunk]
            p_real = probes[w, 0, pl.ds(start, chunk), :]
            p_imag = probes[w, 1, pl.ds(start, chunk), :]
            terms = (p_real * b_real + p_imag * b_imag, p_real * b_imag - p_imag * b_real)
            rows_in = below(start)
            for part in (0, 1):
                for i, j in ((0, 0), (0, 1), (1, 0), (1, 1)):
                    keep = (rows_in if i == 0 else ~rows_in) & (near if j == 0 else ~near)
                    place = (
                        part,
                        pl.ds(pl.multiple_of(row0 + i * side + start, chunk), chunk),
                        pl.ds(pl.multiple_of(col0 + j * side, side), side),
                    )
                    total[place] = total[place] + jnp.where(keep & live, terms[part], zero)

    pack(total[0, odd_rows, :], total[1, odd_rows, :], rim_direct, rim_detour)
    rim_even[...] = total[:, even_rows, :]
    for band, cols in (
        (band_odd, odd_side(meta, band_odd, wide)),
        (band_even, even_side(meta, band_even, wide)),
    ):
        band[...] = total[:, side:tile, cols]


def odd_side(meta, band, wide):
    return pl.ds(pl.multiple_of(meta[GX_ODD] * (wide - band.shape[2]), 128), band.shape[2])


def even_side(meta, band, wide):
    return pl.ds(pl.multiple_of((1 - meta[GX_ODD]) * (wide - band.shape[2]), 128), band.shape[2])


def rim_rows(meta, half):
    odd_row = meta[GY_ODD]
    return (
        pl.ds(pl.multiple_of(odd_row * half, half), half),
        pl.ds(pl.multiple_of((1 - odd_row) * half, half), half),
    )


def sides_kernel(meta, own, rim_odd, rim_even, mid_odd, mid_even):
    tile, half = own.shape[1], rim_odd.shape[2]
    far = tile - half
    for rim, mid, cols in (
        (rim_odd, mid_odd, odd_side(meta, rim_odd, tile)),
        (rim_even, mid_even, even_side(meta, rim_even, tile)),
    ):
        rim[:, :half, :] = own[:, :half, cols]
        rim[:, half:, :] = own[:, far:, cols]
        mid[...] = own[:, half:far, cols]


def edges_kernel(meta, own, side_odd, side_even, _, direct, detour, even, lines):
    tile, half = own.shape[1], side_odd.shape[2]
    wide = lines.shape[2]
    for at, rows in ((0, slice(0, half)), (half, slice(tile - half, tile))):
        lines[:, at : at + half, half : half + tile] = own[:, rows, :]
    lines[:, :, odd_side(meta, side_odd, wide)] = side_odd[...]
    lines[:, :, even_side(meta, side_even, wide)] = side_even[...]
    odd_rows, even_rows = rim_rows(meta, half)
    pack(lines[0, odd_rows, :], lines[1, odd_rows, :], direct, detour)
    even[...] = lines[:, even_rows, :]


def inner_rows(half, tile):
    return (
        (slice(half, 2 * half), slice(0, half)),
        (slice(tile, half + tile), slice(half, 2 * half)),
        slice(2 * half, tile),
    )


def centre_kernel(meta, own, lines, side_odd, side_even, field, total):
    tile, half = own.shape[1], side_odd.shape[2]
    wide = lines.shape[2]
    first, last, mid = inner_rows(half, tile)
    for rows, outer in (first, last):
        field[:, rows, :] = lines[:, outer, :]
    field[:, mid, half : half + tile] = own[:, half : tile - half, :]
    field[:, mid, odd_side(meta, side_odd, wide)] = side_odd[...]
    field[:, mid, even_side(meta, side_even, wide)] = side_even[...]
    total[...] = jnp.zeros_like(total)


def bands_kernel(meta, total, direct, detour, relayed, even, band_odd, band_even, line):
    wide, half = total.shape[2], even.shape[1]
    unpack(meta, direct, detour, relayed, line)
    odd_rows, even_rows = rim_rows(meta, half)
    first, last, _ = inner_rows(half, wide - 2 * half)
    for band, cols in (
        (band_odd, odd_side(meta, band_odd, wide)),
        (band_even, even_side(meta, band_even, wide)),
    ):
        for rows, outer in (first, last):
            band[:, outer, :] = total[:, rows, cols]
        band[:, odd_rows, :] = band[:, odd_rows, :] + line[:, :, cols]
        band[:, even_rows, :] = band[:, even_rows, :] + even[:, :, cols]


def clear_outside(meta, cells, half):
    wide = cells.shape[2]

    @pl.when(meta[EDGE] == 1)
    def _():
        outside = pl.ds(pl.multiple_of(meta[GX_ODD] * (wide - half), half), half)
        cells[:, :, outside] = jnp.zeros((*cells.shape[:2], half), jnp.float32)


def update_edges_kernel(
    meta, field, total, line, even, band_odd, band_even, direct, detour, out_even, lines
):
    wide, half = total.shape[2], even.shape[1]
    odd_rows, even_rows = rim_rows(meta, half)
    first, last, _ = inner_rows(half, wide - 2 * half)
    for rows, outer in (first, last):
        lines[:, outer, :] = field[:, rows, :] - step_size * total[:, rows, :]
    lines[:, odd_rows, :] = lines[:, odd_rows, :] - step_size * line[...]
    lines[:, even_rows, :] = lines[:, even_rows, :] - step_size * even[...]
    for band, cols in (
        (band_odd, odd_side(meta, band_odd, wide)),
        (band_even, even_side(meta, band_even, wide)),
    ):
        lines[:, :, cols] = lines[:, :, cols] - step_size * band[...]
    clear_outside(meta, lines, half)
    pack(lines[0, odd_rows, :], lines[1, odd_rows, :], direct, detour)
    out_even[...] = lines[:, even_rows, :]


def update_centre_kernel(meta, field, total, lines, band_odd, band_even, fresh, zeros):
    wide, half = total.shape[2], lines.shape[1] // 2
    first, last, mid = inner_rows(half, wide - 2 * half)
    fresh[:, mid, :] = field[:, mid, :] - step_size * total[:, mid, :]
    for band, cols in (
        (band_odd, odd_side(meta, band_odd, wide)),
        (band_even, even_side(meta, band_even, wide)),
    ):
        fresh[:, mid, cols] = fresh[:, mid, cols] - step_size * band[...]
    clear_outside(meta, fresh.at[:, mid, :], half)
    for rows, outer in (first, last):
        fresh[:, rows, :] = lines[:, outer, :]
    zeros[...] = jnp.zeros_like(zeros)


def final_kernel(meta, field, total, line, even, mid_odd, mid_even, rim_odd, rim_even, out):
    tile, half = out.shape[1], even.shape[1]
    own = slice(half, half + tile)
    odd_row = meta[GY_ODD]
    far = tile - half
    out[...] = field[:, own, own] - step_size * total[:, own, own]
    for at, rim in ((odd_row * far, line), ((1 - odd_row) * far, even)):
        rows = pl.ds(pl.multiple_of(at, half), half)
        out[:, rows, :] = out[:, rows, :] - step_size * rim[:, :, own]
    for mid, rim, cols in (
        (mid_odd, rim_odd, odd_side(meta, mid_odd, tile)),
        (mid_even, rim_even, even_side(meta, mid_even, tile)),
    ):
        out[:, :half, cols] = out[:, :half, cols] - step_size * rim[:, :half, :]
        out[:, half:far, cols] = out[:, half:far, cols] - step_size * mid[...]
        out[:, far:, cols] = out[:, far:, cols] - step_size * rim[:, half:, :]


def call(kernel, meta, arrays, outs, scratch=(), flops=0, room=0, after=None, aliases=None):
    f32 = jnp.float32
    shapes = [
        jax.ShapeDtypeStruct(*o) if isinstance(o[0], tuple) else jax.ShapeDtypeStruct(o, f32)
        for o in outs
    ]
    shapes_in = [jax.ShapeDtypeStruct(x.shape, x.dtype) for x in arrays]
    moved = sum(math.prod(x.shape) * x.dtype.itemsize for x in [*shapes_in, *shapes])
    late = [] if after is None else [after]
    smem = pl.BlockSpec(memory_space=pltpu.SMEM)
    vmem = pl.BlockSpec(memory_space=pltpu.VMEM)
    anywhere = pl.BlockSpec(memory_space=pl.ANY)
    return pl.pallas_call(
        kernel,
        out_shape=shapes,
        in_specs=[smem] + [vmem] * len(arrays) + [anywhere] * len(late),
        out_specs=[vmem] * len(shapes),
        scratch_shapes=list(scratch),
        input_output_aliases=aliases or {},
        compiler_params=pltpu.CompilerParams(vmem_limit_bytes=room or min(moved + MIB, 6 * MIB)),
        cost_estimate=pl.CostEstimate(flops=flops, bytes_accessed=moved, transcendentals=0),
    )(meta, *arrays, *late)


def local(object_field, probe_field, measured, offsets, counts):
    tile = object_field.shape[1]
    side = probe_field.shape[1]
    half = side // 2
    windows = offsets.shape[2]
    wide = tile + side
    bf = jnp.bfloat16
    place_col, columns_of_tiles = lax.axis_index("gx"), lax.axis_size("gx")
    odd_col = place_col % 2
    edge = (place_col == 0) | (place_col == columns_of_tiles - 1)
    place_row, rows_of_tiles = lax.axis_index("gy"), lax.axis_size("gy")
    odd_row = place_row % 2
    relay = (place_row == 0) | (place_row == rows_of_tiles - 1)
    places = jnp.stack([odd_col, odd_row, edge.astype(jnp.int32), relay.astype(jnp.int32)])
    meta = jnp.concatenate([places, counts[0], offsets[0, 0].reshape(-1)]).astype(jnp.int32)

    column, band = (2, 2 * half, half), (2, 2 * half, side)
    mid_column, mid_band = (2, tile - 2 * half, half), (2, tile - 2 * half, side)
    whole, lines = (2, wide, wide), (2, 2 * half, wide)
    line = (2, half, wide)
    sends = ((half, wide - CUT), (half, wide + CUT), line)

    *rims, mid_odd, mid_even = call(
        sides_kernel,
        places,
        (object_field,),
        (column, column, mid_column, mid_column),
    )
    rims = swap_columns(*rims)
    mids = swap_columns(mid_odd, mid_even)
    probes, tables, amps = call(
        functools.partial(prepare_kernel, side, windows),
        meta,
        (probe_field, measured[0, 0]),
        ((windows, 2, side, side), ((windows, 8, side, side), bf), (windows, side, side)),
        flops=10**9,
        room=12 * MIB,
    )
    *edges, rows = call(edges_kernel, meta, (object_field, *rims), (*sends, lines), after=amps)
    halos = swap_rows(*edges)
    field, total = call(centre_kernel, meta, (object_field, rows, *mids), (whole, whole))
    for iteration in range(ITERS):
        last = iteration + 1 == ITERS
        field, total, *rims, mid_odd, mid_even = call(
            functools.partial(gradient_kernel, side, windows),
            meta,
            (field, total, *halos, probes, tables, amps),
            (whole, whole, *sends, *((mid_column if last else mid_band),) * 2),
            scratch=(pltpu.VMEM((2, side, side), bf),),
            aliases={1: 0, 2: 1},
            flops=windows * 16 * side**3,
            room=8 * MIB,
        )
        rims = swap_rows(*rims)
        shape = column if last else band
        *bands, odd_line = call(bands_kernel, meta, (total, *rims), (shape, shape, line))
        bands = swap_columns(*bands)
        mids = swap_columns(mid_odd, mid_even)
        if last:
            break
        *edges, rows = call(
            update_edges_kernel,
            meta,
            (field, total, odd_line, rims[3], *bands),
            (*sends, lines),
        )
        halos = swap_rows(*edges)
        field, total = call(
            update_centre_kernel, meta, (field, total, rows, *mids), (whole, whole)
        )
    (updated,) = call(
        final_kernel,
        meta,
        (field, total, odd_line, rims[3], *mids, *bands),
        (object_field.shape,),
    )
    return updated


def solution(mesh):
    return jax.shard_map(
        local,
        mesh=mesh,
        in_specs=(
            P(None, "gy", "gx"),
            P(),
            P("gy", "gx", None, None, None),
            P("gy", "gx", None, None),
            P("gy", "gx"),
        ),
        out_specs=P(None, "gy", "gx"),
        check_vma=False,
    )
```

```python
import functools
import math

import jax
import jax.numpy as jnp
from jax import lax
from jax.experimental import pallas as pl
from jax.experimental.pallas import tpu as pltpu
from jax.sharding import PartitionSpec as P


ITERS = 2
step_size = 0.25
amplitude_floor = 0.5

MIB = 1 << 20

GX_ODD, GY_ODD, EDGE, RELAY, LIVE, OFFS = 0, 1, 2, 3, 4, 5


def pairs(count, first):
    ups = [(i, i + 1) for i in range(first, count - 1, 2)]
    return ups + [(b, a) for a, b in ups]


def swap_rows(direct, detour, even_cells):
    count = lax.axis_size("gy")
    low = count // 2 - 1
    far = [(low, low + 1), (low + 1, low)]
    near = [p for p in pairs(count, 1) if p not in far]
    first = lax.ppermute(detour, "gy", near + [(low, 0), (low + 1, count - 1)])
    straight = lax.ppermute(direct, "gy", near + far)
    even = lax.ppermute(even_cells, "gy", pairs(count, 0))
    second = lax.ppermute(first, "gy", [(0, low + 1), (count - 1, low)])
    return straight, first, second, even


def swap_columns(odd_cells, even_cells):
    count = lax.axis_size("gx")
    from_odd = lax.ppermute(odd_cells, "gx", pairs(count, 1))
    from_even = lax.ppermute(even_cells, "gx", pairs(count, 0))
    return from_odd, from_even


CUT = 128


def pack(real, imag, direct, detour):
    wide = real.shape[1]
    direct[:, :wide] = real
    direct[:, wide:] = imag[:, :CUT]
    detour[...] = imag[:, CUT:]


def unpack(meta, direct, detour, relayed, line):
    wide = line.shape[2]
    own = meta[RELAY] == 0
    line[0] = direct[:, :wide]
    line[1, :, :CUT] = direct[:, wide:]
    line[1, :, CUT:] = jnp.where(own, detour[...], jnp.zeros_like(detour)) + relayed[...]


def dot(a, b):
    return jnp.dot(a, b, preferred_element_type=jnp.float32)


def waves(turn, side):
    quarter = side // 4
    moved = turn + quarter // 2
    rest = (moved & (quarter - 1)) - quarter // 2
    which = (moved >> (quarter.bit_length() - 1)) & 3
    x = rest.astype(jnp.float32) * (2.0 * math.pi / side)
    y = x * x
    c = 1.0 + y * (-1 / 2 + y * (1 / 24 + y * (-1 / 720 + y * (1 / 40320))))
    s = x * (1.0 + y * (-1 / 6 + y * (1 / 120 + y * (-1 / 5040 + y * (1 / 362880)))))
    swapped = (which & 1) == 1
    first, second = jnp.where(swapped, s, c), jnp.where(swapped, c, s)
    cos = jnp.where((which == 1) | (which == 2), -first, first)
    sin = jnp.where(which >= 2, -second, second)
    return cos, sin


def table_blocks(shift, half, side):
    freq = 2 * lax.broadcasted_iota(jnp.int32, (half, half), 0)
    cell = lax.broadcasted_iota(jnp.int32, (half, half), 1) - shift
    norm = 1.0 / math.sqrt(side)
    out = []
    for odd in (0, 1):
        c, s = waves((freq + odd) * cell, side)
        c, s = c * norm, s * norm
        out.append((c, s, c.T, s.T))
    return out


def prepare_kernel(side, windows, meta, probe, measured, probes, tables, amps):
    half = side // 2
    bf = jnp.bfloat16
    rows = lax.broadcasted_iota(jnp.int32, (side, side), 0)
    cols = lax.broadcasted_iota(jnp.int32, (side, side), 1)
    place = jnp.where(cols < half, 2 * cols, 2 * (cols - half) + 1)
    picks = (rows == place).astype(jnp.float32).astype(bf)
    place_t = jnp.where(rows < half, 2 * rows, 2 * (rows - half) + 1)
    picks_t = (cols == place_t).astype(jnp.float32).astype(bf)

    def parts(x):
        high = x.astype(bf)
        rest = x - high.astype(jnp.float32)
        mid = rest.astype(bf)
        low = (rest - mid.astype(jnp.float32)).astype(bf)
        return high, mid, low

    def body(w, _):
        row = meta[OFFS + 2 * w] & (side - 1)
        col = meta[OFFS + 2 * w + 1] & (side - 1)
        for part in (0, 1):
            turned = pltpu.roll(probe[part], row, 0)
            probes[w, part] = pltpu.roll(turned, col, 1)
        for axis, shift in ((0, row), (1, col)):
            for odd, (c, s, ct, st) in enumerate(table_blocks(shift, half, side)):
                at = 4 * axis + 2 * odd
                tables[w, at, :half, :half] = c.astype(bf)
                tables[w, at, :half, half:] = s.astype(bf)
                tables[w, at, half:, :half] = (-s).astype(bf)
                tables[w, at, half:, half:] = c.astype(bf)
                tables[w, at + 1, :half, :half] = ct.astype(bf)
                tables[w, at + 1, :half, half:] = (-st).astype(bf)
                tables[w, at + 1, half:, :half] = st.astype(bf)
                tables[w, at + 1, half:, half:] = ct.astype(bf)
        a = [dot(x, picks) for x in parts(measured[w])]
        b = [dot(picks_t, x) for x in parts(a[0] + (a[1] + a[2]))]
        amps[w] = b[0] + (b[1] + b[2])
        return 0

    lax.fori_loop(0, windows, body, 0)


def gradient_kernel(
    side,
    windows,
    meta,
    _field,
    _total,
    halo_direct,
    halo_detour,
    halo_relayed,
    halo_even,
    probes,
    tables,
    amps,
    field,
    total,
    rim_direct,
    rim_detour,
    rim_even,
    *rest,
):
    *bands, mixed = rest
    half = side // 2
    wide = field.shape[2]
    tile = wide - side
    bf = jnp.bfloat16
    odd_row = meta[GY_ODD]
    bottom = half + tile
    odd_rows = pl.ds(pl.multiple_of(odd_row * bottom, half), half)
    even_rows = pl.ds(pl.multiple_of((1 - odd_row) * bottom, half), half)
    unpack(meta, halo_direct, halo_detour, halo_relayed, field.at[:, odd_rows, :])
    field[:, even_rows, :] = halo_even[...]
    chunk = 32
    zero = jnp.float32(0)

    for w in range(windows):
        a, b = meta[OFFS + 2 * w], meta[OFFS + 2 * w + 1]
        live = w < meta[LIVE]
        hi_a, hi_b = (a >= side).astype(jnp.int32), (b >= side).astype(jnp.int32)
        row0, col0 = pl.multiple_of(hi_a * side, side), pl.multiple_of(hi_b * side, side)
        row_in, col_in = a - row0, b - col0
        near = lax.broadcasted_iota(jnp.int32, (chunk, side), 1) >= col_in

        def below(start):
            return (lax.broadcasted_iota(jnp.int32, (chunk, side), 0) + start) >= row_in

        def patch(part, start):
            def at(i, j):
                return field[
                    part,
                    pl.ds(pl.multiple_of(row0 + i * side + start, chunk), chunk),
                    pl.ds(pl.multiple_of(col0 + j * side, side), side),
                ]

            return jnp.where(
                below(start),
                jnp.where(near, at(0, 0), at(0, 1)),
                jnp.where(near, at(1, 0), at(1, 1)),
            )

        def exits(start):
            real, imag = patch(0, start), patch(1, start)
            p_real = probes[w, 0, pl.ds(start, chunk), :]
            p_imag = probes[w, 1, pl.ds(start, chunk), :]
            return p_real * real - p_imag * imag, p_real * imag + p_imag * real

        for i in range(0, half, chunk):
            r0, i0 = exits(i)
            r1, i1 = exits(half + i)
            mixed[0, i : i + chunk, :] = (r0 + r1).astype(bf)
            mixed[0, half + i : half + i + chunk, :] = (i0 + i1).astype(bf)
            mixed[1, i : i + chunk, :] = (r0 - r1).astype(bf)
            mixed[1, half + i : half + i + chunk, :] = (i0 - i1).astype(bf)

        plus, minus = [], []
        for odd in (0, 1):
            h = dot(tables[w, 2 * odd], mixed[odd])
            re0, re1 = h[:half, :half], h[:half, half:]
            im0, im1 = h[half:, :half], h[half:, half:]
            plus.append(jnp.concatenate([re0 + re1, im0 + im1], axis=1).astype(bf))
            minus.append(jnp.concatenate([re0 - re1, im0 - im1], axis=1).astype(bf))

        backs = []
        for odd, sides in ((0, plus), (1, minus)):
            far = dot(jnp.concatenate(sides, axis=0), tables[w, 4 + 2 * odd + 1])
            re, im = far[:, :half], far[:, half:]
            power = jnp.maximum(re * re + im * im, amplitude_floor * amplitude_floor)
            factor = 1.0 - amps[w, :, odd * half : (odd + 1) * half] * lax.rsqrt(power)
            chi = jnp.concatenate([re * factor, im * factor], axis=1).astype(bf)
            backs.append(dot(chi, tables[w, 4 + 2 * odd]))
        left, right = backs[0] + backs[1], backs[0] - backs[1]

        outs = []
        for odd in (0, 1):
            at = slice(odd * half, (odd + 1) * half)
            real = jnp.concatenate([left[at, :half], right[at, :half]], axis=1)
            imag = jnp.concatenate([left[at, half:], right[at, half:]], axis=1)
            stacked = jnp.concatenate([real, imag], axis=0).astype(bf)
            outs.append(dot(tables[w, 2 * odd + 1], stacked))
        upper, lower = outs[0] + outs[1], outs[0] - outs[1]

        for start in range(0, side, chunk):
            back = upper if start < half else lower
            at = start % half
            b_real, b_imag = back[at : at + chunk], back[half + at : half + at + chunk]
            p_real = probes[w, 0, pl.ds(start, chunk), :]
            p_imag = probes[w, 1, pl.ds(start, chunk), :]
            terms = (p_real * b_real + p_imag * b_imag, p_real * b_imag - p_imag * b_real)
            rows_in = below(start)
            for part in (0, 1):
                for i, j in ((0, 0), (0, 1), (1, 0), (1, 1)):
                    keep = (rows_in if i == 0 else ~rows_in) & (near if j == 0 else ~near)
                    place = (
                        part,
                        pl.ds(pl.multiple_of(row0 + i * side + start, chunk), chunk),
                        pl.ds(pl.multiple_of(col0 + j * side, side), side),
                    )
                    total[place] = total[place] + jnp.where(keep & live, terms[part], zero)

    pack(total[0, odd_rows, :], total[1, odd_rows, :], rim_direct, rim_detour)
    rim_even[...] = total[:, even_rows, :]
    first = side
    for band_odd, band_even in zip(bands[::2], bands[1::2]):
        rows = slice(first, first + band_odd.shape[1])
        band_odd[...] = total[:, rows, odd_side(meta, band_odd, wide)]
        band_even[...] = total[:, rows, even_side(meta, band_even, wide)]
        first += band_odd.shape[1]


def odd_side(meta, band, wide):
    return pl.ds(pl.multiple_of(meta[GX_ODD] * (wide - band.shape[2]), 128), band.shape[2])


def even_side(meta, band, wide):
    return pl.ds(pl.multiple_of((1 - meta[GX_ODD]) * (wide - band.shape[2]), 128), band.shape[2])


def rim_rows(meta, half):
    odd_row = meta[GY_ODD]
    return (
        pl.ds(pl.multiple_of(odd_row * half, half), half),
        pl.ds(pl.multiple_of((1 - odd_row) * half, half), half),
    )


def sides_kernel(meta, own, rim_odd, rim_even, mid_odd, mid_even):
    tile, half = own.shape[1], rim_odd.shape[2]
    far = tile - half
    for rim, mid, cols in (
        (rim_odd, mid_odd, odd_side(meta, rim_odd, tile)),
        (rim_even, mid_even, even_side(meta, rim_even, tile)),
    ):
        rim[:, :half, :] = own[:, :half, cols]
        rim[:, half:, :] = own[:, far:, cols]
        mid[...] = own[:, half:far, cols]


def edges_kernel(meta, own, side_odd, side_even, _, direct, detour, even, lines):
    tile, half = own.shape[1], side_odd.shape[2]
    wide = lines.shape[2]
    for at, rows in ((0, slice(0, half)), (half, slice(tile - half, tile))):
        lines[:, at : at + half, half : half + tile] = own[:, rows, :]
    lines[:, :, odd_side(meta, side_odd, wide)] = side_odd[...]
    lines[:, :, even_side(meta, side_even, wide)] = side_even[...]
    odd_rows, even_rows = rim_rows(meta, half)
    pack(lines[0, odd_rows, :], lines[1, odd_rows, :], direct, detour)
    even[...] = lines[:, even_rows, :]


def inner_rows(half, tile):
    return (
        (slice(half, 2 * half), slice(0, half)),
        (slice(tile, half + tile), slice(half, 2 * half)),
        slice(2 * half, tile),
    )


def centre_kernel(meta, own, lines, side_odd, side_even, field, total):
    tile, half = own.shape[1], side_odd.shape[2]
    wide = lines.shape[2]
    first, last, mid = inner_rows(half, tile)
    for rows, outer in (first, last):
        field[:, rows, :] = lines[:, outer, :]
    field[:, mid, half : half + tile] = own[:, half : tile - half, :]
    field[:, mid, odd_side(meta, side_odd, wide)] = side_odd[...]
    field[:, mid, even_side(meta, side_even, wide)] = side_even[...]
    total[...] = jnp.zeros_like(total)


def bands_kernel(meta, total, direct, detour, relayed, even, band_odd, band_even, line):
    wide, half = total.shape[2], even.shape[1]
    unpack(meta, direct, detour, relayed, line)
    odd_rows, even_rows = rim_rows(meta, half)
    first, last, _ = inner_rows(half, wide - 2 * half)
    for band, cols in (
        (band_odd, odd_side(meta, band_odd, wide)),
        (band_even, even_side(meta, band_even, wide)),
    ):
        for rows, outer in (first, last):
            band[:, outer, :] = total[:, rows, cols]
        band[:, odd_rows, :] = band[:, odd_rows, :] + line[:, :, cols]
        band[:, even_rows, :] = band[:, even_rows, :] + even[:, :, cols]


def clear_outside(meta, cells, half):
    wide = cells.shape[2]

    @pl.when(meta[EDGE] == 1)
    def _():
        outside = pl.ds(pl.multiple_of(meta[GX_ODD] * (wide - half), half), half)
        cells[:, :, outside] = jnp.zeros((*cells.shape[:2], half), jnp.float32)


def update_edges_kernel(
    meta, field, total, line, even, band_odd, band_even, direct, detour, out_even, lines
):
    wide, half = total.shape[2], even.shape[1]
    odd_rows, even_rows = rim_rows(meta, half)
    first, last, _ = inner_rows(half, wide - 2 * half)
    for rows, outer in (first, last):
        lines[:, outer, :] = field[:, rows, :] - step_size * total[:, rows, :]
    lines[:, odd_rows, :] = lines[:, odd_rows, :] - step_size * line[...]
    lines[:, even_rows, :] = lines[:, even_rows, :] - step_size * even[...]
    for band, cols in (
        (band_odd, odd_side(meta, band_odd, wide)),
        (band_even, even_side(meta, band_even, wide)),
    ):
        lines[:, :, cols] = lines[:, :, cols] - step_size * band[...]
    clear_outside(meta, lines, half)
    pack(lines[0, odd_rows, :], lines[1, odd_rows, :], direct, detour)
    out_even[...] = lines[:, even_rows, :]


def update_centre_kernel(
    meta, field, total, lines, upper_odd, upper_even, lower_odd, lower_even, fresh, zeros
):
    wide, half = total.shape[2], lines.shape[1] // 2
    first, last, mid = inner_rows(half, wide - 2 * half)
    fresh[:, mid, :] = field[:, mid, :] - step_size * total[:, mid, :]
    start = mid.start
    for odd, even in ((upper_odd, upper_even), (lower_odd, lower_even)):
        rows = slice(start, start + odd.shape[1])
        for band, cols in ((odd, odd_side(meta, odd, wide)), (even, even_side(meta, even, wide))):
            fresh[:, rows, cols] = fresh[:, rows, cols] - step_size * band[...]
        start += odd.shape[1]
    clear_outside(meta, fresh.at[:, mid, :], half)
    for rows, outer in (first, last):
        fresh[:, rows, :] = lines[:, outer, :]
    zeros[...] = jnp.zeros_like(zeros)


def almost_final_kernel(meta, field, total, line, even, mid_odd, mid_even, out, part_odd, part_even):
    tile, half = out.shape[1], even.shape[1]
    own = slice(half, half + tile)
    odd_row = meta[GY_ODD]
    far = tile - half
    out[...] = field[:, own, own] - step_size * total[:, own, own]
    for at, rim in ((odd_row * far, line), ((1 - odd_row) * far, even)):
        rows = pl.ds(pl.multiple_of(at, half), half)
        out[:, rows, :] = out[:, rows, :] - step_size * rim[:, :, own]
    for mid, part, cols in (
        (mid_odd, part_odd, odd_side(meta, mid_odd, tile)),
        (mid_even, part_even, even_side(meta, mid_even, tile)),
    ):
        out[:, half:far, cols] = out[:, half:far, cols] - step_size * mid[...]
        part[:, :half, :] = out[:, :half, cols]
        part[:, half:, :] = out[:, far:, cols]


def final_kernel(meta, _, part_odd, part_even, rim_odd, rim_even, out, ready, sems):
    tile, half = out.shape[1], part_odd.shape[2]
    copies = []
    for i, (part, rim, cols) in enumerate(
        (
            (part_odd, rim_odd, odd_side(meta, part_odd, tile)),
            (part_even, rim_even, even_side(meta, part_even, tile)),
        )
    ):
        ready[i] = part[...] - step_size * rim[...]
        for j, first in enumerate((0, tile - half)):
            copies.append(
                pltpu.make_async_copy(
                    ready.at[i, :, pl.ds(j * half, half), :],
                    out.at[:, pl.ds(first, half), cols],
                    sems.at[len(copies)],
                )
            )
            copies[-1].start()
    for copy in copies:
        copy.wait()


def call(kernel, meta, arrays, outs, scratch=(), flops=0, room=0, after=None, aliases=None, far=False):
    f32 = jnp.float32
    shapes = [
        jax.ShapeDtypeStruct(*o) if isinstance(o[0], tuple) else jax.ShapeDtypeStruct(o, f32)
        for o in outs
    ]
    shapes_in = [jax.ShapeDtypeStruct(x.shape, x.dtype) for x in arrays]
    moved = sum(math.prod(x.shape) * x.dtype.itemsize for x in [*shapes_in, *shapes])
    late = [] if after is None else [after]
    smem = pl.BlockSpec(memory_space=pltpu.SMEM)
    vmem = pl.BlockSpec(memory_space=pltpu.VMEM)
    anywhere = pl.BlockSpec(memory_space=pl.ANY)
    return pl.pallas_call(
        kernel,
        out_shape=shapes,
        in_specs=[smem, anywhere if far else vmem, *[vmem] * (len(arrays) - 1), *[anywhere] * len(late)],
        out_specs=[anywhere if far else vmem] * len(shapes),
        scratch_shapes=list(scratch),
        input_output_aliases=aliases or {},
        compiler_params=pltpu.CompilerParams(vmem_limit_bytes=room or min(moved + MIB, 6 * MIB)),
        cost_estimate=pl.CostEstimate(flops=flops, bytes_accessed=moved, transcendentals=0),
    )(meta, *arrays, *late)


def local(object_field, probe_field, measured, offsets, counts):
    tile = object_field.shape[1]
    side = probe_field.shape[1]
    half = side // 2
    windows = offsets.shape[2]
    wide = tile + side
    bf = jnp.bfloat16
    place_col, columns_of_tiles = lax.axis_index("gx"), lax.axis_size("gx")
    odd_col = place_col % 2
    edge = (place_col == 0) | (place_col == columns_of_tiles - 1)
    place_row, rows_of_tiles = lax.axis_index("gy"), lax.axis_size("gy")
    odd_row = place_row % 2
    relay = (place_row == 0) | (place_row == rows_of_tiles - 1)
    places = jnp.stack([odd_col, odd_row, edge.astype(jnp.int32), relay.astype(jnp.int32)])
    meta = jnp.concatenate([places, counts[0], offsets[0, 0].reshape(-1)]).astype(jnp.int32)

    column, band = (2, 2 * half, half), (2, 2 * half, side)
    mid_column, mid_band = (2, tile - 2 * half, half), (2, tile // 2 - half, side)
    whole, lines = (2, wide, wide), (2, 2 * half, wide)
    line = (2, half, wide)
    sends = ((half, wide + CUT), (half, wide - CUT), line)

    *rims, mid_odd, mid_even = call(
        sides_kernel,
        places,
        (object_field,),
        (column, column, mid_column, mid_column),
    )
    rims = swap_columns(*rims)
    mids = swap_columns(mid_odd, mid_even)
    probes, tables, amps = call(
        functools.partial(prepare_kernel, side, windows),
        meta,
        (probe_field, measured[0, 0]),
        ((windows, 2, side, side), ((windows, 8, side, side), bf), (windows, side, side)),
        flops=10**9,
        room=12 * MIB,
    )
    *edges, rows = call(edges_kernel, meta, (object_field, *rims), (*sends, lines), after=amps)
    halos = swap_rows(*edges)
    field, total = call(centre_kernel, meta, (object_field, rows, *mids), (whole, whole))
    for iteration in range(ITERS):
        last = iteration + 1 == ITERS
        field, total, *rest = call(
            functools.partial(gradient_kernel, side, windows),
            meta,
            (field, total, *halos, probes, tables, amps),
            (whole, whole, *sends, *((mid_column,) * 2 if last else (mid_band,) * 4)),
            scratch=(pltpu.VMEM((2, side, side), bf),),
            aliases={1: 0, 2: 1},
            flops=windows * 16 * side**3,
            room=8 * MIB,
        )
        rims = swap_rows(*rest[:3])
        shape = column if last else band
        *bands, odd_line = call(bands_kernel, meta, (total, *rims), (shape, shape, line))
        bands = swap_columns(*bands)
        mids = swap_columns(*rest[3:5])
        if last:
            break
        mids += swap_columns(*rest[5:])
        *edges, rows = call(
            update_edges_kernel,
            meta,
            (field, total, odd_line, rims[3], *bands),
            (*sends, lines),
        )
        halos = swap_rows(*edges)
        field, total = call(
            update_centre_kernel, meta, (field, total, rows, *mids), (whole, whole)
        )
    updated, *parts = call(
        almost_final_kernel,
        meta,
        (field, total, odd_line, rims[3], *mids),
        (object_field.shape, column, column),
    )
    (updated,) = call(
        final_kernel,
        meta,
        (updated, *parts, *bands),
        (object_field.shape,),
        scratch=(pltpu.VMEM((2, *column), jnp.float32), pltpu.SemaphoreType.DMA((4,))),
        aliases={1: 0},
        far=True,
    )
    return updated


def solution(mesh):
    return jax.shard_map(
        local,
        mesh=mesh,
        in_specs=(
            P(None, "gy", "gx"),
            P(),
            P("gy", "gx", None, None, None),
            P("gy", "gx", None, None),
            P("gy", "gx"),
        ),
        out_specs=P(None, "gy", "gx"),
        check_vma=False,
    )
```

```python
import functools
import math

import jax
import jax.numpy as jnp
from jax import lax
from jax.experimental import pallas as pl
from jax.experimental.pallas import tpu as pltpu
from jax.sharding import PartitionSpec as P


ITERS = 2
step_size = 0.25
amplitude_floor = 0.5

MIB = 1 << 20

GX_ODD, GY_ODD, EDGE, RELAY, LIVE, OFFS = 0, 1, 2, 3, 4, 5


def pairs(count, first):
    ups = [(i, i + 1) for i in range(first, count - 1, 2)]
    return ups + [(b, a) for a, b in ups]


def swap_odd(direct, detour):
    count = lax.axis_size("gy")
    low = count // 2 - 1
    far = [(low, low + 1), (low + 1, low)]
    near = [p for p in pairs(count, 1) if p not in far]
    first = lax.ppermute(detour, "gy", near + [(low, 0), (low + 1, count - 1)])
    straight = lax.ppermute(direct, "gy", near + far)
    second = lax.ppermute(first, "gy", [(0, low + 1), (count - 1, low)])
    return straight, first, second


def swap_even(cells):
    return lax.ppermute(cells, "gy", pairs(lax.axis_size("gy"), 0))


def swap_columns(odd_cells, even_cells):
    count = lax.axis_size("gx")
    from_odd = lax.ppermute(odd_cells, "gx", pairs(count, 1))
    from_even = lax.ppermute(even_cells, "gx", pairs(count, 0))
    return from_odd, from_even


CUT = 128


def pack(real, imag, direct, detour):
    wide = real.shape[1]
    direct[:, :wide] = real
    direct[:, wide:] = imag[:, :CUT]
    detour[...] = imag[:, CUT:]


def unpack(meta, direct, detour, relayed, line):
    wide = line.shape[2]
    own = meta[RELAY] == 0
    line[0] = direct[:, :wide]
    line[1, :, :CUT] = direct[:, wide:]
    line[1, :, CUT:] = jnp.where(own, detour[...], jnp.zeros_like(detour)) + relayed[...]


def dot(a, b):
    return jnp.dot(a, b, preferred_element_type=jnp.float32)


def waves(turn, side):
    quarter = side // 4
    moved = turn + quarter // 2
    rest = (moved & (quarter - 1)) - quarter // 2
    which = (moved >> (quarter.bit_length() - 1)) & 3
    x = rest.astype(jnp.float32) * (2.0 * math.pi / side)
    y = x * x
    c = 1.0 + y * (-1 / 2 + y * (1 / 24 + y * (-1 / 720 + y * (1 / 40320))))
    s = x * (1.0 + y * (-1 / 6 + y * (1 / 120 + y * (-1 / 5040 + y * (1 / 362880)))))
    swapped = (which & 1) == 1
    first, second = jnp.where(swapped, s, c), jnp.where(swapped, c, s)
    cos = jnp.where((which == 1) | (which == 2), -first, first)
    sin = jnp.where(which >= 2, -second, second)
    return cos, sin


def table_blocks(shift, half, side):
    freq = 2 * lax.broadcasted_iota(jnp.int32, (half, half), 0)
    cell = lax.broadcasted_iota(jnp.int32, (half, half), 1) - shift
    norm = 1.0 / math.sqrt(side)
    out = []
    for odd in (0, 1):
        c, s = waves((freq + odd) * cell, side)
        c, s = c * norm, s * norm
        out.append((c, s, c.T, s.T))
    return out


def prepare_kernel(side, windows, meta, probe, measured, probes, tables, amps):
    half = side // 2
    bf = jnp.bfloat16
    rows = lax.broadcasted_iota(jnp.int32, (side, side), 0)
    cols = lax.broadcasted_iota(jnp.int32, (side, side), 1)
    place = jnp.where(cols < half, 2 * cols, 2 * (cols - half) + 1)
    picks = (rows == place).astype(jnp.float32).astype(bf)
    place_t = jnp.where(rows < half, 2 * rows, 2 * (rows - half) + 1)
    picks_t = (cols == place_t).astype(jnp.float32).astype(bf)

    def parts(x):
        high = x.astype(bf)
        rest = x - high.astype(jnp.float32)
        mid = rest.astype(bf)
        low = (rest - mid.astype(jnp.float32)).astype(bf)
        return high, mid, low

    def body(w, _):
        row = meta[OFFS + 2 * w] & (side - 1)
        col = meta[OFFS + 2 * w + 1] & (side - 1)
        for part in (0, 1):
            turned = pltpu.roll(probe[part], row, 0)
            probes[w, part] = pltpu.roll(turned, col, 1)
        for axis, shift in ((0, row), (1, col)):
            for odd, (c, s, ct, st) in enumerate(table_blocks(shift, half, side)):
                at = 4 * axis + 2 * odd
                tables[w, at, :half, :half] = c.astype(bf)
                tables[w, at, :half, half:] = s.astype(bf)
                tables[w, at, half:, :half] = (-s).astype(bf)
                tables[w, at, half:, half:] = c.astype(bf)
                tables[w, at + 1, :half, :half] = ct.astype(bf)
                tables[w, at + 1, :half, half:] = (-st).astype(bf)
                tables[w, at + 1, half:, :half] = st.astype(bf)
                tables[w, at + 1, half:, half:] = ct.astype(bf)
        a = [dot(x, picks) for x in parts(measured[w])]
        b = [dot(picks_t, x) for x in parts(a[0] + (a[1] + a[2]))]
        amps[w] = b[0] + (b[1] + b[2])
        return 0

    lax.fori_loop(0, windows, body, 0)


def gradient_kernel(
    side,
    windows,
    meta,
    _field,
    _total,
    halo_direct,
    halo_detour,
    halo_relayed,
    halo_even,
    probes,
    tables,
    amps,
    field,
    total,
    rim_direct,
    rim_detour,
    rim_even,
    *rest,
):
    *bands, mixed = rest
    half = side // 2
    wide = field.shape[2]
    tile = wide - side
    bf = jnp.bfloat16
    odd_row = meta[GY_ODD]
    bottom = half + tile
    odd_rows = pl.ds(pl.multiple_of(odd_row * bottom, half), half)
    even_rows = pl.ds(pl.multiple_of((1 - odd_row) * bottom, half), half)
    unpack(meta, halo_direct, halo_detour, halo_relayed, field.at[:, odd_rows, :])
    field[:, even_rows, :] = halo_even[...]
    chunk = 32
    zero = jnp.float32(0)

    for w in range(windows):
        a, b = meta[OFFS + 2 * w], meta[OFFS + 2 * w + 1]
        live = w < meta[LIVE]
        hi_a, hi_b = (a >= side).astype(jnp.int32), (b >= side).astype(jnp.int32)
        row0, col0 = pl.multiple_of(hi_a * side, side), pl.multiple_of(hi_b * side, side)
        row_in, col_in = a - row0, b - col0
        near = lax.broadcasted_iota(jnp.int32, (chunk, side), 1) >= col_in

        def below(start):
            return (lax.broadcasted_iota(jnp.int32, (chunk, side), 0) + start) >= row_in

        def patch(part, start):
            def at(i, j):
                return field[
                    part,
                    pl.ds(pl.multiple_of(row0 + i * side + start, chunk), chunk),
                    pl.ds(pl.multiple_of(col0 + j * side, side), side),
                ]

            return jnp.where(
                below(start),
                jnp.where(near, at(0, 0), at(0, 1)),
                jnp.where(near, at(1, 0), at(1, 1)),
            )

        def exits(start):
            real, imag = patch(0, start), patch(1, start)
            p_real = probes[w, 0, pl.ds(start, chunk), :]
            p_imag = probes[w, 1, pl.ds(start, chunk), :]
            return p_real * real - p_imag * imag, p_real * imag + p_imag * real

        for i in range(0, half, chunk):
            r0, i0 = exits(i)
            r1, i1 = exits(half + i)
            mixed[0, i : i + chunk, :] = (r0 + r1).astype(bf)
            mixed[0, half + i : half + i + chunk, :] = (i0 + i1).astype(bf)
            mixed[1, i : i + chunk, :] = (r0 - r1).astype(bf)
            mixed[1, half + i : half + i + chunk, :] = (i0 - i1).astype(bf)

        plus, minus = [], []
        for odd in (0, 1):
            h = dot(tables[w, 2 * odd], mixed[odd])
            re0, re1 = h[:half, :half], h[:half, half:]
            im0, im1 = h[half:, :half], h[half:, half:]
            plus.append(jnp.concatenate([re0 + re1, im0 + im1], axis=1).astype(bf))
            minus.append(jnp.concatenate([re0 - re1, im0 - im1], axis=1).astype(bf))

        backs = []
        for odd, sides in ((0, plus), (1, minus)):
            far = dot(jnp.concatenate(sides, axis=0), tables[w, 4 + 2 * odd + 1])
            re, im = far[:, :half], far[:, half:]
            power = jnp.maximum(re * re + im * im, amplitude_floor * amplitude_floor)
            factor = 1.0 - amps[w, :, odd * half : (odd + 1) * half] * lax.rsqrt(power)
            chi = jnp.concatenate([re * factor, im * factor], axis=1).astype(bf)
            backs.append(dot(chi, tables[w, 4 + 2 * odd]))
        left, right = backs[0] + backs[1], backs[0] - backs[1]

        outs = []
        for odd in (0, 1):
            at = slice(odd * half, (odd + 1) * half)
            real = jnp.concatenate([left[at, :half], right[at, :half]], axis=1)
            imag = jnp.concatenate([left[at, half:], right[at, half:]], axis=1)
            stacked = jnp.concatenate([real, imag], axis=0).astype(bf)
            outs.append(dot(tables[w, 2 * odd + 1], stacked))
        upper, lower = outs[0] + outs[1], outs[0] - outs[1]

        for start in range(0, side, chunk):
            back = upper if start < half else lower
            at = start % half
            b_real, b_imag = back[at : at + chunk], back[half + at : half + at + chunk]
            p_real = probes[w, 0, pl.ds(start, chunk), :]
            p_imag = probes[w, 1, pl.ds(start, chunk), :]
            terms = (p_real * b_real + p_imag * b_imag, p_real * b_imag - p_imag * b_real)
            rows_in = below(start)
            for part in (0, 1):
                for i, j in ((0, 0), (0, 1), (1, 0), (1, 1)):
                    keep = (rows_in if i == 0 else ~rows_in) & (near if j == 0 else ~near)
                    place = (
                        part,
                        pl.ds(pl.multiple_of(row0 + i * side + start, chunk), chunk),
                        pl.ds(pl.multiple_of(col0 + j * side, side), side),
                    )
                    total[place] = total[place] + jnp.where(keep & live, terms[part], zero)

    pack(total[0, odd_rows, :], total[1, odd_rows, :], rim_direct, rim_detour)
    rim_even[...] = total[:, even_rows, :]
    first = side
    for band_odd, band_even in zip(bands[::2], bands[1::2]):
        rows = slice(first, first + band_odd.shape[1])
        band_odd[...] = total[:, rows, odd_side(meta, band_odd, wide)]
        band_even[...] = total[:, rows, even_side(meta, band_even, wide)]
        first += band_odd.shape[1]


def odd_side(meta, band, wide):
    return pl.ds(pl.multiple_of(meta[GX_ODD] * (wide - band.shape[2]), 128), band.shape[2])


def even_side(meta, band, wide):
    return pl.ds(pl.multiple_of((1 - meta[GX_ODD]) * (wide - band.shape[2]), 128), band.shape[2])


def both_sides(meta, odd, even, wide):
    return (odd, odd_side(meta, odd, wide)), (even, even_side(meta, even, wide))


def strip(meta, odd, half, tile, margin):
    low = meta[GY_ODD] if odd else 1 - meta[GY_ODD]
    return pl.ds(pl.multiple_of(margin + low * (tile - half), half), half)


def sides_kernel(meta, own, odd_a, odd_b, even_a, even_b, mid_a, mid_b):
    tile, half = own.shape[1], odd_a.shape[1]
    for rows, pair in (
        (strip(meta, True, half, tile, 0), (odd_a, odd_b)),
        (strip(meta, False, half, tile, 0), (even_a, even_b)),
        (slice(half, tile - half), (mid_a, mid_b)),
    ):
        for out, cols in both_sides(meta, *pair, tile):
            out[...] = own[:, rows, cols]


def edge_kernel(odd, meta, own, side_odd, side_even, _, *outs):
    *sends, line = outs
    tile, half = own.shape[1], side_odd.shape[2]
    wide = line.shape[2]
    line[:, :, half : half + tile] = own[:, strip(meta, odd, half, tile, 0), :]
    for side, cols in both_sides(meta, side_odd, side_even, wide):
        line[:, :, cols] = side[...]
    if odd:
        pack(line[0], line[1], *sends)


def centre_kernel(meta, own, odd_line, even_line, side_odd, side_even, field, total):
    tile, half = own.shape[1], side_odd.shape[2]
    wide = field.shape[2]
    mid = slice(2 * half, tile)
    field[:, strip(meta, True, half, tile, half), :] = odd_line[...]
    field[:, strip(meta, False, half, tile, half), :] = even_line[...]
    field[:, mid, half : half + tile] = own[:, half : tile - half, :]
    for side, cols in both_sides(meta, side_odd, side_even, wide):
        field[:, mid, cols] = side[...]
    total[...] = jnp.zeros_like(total)


def odd_bands_kernel(meta, total, direct, detour, relayed, band_odd, band_even, line):
    wide, half = total.shape[2], line.shape[1]
    unpack(meta, direct, detour, relayed, line)
    rows = strip(meta, True, half, wide - 2 * half, half)
    for band, cols in both_sides(meta, band_odd, band_even, wide):
        band[...] = total[:, rows, cols] + line[:, :, cols]


def even_bands_kernel(meta, total, line, band_odd, band_even):
    wide, half = total.shape[2], line.shape[1]
    rows = strip(meta, False, half, wide - 2 * half, half)
    for band, cols in both_sides(meta, band_odd, band_even, wide):
        band[...] = total[:, rows, cols] + line[:, :, cols]


def clear_outside(meta, cells, half):
    wide = cells.shape[2]

    @pl.when(meta[EDGE] == 1)
    def _():
        outside = pl.ds(pl.multiple_of(meta[GX_ODD] * (wide - half), half), half)
        cells[:, :, outside] = jnp.zeros((*cells.shape[:2], half), jnp.float32)


def update_edge_kernel(odd, meta, field, total, line, band_odd, band_even, *outs):
    *sends, fresh = outs
    wide, half = total.shape[2], line.shape[1]
    rows = strip(meta, odd, half, wide - 2 * half, half)
    fresh[...] = field[:, rows, :] - step_size * (total[:, rows, :] + line[...])
    for band, cols in both_sides(meta, band_odd, band_even, wide):
        fresh[:, :, cols] = fresh[:, :, cols] - step_size * band[...]
    clear_outside(meta, fresh, half)
    if odd:
        pack(fresh[0], fresh[1], *sends)


def update_centre_kernel(
    meta,
    field,
    total,
    odd_line,
    even_line,
    upper_odd,
    upper_even,
    lower_odd,
    lower_even,
    fresh,
    zeros,
):
    wide, half = total.shape[2], odd_line.shape[1]
    tile = wide - 2 * half
    mid = slice(2 * half, tile)
    fresh[:, mid, :] = field[:, mid, :] - step_size * total[:, mid, :]
    start = mid.start
    for pair in ((upper_odd, upper_even), (lower_odd, lower_even)):
        rows = slice(start, start + pair[0].shape[1])
        for band, cols in both_sides(meta, *pair, wide):
            fresh[:, rows, cols] = fresh[:, rows, cols] - step_size * band[...]
        start = rows.stop
    clear_outside(meta, fresh.at[:, mid, :], half)
    fresh[:, strip(meta, True, half, tile, half), :] = odd_line[...]
    fresh[:, strip(meta, False, half, tile, half), :] = even_line[...]
    zeros[...] = jnp.zeros_like(zeros)


def almost_final_kernel(
    meta,
    field,
    total,
    odd_line,
    even_line,
    mid_odd,
    mid_even,
    even_odd,
    even_even,
    out,
    part_odd,
    part_even,
):
    tile, half = out.shape[1], odd_line.shape[1]
    own = slice(half, half + tile)
    out[...] = field[:, own, own] - step_size * total[:, own, own]
    odd_rows = strip(meta, True, half, tile, 0)
    even_rows = strip(meta, False, half, tile, 0)
    for rows, line in ((odd_rows, odd_line), (even_rows, even_line)):
        out[:, rows, :] = out[:, rows, :] - step_size * line[:, :, own]
    mid = slice(half, tile - half)
    for rows, pair in ((mid, (mid_odd, mid_even)), (even_rows, (even_odd, even_even))):
        for band, cols in both_sides(meta, *pair, tile):
            out[:, rows, cols] = out[:, rows, cols] - step_size * band[...]
    for part, cols in both_sides(meta, part_odd, part_even, tile):
        part[...] = out[:, odd_rows, cols]


def final_kernel(meta, _, part_odd, part_even, band_odd, band_even, out, ready, sems):
    tile, half = out.shape[1], part_odd.shape[1]
    rows = strip(meta, True, half, tile, 0)
    copies = []
    for (part, cols), band in zip(
        both_sides(meta, part_odd, part_even, tile), (band_odd, band_even)
    ):
        i = len(copies)
        ready[i] = part[...] - step_size * band[...]
        copies.append(pltpu.make_async_copy(ready.at[i], out.at[:, rows, cols], sems.at[i]))
        copies[-1].start()
    for copy in copies:
        copy.wait()


def call(kernel, meta, arrays, outs, scratch=(), flops=0, room=0, after=None, aliases=None, far=False):
    f32 = jnp.float32
    shapes = [
        jax.ShapeDtypeStruct(*o) if isinstance(o[0], tuple) else jax.ShapeDtypeStruct(o, f32)
        for o in outs
    ]
    shapes_in = [jax.ShapeDtypeStruct(x.shape, x.dtype) for x in arrays]
    moved = sum(math.prod(x.shape) * x.dtype.itemsize for x in [*shapes_in, *shapes])
    late = [] if after is None else [after]
    smem = pl.BlockSpec(memory_space=pltpu.SMEM)
    vmem = pl.BlockSpec(memory_space=pltpu.VMEM)
    anywhere = pl.BlockSpec(memory_space=pl.ANY)
    return pl.pallas_call(
        kernel,
        out_shape=shapes,
        in_specs=[smem, anywhere if far else vmem, *[vmem] * (len(arrays) - 1), *[anywhere] * len(late)],
        out_specs=[anywhere if far else vmem] * len(shapes),
        scratch_shapes=list(scratch),
        input_output_aliases=aliases or {},
        compiler_params=pltpu.CompilerParams(vmem_limit_bytes=room or min(moved + MIB, 6 * MIB)),
        cost_estimate=pl.CostEstimate(flops=flops, bytes_accessed=moved, transcendentals=0),
    )(meta, *arrays, *late)


def local(object_field, probe_field, measured, offsets, counts):
    tile = object_field.shape[1]
    side = probe_field.shape[1]
    half = side // 2
    windows = offsets.shape[2]
    wide = tile + side
    bf = jnp.bfloat16
    place_col, columns_of_tiles = lax.axis_index("gx"), lax.axis_size("gx")
    odd_col = place_col % 2
    edge = (place_col == 0) | (place_col == columns_of_tiles - 1)
    place_row, rows_of_tiles = lax.axis_index("gy"), lax.axis_size("gy")
    odd_row = place_row % 2
    relay = (place_row == 0) | (place_row == rows_of_tiles - 1)
    places = jnp.stack([odd_col, odd_row, edge.astype(jnp.int32), relay.astype(jnp.int32)])
    meta = jnp.concatenate([places, counts[0], offsets[0, 0].reshape(-1)]).astype(jnp.int32)

    column, band = (2, half, half), (2, half, side)
    mid_column, mid_band = (2, tile - 2 * half, half), (2, tile // 2 - half, side)
    whole, line = (2, wide, wide), (2, half, wide)
    parts = ((half, wide + CUT), (half, wide - CUT))

    def step(kernel, *args, **kwargs):
        return call(kernel, meta, *args, **kwargs)

    sides = call(sides_kernel, places, (object_field,), (column,) * 4 + (mid_column,) * 2)
    odd_sides = swap_columns(*sides[:2])
    even_sides = swap_columns(*sides[2:4])
    mids = swap_columns(*sides[4:])
    probes, tables, amps = step(
        functools.partial(prepare_kernel, side, windows),
        (probe_field, measured[0, 0]),
        ((windows, 2, side, side), ((windows, 8, side, side), bf), (windows, side, side)),
        flops=10**9,
        room=12 * MIB,
    )
    *sends, odd_line = step(
        functools.partial(edge_kernel, True), (object_field, *odd_sides), (*parts, line), after=amps
    )
    odd_halo = swap_odd(*sends)
    (even_line,) = step(functools.partial(edge_kernel, False), (object_field, *even_sides), (line,), after=amps)
    even_halo = swap_even(even_line)
    field, total = step(centre_kernel, (object_field, odd_line, even_line, *mids), (whole, whole))
    for i in range(1, ITERS + 1):
        last = i == ITERS
        field, total, *rest = step(
            functools.partial(gradient_kernel, side, windows),
            (field, total, *odd_halo, even_halo, probes, tables, amps),
            (whole, whole, *parts, line, *((mid_column,) * 2 if last else (mid_band,) * 4)),
            scratch=(pltpu.VMEM((2, side, side), bf),),
            aliases={1: 0, 2: 1},
            flops=windows * 16 * side**3,
            room=8 * MIB,
        )
        odd_rim = swap_odd(*rest[:2])
        even_rim = swap_even(rest[2])
        mids = swap_columns(*rest[3:5])
        shape = column if last else band
        evens = step(even_bands_kernel, (total, even_rim), (shape, shape))
        evens = swap_columns(*evens)
        *odds, odd_rim = step(odd_bands_kernel, (total, *odd_rim), (shape, shape, line))
        odds = swap_columns(*odds)
        if last:
            break
        lower = swap_columns(*rest[5:])
        (even_line,) = step(functools.partial(update_edge_kernel, False), (field, total, even_rim, *evens), (line,))
        even_halo = swap_even(even_line)
        *sends, odd_line = step(
            functools.partial(update_edge_kernel, True), (field, total, odd_rim, *odds), (*parts, line)
        )
        odd_halo = swap_odd(*sends)
        field, total = step(update_centre_kernel, (field, total, odd_line, even_line, *mids, *lower), (whole, whole))
    updated, *ends = step(
        almost_final_kernel, (field, total, odd_rim, even_rim, *mids, *evens), (object_field.shape, column, column)
    )
    (updated,) = step(
        final_kernel,
        (updated, *ends, *odds),
        (object_field.shape,),
        scratch=(pltpu.VMEM((2, *column), jnp.float32), pltpu.SemaphoreType.DMA((2,))),
        aliases={1: 0},
        far=True,
    )
    return updated


def solution(mesh):
    return jax.shard_map(
        local,
        mesh=mesh,
        in_specs=(
            P(None, "gy", "gx"),
            P(),
            P("gy", "gx", None, None, None),
            P("gy", "gx", None, None),
            P("gy", "gx"),
        ),
        out_specs=P(None, "gy", "gx"),
        check_vma=False,
    )
```

```python
import functools
import math

import jax
import jax.numpy as jnp
from jax import lax
from jax.experimental import pallas as pl
from jax.experimental.pallas import tpu as pltpu
from jax.sharding import PartitionSpec as P


ITERS = 2
step_size = 0.25
amplitude_floor = 0.5

MIB = 1 << 20

GX_ODD, GY_ODD, EDGE, RELAY, LIVE, OFFS = 0, 1, 2, 3, 4, 5


def pairs(count, first):
    ups = [(i, i + 1) for i in range(first, count - 1, 2)]
    return ups + [(b, a) for a, b in ups]


def swap_rows(direct, detour, even_cells):
    count = lax.axis_size("gy")
    low = count // 2 - 1
    far = [(low, low + 1), (low + 1, low)]
    near = [p for p in pairs(count, 1) if p not in far]
    first = lax.ppermute(detour, "gy", near + [(low, 0), (low + 1, count - 1)])
    straight = lax.ppermute(direct, "gy", near + far)
    even = lax.ppermute(even_cells, "gy", pairs(count, 0))
    second = lax.ppermute(first, "gy", [(0, low + 1), (count - 1, low)])
    return straight, first, second, even


def swap_columns(odd_cells, even_cells):
    count = lax.axis_size("gx")
    from_odd = lax.ppermute(odd_cells, "gx", pairs(count, 1))
    from_even = lax.ppermute(even_cells, "gx", pairs(count, 0))
    return from_odd, from_even


STRAIGHT = 512


def pack(real, imag, direct, detour):
    rest = real.shape[1] - STRAIGHT
    direct[...] = real[:, :STRAIGHT]
    detour[:, :rest] = real[:, STRAIGHT:]
    detour[:, rest:] = imag


def unpack(meta, direct, detour, relayed, line):
    rest = line.shape[2] - STRAIGHT
    own = meta[RELAY] == 0
    line[0, :, :STRAIGHT] = direct[...]
    cells = jnp.where(own, detour[...], jnp.zeros_like(detour)) + relayed[...]
    line[0, :, STRAIGHT:] = cells[:, :rest]
    line[1] = cells[:, rest:]


def dot(a, b):
    return jnp.dot(a, b, preferred_element_type=jnp.float32)


def waves(turn, side):
    quarter = side // 4
    moved = turn + quarter // 2
    rest = (moved & (quarter - 1)) - quarter // 2
    which = (moved >> (quarter.bit_length() - 1)) & 3
    x = rest.astype(jnp.float32) * (2.0 * math.pi / side)
    y = x * x
    c = 1.0 + y * (-1 / 2 + y * (1 / 24 + y * (-1 / 720 + y * (1 / 40320))))
    s = x * (1.0 + y * (-1 / 6 + y * (1 / 120 + y * (-1 / 5040 + y * (1 / 362880)))))
    swapped = (which & 1) == 1
    first, second = jnp.where(swapped, s, c), jnp.where(swapped, c, s)
    cos = jnp.where((which == 1) | (which == 2), -first, first)
    sin = jnp.where(which >= 2, -second, second)
    return cos, sin


def table_blocks(shift, half, side):
    freq = 2 * lax.broadcasted_iota(jnp.int32, (half, half), 0)
    cell = lax.broadcasted_iota(jnp.int32, (half, half), 1) - shift
    norm = 1.0 / math.sqrt(side)
    out = []
    for odd in (0, 1):
        c, s = waves((freq + odd) * cell, side)
        c, s = c * norm, s * norm
        out.append((c, s, c.T, s.T))
    return out


def prepare_kernel(side, windows, meta, probe, measured, probes, tables, amps):
    half = side // 2
    bf = jnp.bfloat16
    rows = lax.broadcasted_iota(jnp.int32, (side, side), 0)
    cols = lax.broadcasted_iota(jnp.int32, (side, side), 1)
    place = jnp.where(cols < half, 2 * cols, 2 * (cols - half) + 1)
    picks = (rows == place).astype(jnp.float32).astype(bf)
    place_t = jnp.where(rows < half, 2 * rows, 2 * (rows - half) + 1)
    picks_t = (cols == place_t).astype(jnp.float32).astype(bf)

    def parts(x):
        high = x.astype(bf)
        rest = x - high.astype(jnp.float32)
        mid = rest.astype(bf)
        low = (rest - mid.astype(jnp.float32)).astype(bf)
        return high, mid, low

    def body(w, _):
        row = meta[OFFS + 2 * w] & (side - 1)
        col = meta[OFFS + 2 * w + 1] & (side - 1)
        for part in (0, 1):
            turned = pltpu.roll(probe[part], row, 0)
            probes[w, part] = pltpu.roll(turned, col, 1)
        for axis, shift in ((0, row), (1, col)):
            for odd, (c, s, ct, st) in enumerate(table_blocks(shift, half, side)):
                at = 4 * axis + 2 * odd
                tables[w, at, :half, :half] = c.astype(bf)
                tables[w, at, :half, half:] = s.astype(bf)
                tables[w, at, half:, :half] = (-s).astype(bf)
                tables[w, at, half:, half:] = c.astype(bf)
                tables[w, at + 1, :half, :half] = ct.astype(bf)
                tables[w, at + 1, :half, half:] = (-st).astype(bf)
                tables[w, at + 1, half:, :half] = st.astype(bf)
                tables[w, at + 1, half:, half:] = ct.astype(bf)
        a = [dot(x, picks) for x in parts(measured[w])]
        b = [dot(picks_t, x) for x in parts(a[0] + (a[1] + a[2]))]
        amps[w] = b[0] + (b[1] + b[2])
        return 0

    lax.fori_loop(0, windows, body, 0)


def gradient_kernel(
    side,
    windows,
    meta,
    _field,
    _total,
    halo_direct,
    halo_detour,
    halo_relayed,
    halo_even,
    probes,
    tables,
    amps,
    field,
    total,
    rim_direct,
    rim_detour,
    rim_even,
    *rest,
):
    *bands, mixed = rest
    half = side // 2
    wide = field.shape[2]
    tile = wide - side
    bf = jnp.bfloat16
    odd_row = meta[GY_ODD]
    bottom = half + tile
    odd_rows = pl.ds(pl.multiple_of(odd_row * bottom, half), half)
    even_rows = pl.ds(pl.multiple_of((1 - odd_row) * bottom, half), half)
    unpack(meta, halo_direct, halo_detour, halo_relayed, field.at[:, odd_rows, :])
    field[:, even_rows, :] = halo_even[...]
    chunk = 32
    zero = jnp.float32(0)

    for w in range(windows):
        a, b = meta[OFFS + 2 * w], meta[OFFS + 2 * w + 1]
        live = w < meta[LIVE]
        hi_a, hi_b = (a >= side).astype(jnp.int32), (b >= side).astype(jnp.int32)
        row0, col0 = pl.multiple_of(hi_a * side, side), pl.multiple_of(hi_b * side, side)
        row_in, col_in = a - row0, b - col0
        near = lax.broadcasted_iota(jnp.int32, (chunk, side), 1) >= col_in

        def below(start):
            return (lax.broadcasted_iota(jnp.int32, (chunk, side), 0) + start) >= row_in

        def patch(part, start):
            def at(i, j):
                return field[
                    part,
                    pl.ds(pl.multiple_of(row0 + i * side + start, chunk), chunk),
                    pl.ds(pl.multiple_of(col0 + j * side, side), side),
                ]

            return jnp.where(
                below(start),
                jnp.where(near, at(0, 0), at(0, 1)),
                jnp.where(near, at(1, 0), at(1, 1)),
            )

        def exits(start):
            real, imag = patch(0, start), patch(1, start)
            p_real = probes[w, 0, pl.ds(start, chunk), :]
            p_imag = probes[w, 1, pl.ds(start, chunk), :]
            return p_real * real - p_imag * imag, p_real * imag + p_imag * real

        for i in range(0, half, chunk):
            r0, i0 = exits(i)
            r1, i1 = exits(half + i)
            mixed[0, i : i + chunk, :] = (r0 + r1).astype(bf)
            mixed[0, half + i : half + i + chunk, :] = (i0 + i1).astype(bf)
            mixed[1, i : i + chunk, :] = (r0 - r1).astype(bf)
            mixed[1, half + i : half + i + chunk, :] = (i0 - i1).astype(bf)

        plus, minus = [], []
        for odd in (0, 1):
            h = dot(tables[w, 2 * odd], mixed[odd])
            re0, re1 = h[:half, :half], h[:half, half:]
            im0, im1 = h[half:, :half], h[half:, half:]
            plus.append(jnp.concatenate([re0 + re1, im0 + im1], axis=1).astype(bf))
            minus.append(jnp.concatenate([re0 - re1, im0 - im1], axis=1).astype(bf))

        backs = []
        for odd, sides in ((0, plus), (1, minus)):
            far = dot(jnp.concatenate(sides, axis=0), tables[w, 4 + 2 * odd + 1])
            re, im = far[:, :half], far[:, half:]
            power = jnp.maximum(re * re + im * im, amplitude_floor * amplitude_floor)
            factor = 1.0 - amps[w, :, odd * half : (odd + 1) * half] * lax.rsqrt(power)
            chi = jnp.concatenate([re * factor, im * factor], axis=1).astype(bf)
            backs.append(dot(chi, tables[w, 4 + 2 * odd]))
        left, right = backs[0] + backs[1], backs[0] - backs[1]

        outs = []
        for odd in (0, 1):
            at = slice(odd * half, (odd + 1) * half)
            real = jnp.concatenate([left[at, :half], right[at, :half]], axis=1)
            imag = jnp.concatenate([left[at, half:], right[at, half:]], axis=1)
            stacked = jnp.concatenate([real, imag], axis=0).astype(bf)
            outs.append(dot(tables[w, 2 * odd + 1], stacked))
        upper, lower = outs[0] + outs[1], outs[0] - outs[1]

        for start in range(0, side, chunk):
            back = upper if start < half else lower
            at = start % half
            b_real, b_imag = back[at : at + chunk], back[half + at : half + at + chunk]
            p_real = probes[w, 0, pl.ds(start, chunk), :]
            p_imag = probes[w, 1, pl.ds(start, chunk), :]
            terms = (p_real * b_real + p_imag * b_imag, p_real * b_imag - p_imag * b_real)
            rows_in = below(start)
            for part in (0, 1):
                for i, j in ((0, 0), (0, 1), (1, 0), (1, 1)):
                    keep = (rows_in if i == 0 else ~rows_in) & (near if j == 0 else ~near)
                    place = (
                        part,
                        pl.ds(pl.multiple_of(row0 + i * side + start, chunk), chunk),
                        pl.ds(pl.multiple_of(col0 + j * side, side), side),
                    )
                    total[place] = total[place] + jnp.where(keep & live, terms[part], zero)

    pack(total[0, odd_rows, :], total[1, odd_rows, :], rim_direct, rim_detour)
    rim_even[...] = total[:, even_rows, :]
    first = side
    for band_odd, band_even in zip(bands[::2], bands[1::2]):
        rows = slice(first, first + band_odd.shape[1])
        band_odd[...] = total[:, rows, odd_side(meta, band_odd, wide)]
        band_even[...] = total[:, rows, even_side(meta, band_even, wide)]
        first += band_odd.shape[1]


def odd_side(meta, band, wide):
    return pl.ds(pl.multiple_of(meta[GX_ODD] * (wide - band.shape[2]), 128), band.shape[2])


def even_side(meta, band, wide):
    return pl.ds(pl.multiple_of((1 - meta[GX_ODD]) * (wide - band.shape[2]), 128), band.shape[2])


def rim_rows(meta, half):
    odd_row = meta[GY_ODD]
    return (
        pl.ds(pl.multiple_of(odd_row * half, half), half),
        pl.ds(pl.multiple_of((1 - odd_row) * half, half), half),
    )


def sides_kernel(meta, own, rim_odd, rim_even, mid_odd, mid_even):
    tile, half = own.shape[1], rim_odd.shape[2]
    far = tile - half
    for rim, mid, cols in (
        (rim_odd, mid_odd, odd_side(meta, rim_odd, tile)),
        (rim_even, mid_even, even_side(meta, rim_even, tile)),
    ):
        rim[:, :half, :] = own[:, :half, cols]
        rim[:, half:, :] = own[:, far:, cols]
        mid[...] = own[:, half:far, cols]


def edges_kernel(meta, own, side_odd, side_even, _, direct, detour, even, lines):
    tile, half = own.shape[1], side_odd.shape[2]
    wide = lines.shape[2]
    for at, rows in ((0, slice(0, half)), (half, slice(tile - half, tile))):
        lines[:, at : at + half, half : half + tile] = own[:, rows, :]
    lines[:, :, odd_side(meta, side_odd, wide)] = side_odd[...]
    lines[:, :, even_side(meta, side_even, wide)] = side_even[...]
    odd_rows, even_rows = rim_rows(meta, half)
    pack(lines[0, odd_rows, :], lines[1, odd_rows, :], direct, detour)
    even[...] = lines[:, even_rows, :]


def inner_rows(half, tile):
    return (
        (slice(half, 2 * half), slice(0, half)),
        (slice(tile, half + tile), slice(half, 2 * half)),
        slice(2 * half, tile),
    )


def centre_kernel(meta, own, lines, side_odd, side_even, field, total):
    tile, half = own.shape[1], side_odd.shape[2]
    wide = lines.shape[2]
    first, last, mid = inner_rows(half, tile)
    for rows, outer in (first, last):
        field[:, rows, :] = lines[:, outer, :]
    field[:, mid, half : half + tile] = own[:, half : tile - half, :]
    field[:, mid, odd_side(meta, side_odd, wide)] = side_odd[...]
    field[:, mid, even_side(meta, side_even, wide)] = side_even[...]
    total[...] = jnp.zeros_like(total)


def bands_kernel(meta, total, direct, detour, relayed, even, band_odd, band_even, line):
    wide, half = total.shape[2], even.shape[1]
    unpack(meta, direct, detour, relayed, line)
    odd_rows, even_rows = rim_rows(meta, half)
    first, last, _ = inner_rows(half, wide - 2 * half)
    for band, cols in (
        (band_odd, odd_side(meta, band_odd, wide)),
        (band_even, even_side(meta, band_even, wide)),
    ):
        for rows, outer in (first, last):
            band[:, outer, :] = total[:, rows, cols]
        band[:, odd_rows, :] = band[:, odd_rows, :] + line[:, :, cols]
        band[:, even_rows, :] = band[:, even_rows, :] + even[:, :, cols]


def clear_outside(meta, cells, half):
    wide = cells.shape[2]

    @pl.when(meta[EDGE] == 1)
    def _():
        outside = pl.ds(pl.multiple_of(meta[GX_ODD] * (wide - half), half), half)
        cells[:, :, outside] = jnp.zeros((*cells.shape[:2], half), jnp.float32)


def update_edges_kernel(
    meta, field, total, line, even, band_odd, band_even, direct, detour, out_even, lines
):
    wide, half = total.shape[2], even.shape[1]
    odd_rows, even_rows = rim_rows(meta, half)
    first, last, _ = inner_rows(half, wide - 2 * half)
    for rows, outer in (first, last):
        lines[:, outer, :] = field[:, rows, :] - step_size * total[:, rows, :]
    lines[:, odd_rows, :] = lines[:, odd_rows, :] - step_size * line[...]
    lines[:, even_rows, :] = lines[:, even_rows, :] - step_size * even[...]
    for band, cols in (
        (band_odd, odd_side(meta, band_odd, wide)),
        (band_even, even_side(meta, band_even, wide)),
    ):
        lines[:, :, cols] = lines[:, :, cols] - step_size * band[...]
    clear_outside(meta, lines, half)
    pack(lines[0, odd_rows, :], lines[1, odd_rows, :], direct, detour)
    out_even[...] = lines[:, even_rows, :]


def update_centre_kernel(
    meta, field, total, lines, upper_odd, upper_even, lower_odd, lower_even, fresh, zeros
):
    wide, half = total.shape[2], lines.shape[1] // 2
    first, last, mid = inner_rows(half, wide - 2 * half)
    fresh[:, mid, :] = field[:, mid, :] - step_size * total[:, mid, :]
    start = mid.start
    for odd, even in ((upper_odd, upper_even), (lower_odd, lower_even)):
        rows = slice(start, start + odd.shape[1])
        for band, cols in ((odd, odd_side(meta, odd, wide)), (even, even_side(meta, even, wide))):
            fresh[:, rows, cols] = fresh[:, rows, cols] - step_size * band[...]
        start += odd.shape[1]
    clear_outside(meta, fresh.at[:, mid, :], half)
    for rows, outer in (first, last):
        fresh[:, rows, :] = lines[:, outer, :]
    zeros[...] = jnp.zeros_like(zeros)


def almost_final_kernel(meta, field, total, line, even, mid_odd, mid_even, out, part_odd, part_even):
    tile, half = out.shape[1], even.shape[1]
    own = slice(half, half + tile)
    odd_row = meta[GY_ODD]
    far = tile - half
    out[...] = field[:, own, own] - step_size * total[:, own, own]
    for at, rim in ((odd_row * far, line), ((1 - odd_row) * far, even)):
        rows = pl.ds(pl.multiple_of(at, half), half)
        out[:, rows, :] = out[:, rows, :] - step_size * rim[:, :, own]
    for mid, part, cols in (
        (mid_odd, part_odd, odd_side(meta, mid_odd, tile)),
        (mid_even, part_even, even_side(meta, mid_even, tile)),
    ):
        out[:, half:far, cols] = out[:, half:far, cols] - step_size * mid[...]
        part[:, :half, :] = out[:, :half, cols]
        part[:, half:, :] = out[:, far:, cols]


def final_kernel(meta, _, part_odd, part_even, rim_odd, rim_even, out, ready, sems):
    tile, half = out.shape[1], part_odd.shape[2]
    copies = []
    for i, (part, rim, cols) in enumerate(
        (
            (part_odd, rim_odd, odd_side(meta, part_odd, tile)),
            (part_even, rim_even, even_side(meta, part_even, tile)),
        )
    ):
        ready[i] = part[...] - step_size * rim[...]
        for j, first in enumerate((0, tile - half)):
            copies.append(
                pltpu.make_async_copy(
                    ready.at[i, :, pl.ds(j * half, half), :],
                    out.at[:, pl.ds(first, half), cols],
                    sems.at[len(copies)],
                )
            )
            copies[-1].start()
    for copy in copies:
        copy.wait()


def call(kernel, meta, arrays, outs, scratch=(), flops=0, room=0, after=None, aliases=None, far=False):
    f32 = jnp.float32
    shapes = [
        jax.ShapeDtypeStruct(*o) if isinstance(o[0], tuple) else jax.ShapeDtypeStruct(o, f32)
        for o in outs
    ]
    shapes_in = [jax.ShapeDtypeStruct(x.shape, x.dtype) for x in arrays]
    moved = sum(math.prod(x.shape) * x.dtype.itemsize for x in [*shapes_in, *shapes])
    late = [] if after is None else [after]
    smem = pl.BlockSpec(memory_space=pltpu.SMEM)
    vmem = pl.BlockSpec(memory_space=pltpu.VMEM)
    anywhere = pl.BlockSpec(memory_space=pl.ANY)
    return pl.pallas_call(
        kernel,
        out_shape=shapes,
        in_specs=[smem, anywhere if far else vmem, *[vmem] * (len(arrays) - 1), *[anywhere] * len(late)],
        out_specs=[anywhere if far else vmem] * len(shapes),
        scratch_shapes=list(scratch),
        input_output_aliases=aliases or {},
        compiler_params=pltpu.CompilerParams(vmem_limit_bytes=room or min(moved + MIB, 6 * MIB)),
        cost_estimate=pl.CostEstimate(flops=flops, bytes_accessed=moved, transcendentals=0),
    )(meta, *arrays, *late)


def local(object_field, probe_field, measured, offsets, counts):
    tile = object_field.shape[1]
    side = probe_field.shape[1]
    half = side // 2
    windows = offsets.shape[2]
    wide = tile + side
    bf = jnp.bfloat16
    place_col, columns_of_tiles = lax.axis_index("gx"), lax.axis_size("gx")
    odd_col = place_col % 2
    edge = (place_col == 0) | (place_col == columns_of_tiles - 1)
    place_row, rows_of_tiles = lax.axis_index("gy"), lax.axis_size("gy")
    odd_row = place_row % 2
    relay = (place_row == 0) | (place_row == rows_of_tiles - 1)
    places = jnp.stack([odd_col, odd_row, edge.astype(jnp.int32), relay.astype(jnp.int32)])
    meta = jnp.concatenate([places, counts[0], offsets[0, 0].reshape(-1)]).astype(jnp.int32)

    column, band = (2, 2 * half, half), (2, 2 * half, side)
    mid_column, mid_band = (2, tile - 2 * half, half), (2, tile // 2 - half, side)
    whole, lines = (2, wide, wide), (2, 2 * half, wide)
    line = (2, half, wide)
    sends = ((half, STRAIGHT), (half, 2 * wide - STRAIGHT), line)

    *rims, mid_odd, mid_even = call(
        sides_kernel,
        places,
        (object_field,),
        (column, column, mid_column, mid_column),
    )
    rims = swap_columns(*rims)
    mids = swap_columns(mid_odd, mid_even)
    probes, tables, amps = call(
        functools.partial(prepare_kernel, side, windows),
        meta,
        (probe_field, measured[0, 0]),
        ((windows, 2, side, side), ((windows, 8, side, side), bf), (windows, side, side)),
        flops=10**9,
        room=12 * MIB,
    )
    *edges, rows = call(edges_kernel, meta, (object_field, *rims), (*sends, lines), after=amps)
    halos = swap_rows(*edges)
    field, total = call(centre_kernel, meta, (object_field, rows, *mids), (whole, whole))
    for iteration in range(ITERS):
        last = iteration + 1 == ITERS
        field, total, *rest = call(
            functools.partial(gradient_kernel, side, windows),
            meta,
            (field, total, *halos, probes, tables, amps),
            (whole, whole, *sends, *((mid_column,) * 2 if last else (mid_band,) * 4)),
            scratch=(pltpu.VMEM((2, side, side), bf),),
            aliases={1: 0, 2: 1},
            flops=windows * 16 * side**3,
            room=8 * MIB,
        )
        rims = swap_rows(*rest[:3])
        shape = column if last else band
        *bands, odd_line = call(bands_kernel, meta, (total, *rims), (shape, shape, line))
        bands = swap_columns(*bands)
        mids = swap_columns(*rest[3:5])
        if last:
            break
        mids += swap_columns(*rest[5:])
        *edges, rows = call(
            update_edges_kernel,
            meta,
            (field, total, odd_line, rims[3], *bands),
            (*sends, lines),
        )
        halos = swap_rows(*edges)
        field, total = call(
            update_centre_kernel, meta, (field, total, rows, *mids), (whole, whole)
        )
    updated, *parts = call(
        almost_final_kernel,
        meta,
        (field, total, odd_line, rims[3], *mids),
        (object_field.shape, column, column),
    )
    (updated,) = call(
        final_kernel,
        meta,
        (updated, *parts, *bands),
        (object_field.shape,),
        scratch=(pltpu.VMEM((2, *column), jnp.float32), pltpu.SemaphoreType.DMA((4,))),
        aliases={1: 0},
        far=True,
    )
    return updated


def solution(mesh):
    return jax.shard_map(
        local,
        mesh=mesh,
        in_specs=(
            P(None, "gy", "gx"),
            P(),
            P("gy", "gx", None, None, None),
            P("gy", "gx", None, None),
            P("gy", "gx"),
        ),
        out_specs=P(None, "gy", "gx"),
        check_vma=False,
    )
```

```python
import functools
import math

import jax
import jax.numpy as jnp
from jax import lax
from jax.experimental import pallas as pl
from jax.experimental.pallas import tpu as pltpu
from jax.sharding import PartitionSpec as P


ITERS = 2
step_size = 0.25
amplitude_floor = 0.5

MIB = 1 << 20

GX_ODD, GY_ODD, EDGE, RELAY, LIVE, OFFS = 0, 1, 2, 3, 4, 5


def pairs(count, first):
    ups = [(i, i + 1) for i in range(first, count - 1, 2)]
    return ups + [(b, a) for a, b in ups]


def swap_odd(direct, detour):
    count = lax.axis_size("gy")
    low = count // 2 - 1
    far = [(low, low + 1), (low + 1, low)]
    near = [p for p in pairs(count, 1) if p not in far]
    first = lax.ppermute(detour, "gy", near + [(low, 0), (low + 1, count - 1)])
    straight = lax.ppermute(direct, "gy", near + far)
    second = lax.ppermute(first, "gy", [(0, low + 1), (count - 1, low)])
    return straight, first, second


def swap_even(cells):
    return lax.ppermute(cells, "gy", pairs(lax.axis_size("gy"), 0))


def swap_rows(direct, detour, even_cells):
    return *swap_odd(direct, detour), swap_even(even_cells)


def swap_columns(odd_cells, even_cells):
    count = lax.axis_size("gx")
    from_odd = lax.ppermute(odd_cells, "gx", pairs(count, 1))
    from_even = lax.ppermute(even_cells, "gx", pairs(count, 0))
    return from_odd, from_even


CUT = 128


def pack(real, imag, direct, detour):
    wide = real.shape[1]
    direct[:, :wide] = real
    direct[:, wide:] = imag[:, :CUT]
    detour[...] = imag[:, CUT:]


def unpack(meta, direct, detour, relayed, line):
    wide = line.shape[2]
    own = meta[RELAY] == 0
    line[0] = direct[:, :wide]
    line[1, :, :CUT] = direct[:, wide:]
    line[1, :, CUT:] = jnp.where(own, detour[...], jnp.zeros_like(detour)) + relayed[...]


def dot(a, b):
    return jnp.dot(a, b, preferred_element_type=jnp.float32)


def waves(turn, side):
    quarter = side // 4
    moved = turn + quarter // 2
    rest = (moved & (quarter - 1)) - quarter // 2
    which = (moved >> (quarter.bit_length() - 1)) & 3
    x = rest.astype(jnp.float32) * (2.0 * math.pi / side)
    y = x * x
    c = 1.0 + y * (-1 / 2 + y * (1 / 24 + y * (-1 / 720 + y * (1 / 40320))))
    s = x * (1.0 + y * (-1 / 6 + y * (1 / 120 + y * (-1 / 5040 + y * (1 / 362880)))))
    swapped = (which & 1) == 1
    first, second = jnp.where(swapped, s, c), jnp.where(swapped, c, s)
    cos = jnp.where((which == 1) | (which == 2), -first, first)
    sin = jnp.where(which >= 2, -second, second)
    return cos, sin


def table_blocks(shift, half, side):
    freq = 2 * lax.broadcasted_iota(jnp.int32, (half, half), 0)
    cell = lax.broadcasted_iota(jnp.int32, (half, half), 1) - shift
    norm = 1.0 / math.sqrt(side)
    out = []
    for odd in (0, 1):
        c, s = waves((freq + odd) * cell, side)
        c, s = c * norm, s * norm
        out.append((c, s, c.T, s.T))
    return out


def prepare_kernel(side, windows, meta, probe, measured, probes, tables, amps):
    half = side // 2
    bf = jnp.bfloat16
    rows = lax.broadcasted_iota(jnp.int32, (side, side), 0)
    cols = lax.broadcasted_iota(jnp.int32, (side, side), 1)
    place = jnp.where(cols < half, 2 * cols, 2 * (cols - half) + 1)
    picks = (rows == place).astype(jnp.float32).astype(bf)
    place_t = jnp.where(rows < half, 2 * rows, 2 * (rows - half) + 1)
    picks_t = (cols == place_t).astype(jnp.float32).astype(bf)

    def parts(x):
        high = x.astype(bf)
        rest = x - high.astype(jnp.float32)
        mid = rest.astype(bf)
        low = (rest - mid.astype(jnp.float32)).astype(bf)
        return high, mid, low

    def body(w, _):
        row = meta[OFFS + 2 * w] & (side - 1)
        col = meta[OFFS + 2 * w + 1] & (side - 1)
        for part in (0, 1):
            turned = pltpu.roll(probe[part], row, 0)
            probes[w, part] = pltpu.roll(turned, col, 1)
        for axis, shift in ((0, row), (1, col)):
            for odd, (c, s, ct, st) in enumerate(table_blocks(shift, half, side)):
                at = 4 * axis + 2 * odd
                tables[w, at, :half, :half] = c.astype(bf)
                tables[w, at, :half, half:] = s.astype(bf)
                tables[w, at, half:, :half] = (-s).astype(bf)
                tables[w, at, half:, half:] = c.astype(bf)
                tables[w, at + 1, :half, :half] = ct.astype(bf)
                tables[w, at + 1, :half, half:] = (-st).astype(bf)
                tables[w, at + 1, half:, :half] = st.astype(bf)
                tables[w, at + 1, half:, half:] = ct.astype(bf)
        a = [dot(x, picks) for x in parts(measured[w])]
        b = [dot(picks_t, x) for x in parts(a[0] + (a[1] + a[2]))]
        amps[w] = b[0] + (b[1] + b[2])
        return 0

    lax.fori_loop(0, windows, body, 0)


def gradient_kernel(
    side,
    windows,
    meta,
    _field,
    _total,
    halo_direct,
    halo_detour,
    halo_relayed,
    halo_even,
    probes,
    tables,
    amps,
    field,
    total,
    rim_direct,
    rim_detour,
    rim_even,
    *rest,
):
    *bands, mixed, terms = rest
    half = side // 2
    wide = field.shape[2]
    tile = wide - side
    bf = jnp.bfloat16
    odd_row = meta[GY_ODD]
    bottom = half + tile
    odd_rows = pl.ds(pl.multiple_of(odd_row * bottom, half), half)
    even_rows = pl.ds(pl.multiple_of((1 - odd_row) * bottom, half), half)
    unpack(meta, halo_direct, halo_detour, halo_relayed, field.at[:, odd_rows, :])
    field[:, even_rows, :] = halo_even[...]
    chunk, lanes = 32, 128
    zero = jnp.float32(0)

    for w in range(windows):
        a, b = meta[OFFS + 2 * w], meta[OFFS + 2 * w + 1]
        live = w < meta[LIVE]
        hi_a, hi_b = (a >= side).astype(jnp.int32), (b >= side).astype(jnp.int32)
        row0, col0 = pl.multiple_of(hi_a * side, side), pl.multiple_of(hi_b * side, side)
        row_in, col_in = a - row0, b - col0
        near = lax.broadcasted_iota(jnp.int32, (chunk, side), 1) >= col_in

        def below(start):
            return (lax.broadcasted_iota(jnp.int32, (chunk, side), 0) + start) >= row_in

        def patch(part, start):
            def at(i, j):
                return field[
                    part,
                    pl.ds(pl.multiple_of(row0 + i * side + start, chunk), chunk),
                    pl.ds(pl.multiple_of(col0 + j * side, side), side),
                ]

            return jnp.where(
                below(start),
                jnp.where(near, at(0, 0), at(0, 1)),
                jnp.where(near, at(1, 0), at(1, 1)),
            )

        def exits(start):
            real, imag = patch(0, start), patch(1, start)
            p_real = probes[w, 0, pl.ds(start, chunk), :]
            p_imag = probes[w, 1, pl.ds(start, chunk), :]
            return p_real * real - p_imag * imag, p_real * imag + p_imag * real

        for i in range(0, half, chunk):
            r0, i0 = exits(i)
            r1, i1 = exits(half + i)
            mixed[0, i : i + chunk, :] = (r0 + r1).astype(bf)
            mixed[0, half + i : half + i + chunk, :] = (i0 + i1).astype(bf)
            mixed[1, i : i + chunk, :] = (r0 - r1).astype(bf)
            mixed[1, half + i : half + i + chunk, :] = (i0 - i1).astype(bf)

        plus, minus = [], []
        for odd in (0, 1):
            h = dot(tables[w, 2 * odd], mixed[odd])
            re0, re1 = h[:half, :half], h[:half, half:]
            im0, im1 = h[half:, :half], h[half:, half:]
            plus.append(jnp.concatenate([re0 + re1, im0 + im1], axis=1).astype(bf))
            minus.append(jnp.concatenate([re0 - re1, im0 - im1], axis=1).astype(bf))

        backs = []
        for odd, sides in ((0, plus), (1, minus)):
            far = dot(jnp.concatenate(sides, axis=0), tables[w, 4 + 2 * odd + 1])
            re, im = far[:, :half], far[:, half:]
            power = jnp.maximum(re * re + im * im, amplitude_floor * amplitude_floor)
            factor = 1.0 - amps[w, :, odd * half : (odd + 1) * half] * lax.rsqrt(power)
            chi = jnp.concatenate([re * factor, im * factor], axis=1).astype(bf)
            backs.append(dot(chi, tables[w, 4 + 2 * odd]))
        left, right = backs[0] + backs[1], backs[0] - backs[1]

        outs = []
        for odd in (0, 1):
            at = slice(odd * half, (odd + 1) * half)
            real = jnp.concatenate([left[at, :half], right[at, :half]], axis=1)
            imag = jnp.concatenate([left[at, half:], right[at, half:]], axis=1)
            stacked = jnp.concatenate([real, imag], axis=0).astype(bf)
            outs.append(dot(tables[w, 2 * odd + 1], stacked))
        upper, lower = outs[0] + outs[1], outs[0] - outs[1]

        never = 2 * side
        cut_row, cut_col = jnp.minimum(row_in // chunk, side // chunk - 1), jnp.minimum(col_in // lanes, side // lanes - 1)
        cut_row, cut_col = pl.multiple_of(cut_row * chunk, chunk), pl.multiple_of(cut_col * lanes, lanes)
        rows_before = jnp.where((cut_row + chunk > row_in) & live, row_in, -1) - cut_row
        cols_before = jnp.where(cut_col + lanes > col_in, col_in, -1) - cut_col
        iota_r = lax.broadcasted_iota(jnp.int32, (chunk, lanes), 0)
        iota_c = lax.broadcasted_iota(jnp.int32, (chunk, lanes), 1)

        def placed(first, size, cut):
            moved = first + size <= cut
            return jnp.where(moved, side, 0) + first, jnp.where(moved, 0, cut) - first

        columns = []
        for first in range(0, side, lanes):
            at, least = placed(first, lanes, col_in)
            columns.append((first, pl.multiple_of(col0 + at, lanes), iota_c >= least))
        columns.append((cut_col, pl.multiple_of(col0 + side + cut_col, lanes), iota_c < cols_before))

        def add(part, row, col, term, keep):
            cells = (part, pl.ds(row, chunk), pl.ds(col, lanes))
            total[cells] = total[cells] + jnp.where(keep, term, zero)

        for start in range(0, side, chunk):
            back = upper if start < half else lower
            at = start % half
            b_real, b_imag = back[at : at + chunk], back[half + at : half + at + chunk]
            p_real = probes[w, 0, pl.ds(start, chunk), :]
            p_imag = probes[w, 1, pl.ds(start, chunk), :]
            both = (p_real * b_real + p_imag * b_imag, p_real * b_imag - p_imag * b_real)
            row, least = placed(start, chunk, row_in)
            row, keep = pl.multiple_of(row0 + row, chunk), iota_r >= jnp.where(live, least, never)
            for part in (0, 1):
                terms[part, start : start + chunk, :] = both[part]
                for first, col, wanted in columns[:-1]:
                    add(part, row, col, both[part][:, first : first + lanes], keep & wanted)
        first, col, wanted = columns[-1]
        for start in range(0, side, chunk):
            row, least = placed(start, chunk, row_in)
            row, keep = pl.multiple_of(row0 + row, chunk), iota_r >= jnp.where(live, least, never)
            for part in (0, 1):
                term = terms[part, start : start + chunk, pl.ds(first, lanes)]
                add(part, row, col, term, keep & wanted)
        row = pl.multiple_of(row0 + side + cut_row, chunk)
        keep = iota_r < rows_before
        for part in (0, 1):
            for first, col, wanted in columns:
                term = terms[part, pl.ds(cut_row, chunk), pl.ds(first, lanes)]
                add(part, row, col, term, keep & wanted)

    pack(total[0, odd_rows, :], total[1, odd_rows, :], rim_direct, rim_detour)
    rim_even[...] = total[:, even_rows, :]
    first = side
    for band_odd, band_even in zip(bands[::2], bands[1::2]):
        rows = slice(first, first + band_odd.shape[1])
        band_odd[...] = total[:, rows, odd_side(meta, band_odd, wide)]
        band_even[...] = total[:, rows, even_side(meta, band_even, wide)]
        first += band_odd.shape[1]


def odd_side(meta, band, wide):
    return pl.ds(pl.multiple_of(meta[GX_ODD] * (wide - band.shape[2]), 128), band.shape[2])


def even_side(meta, band, wide):
    return pl.ds(pl.multiple_of((1 - meta[GX_ODD]) * (wide - band.shape[2]), 128), band.shape[2])


def rim_rows(meta, half):
    odd_row = meta[GY_ODD]
    return (
        pl.ds(pl.multiple_of(odd_row * half, half), half),
        pl.ds(pl.multiple_of((1 - odd_row) * half, half), half),
    )


def both_sides(meta, odd, even, wide):
    return (odd, odd_side(meta, odd, wide)), (even, even_side(meta, even, wide))


def strip(meta, odd, half, tile, margin):
    low = meta[GY_ODD] if odd else 1 - meta[GY_ODD]
    return pl.ds(pl.multiple_of(margin + low * (tile - half), half), half)


def sides_kernel(meta, own, odd_a, odd_b, even_a, even_b, mid_a, mid_b, odd_own):
    tile, half = own.shape[1], odd_a.shape[1]
    for rows, pair in (
        (strip(meta, True, half, tile, 0), (odd_a, odd_b)),
        (strip(meta, False, half, tile, 0), (even_a, even_b)),
        (slice(half, tile - half), (mid_a, mid_b)),
    ):
        for out, cols in both_sides(meta, *pair, tile):
            out[...] = own[:, rows, cols]
    odd_own[...] = own[:, strip(meta, True, half, tile, 0), :]


def edge_kernel(odd, meta, own, side_odd, side_even, *outs):
    *sends, line = outs
    tile, half = own.shape[2], side_odd.shape[2]
    wide = line.shape[2]
    if odd:
        line[:, :, half : half + tile] = own[...]
    else:
        line[:, :, half : half + tile] = own[:, strip(meta, False, half, tile, 0), :]
    for side, cols in both_sides(meta, side_odd, side_even, wide):
        line[:, :, cols] = side[...]
    if odd:
        pack(line[0], line[1], *sends)


def inner_rows(half, tile):
    return (
        (slice(half, 2 * half), slice(0, half)),
        (slice(tile, half + tile), slice(half, 2 * half)),
        slice(2 * half, tile),
    )


def centre_kernel(meta, own, odd_line, even_line, side_odd, side_even, field, total):
    tile, half = own.shape[1], side_odd.shape[2]
    wide = field.shape[2]
    mid = slice(2 * half, tile)
    field[:, strip(meta, True, half, tile, half), :] = odd_line[...]
    field[:, strip(meta, False, half, tile, half), :] = even_line[...]
    field[:, mid, half : half + tile] = own[:, half : tile - half, :]
    for side, cols in both_sides(meta, side_odd, side_even, wide):
        field[:, mid, cols] = side[...]
    total[...] = jnp.zeros_like(total)


def bands_kernel(meta, total, direct, detour, relayed, even, band_odd, band_even, line):
    wide, half = total.shape[2], even.shape[1]
    unpack(meta, direct, detour, relayed, line)
    odd_rows, even_rows = rim_rows(meta, half)
    first, last, _ = inner_rows(half, wide - 2 * half)
    for band, cols in (
        (band_odd, odd_side(meta, band_odd, wide)),
        (band_even, even_side(meta, band_even, wide)),
    ):
        for rows, outer in (first, last):
            band[:, outer, :] = total[:, rows, cols]
        band[:, odd_rows, :] = band[:, odd_rows, :] + line[:, :, cols]
        band[:, even_rows, :] = band[:, even_rows, :] + even[:, :, cols]


def clear_outside(meta, cells, half):
    wide = cells.shape[2]

    @pl.when(meta[EDGE] == 1)
    def _():
        outside = pl.ds(pl.multiple_of(meta[GX_ODD] * (wide - half), half), half)
        cells[:, :, outside] = jnp.zeros((*cells.shape[:2], half), jnp.float32)


def update_edges_kernel(
    meta, field, total, line, even, band_odd, band_even, direct, detour, out_even, lines
):
    wide, half = total.shape[2], even.shape[1]
    odd_rows, even_rows = rim_rows(meta, half)
    first, last, _ = inner_rows(half, wide - 2 * half)
    for rows, outer in (first, last):
        lines[:, outer, :] = field[:, rows, :] - step_size * total[:, rows, :]
    lines[:, odd_rows, :] = lines[:, odd_rows, :] - step_size * line[...]
    lines[:, even_rows, :] = lines[:, even_rows, :] - step_size * even[...]
    for band, cols in (
        (band_odd, odd_side(meta, band_odd, wide)),
        (band_even, even_side(meta, band_even, wide)),
    ):
        lines[:, :, cols] = lines[:, :, cols] - step_size * band[...]
    clear_outside(meta, lines, half)
    pack(lines[0, odd_rows, :], lines[1, odd_rows, :], direct, detour)
    out_even[...] = lines[:, even_rows, :]


def update_centre_kernel(
    meta, field, total, lines, upper_odd, upper_even, lower_odd, lower_even, fresh, zeros
):
    wide, half = total.shape[2], lines.shape[1] // 2
    first, last, mid = inner_rows(half, wide - 2 * half)
    fresh[:, mid, :] = field[:, mid, :] - step_size * total[:, mid, :]
    start = mid.start
    for odd, even in ((upper_odd, upper_even), (lower_odd, lower_even)):
        rows = slice(start, start + odd.shape[1])
        for band, cols in ((odd, odd_side(meta, odd, wide)), (even, even_side(meta, even, wide))):
            fresh[:, rows, cols] = fresh[:, rows, cols] - step_size * band[...]
        start += odd.shape[1]
    clear_outside(meta, fresh.at[:, mid, :], half)
    for rows, outer in (first, last):
        fresh[:, rows, :] = lines[:, outer, :]
    zeros[...] = jnp.zeros_like(zeros)


def almost_final_kernel(meta, field, total, line, even, mid_odd, mid_even, out, part_odd, part_even):
    tile, half = out.shape[1], even.shape[1]
    own = slice(half, half + tile)
    odd_row = meta[GY_ODD]
    far = tile - half
    out[...] = field[:, own, own] - step_size * total[:, own, own]
    for at, rim in ((odd_row * far, line), ((1 - odd_row) * far, even)):
        rows = pl.ds(pl.multiple_of(at, half), half)
        out[:, rows, :] = out[:, rows, :] - step_size * rim[:, :, own]
    for mid, part, cols in (
        (mid_odd, part_odd, odd_side(meta, mid_odd, tile)),
        (mid_even, part_even, even_side(meta, mid_even, tile)),
    ):
        out[:, half:far, cols] = out[:, half:far, cols] - step_size * mid[...]
        part[:, :half, :] = out[:, :half, cols]
        part[:, half:, :] = out[:, far:, cols]


def final_kernel(meta, _, part_odd, part_even, rim_odd, rim_even, out, ready, sems):
    tile, half = out.shape[1], part_odd.shape[2]
    copies = []
    for i, (part, rim, cols) in enumerate(
        (
            (part_odd, rim_odd, odd_side(meta, part_odd, tile)),
            (part_even, rim_even, even_side(meta, part_even, tile)),
        )
    ):
        ready[i] = part[...] - step_size * rim[...]
        for j, first in enumerate((0, tile - half)):
            copies.append(
                pltpu.make_async_copy(
                    ready.at[i, :, pl.ds(j * half, half), :],
                    out.at[:, pl.ds(first, half), cols],
                    sems.at[len(copies)],
                )
            )
            copies[-1].start()
    for copy in copies:
        copy.wait()


def call(kernel, meta, arrays, outs, scratch=(), flops=0, room=0, after=None, aliases=None, far=False):
    f32 = jnp.float32
    shapes = [
        jax.ShapeDtypeStruct(*o) if isinstance(o[0], tuple) else jax.ShapeDtypeStruct(o, f32)
        for o in outs
    ]
    shapes_in = [jax.ShapeDtypeStruct(x.shape, x.dtype) for x in arrays]
    moved = sum(math.prod(x.shape) * x.dtype.itemsize for x in [*shapes_in, *shapes])
    late = [] if after is None else [after]
    smem = pl.BlockSpec(memory_space=pltpu.SMEM)
    vmem = pl.BlockSpec(memory_space=pltpu.VMEM)
    anywhere = pl.BlockSpec(memory_space=pl.ANY)
    return pl.pallas_call(
        kernel,
        out_shape=shapes,
        in_specs=[smem, anywhere if far else vmem, *[vmem] * (len(arrays) - 1), *[anywhere] * len(late)],
        out_specs=[anywhere if far else vmem] * len(shapes),
        scratch_shapes=list(scratch),
        input_output_aliases=aliases or {},
        compiler_params=pltpu.CompilerParams(vmem_limit_bytes=room or min(moved + MIB, 6 * MIB)),
        cost_estimate=pl.CostEstimate(flops=flops, bytes_accessed=moved, transcendentals=0),
    )(meta, *arrays, *late)


def local(object_field, probe_field, measured, offsets, counts):
    tile = object_field.shape[1]
    side = probe_field.shape[1]
    half = side // 2
    windows = offsets.shape[2]
    wide = tile + side
    bf = jnp.bfloat16
    place_col, columns_of_tiles = lax.axis_index("gx"), lax.axis_size("gx")
    odd_col = place_col % 2
    edge = (place_col == 0) | (place_col == columns_of_tiles - 1)
    place_row, rows_of_tiles = lax.axis_index("gy"), lax.axis_size("gy")
    odd_row = place_row % 2
    relay = (place_row == 0) | (place_row == rows_of_tiles - 1)
    places = jnp.stack([odd_col, odd_row, edge.astype(jnp.int32), relay.astype(jnp.int32)])
    meta = jnp.concatenate([places, counts[0], offsets[0, 0].reshape(-1)]).astype(jnp.int32)

    column, band = (2, 2 * half, half), (2, 2 * half, side)
    mid_column, mid_band = (2, tile - 2 * half, half), (2, tile // 2 - half, side)
    whole, lines = (2, wide, wide), (2, 2 * half, wide)
    line = (2, half, wide)
    sends = ((half, wide + CUT), (half, wide - CUT), line)

    block = (2, half, half)
    *sides, odd_own = call(
        sides_kernel,
        places,
        (object_field,),
        (*(block,) * 4, *(mid_column,) * 2, (2, half, tile)),
    )
    odd_sides = swap_columns(*sides[:2])
    even_sides = swap_columns(*sides[2:4])
    mids = swap_columns(*sides[4:])
    *parts, odd_line = call(
        functools.partial(edge_kernel, True),
        meta,
        (odd_own, *odd_sides),
        (*sends[:2], line),
    )
    odd_halo = swap_odd(*parts)
    (even_line,) = call(
        functools.partial(edge_kernel, False), meta, (object_field, *even_sides), (line,)
    )
    halos = (*odd_halo, swap_even(even_line))
    probes, tables, amps = call(
        functools.partial(prepare_kernel, side, windows),
        meta,
        (probe_field, measured[0, 0]),
        ((windows, 2, side, side), ((windows, 8, side, side), bf), (windows, side, side)),
        flops=10**9,
        room=12 * MIB,
    )
    field, total = call(
        centre_kernel, meta, (object_field, odd_line, even_line, *mids), (whole, whole)
    )
    for iteration in range(ITERS):
        last = iteration + 1 == ITERS
        field, total, *rest = call(
            functools.partial(gradient_kernel, side, windows),
            meta,
            (field, total, *halos, probes, tables, amps),
            (whole, whole, *sends, *((mid_column,) * 2 if last else (mid_band,) * 4)),
            scratch=(pltpu.VMEM((2, side, side), bf), pltpu.VMEM((2, side, side), jnp.float32)),
            aliases={1: 0, 2: 1},
            flops=windows * 16 * side**3,
            room=8 * MIB,
        )
        rims = swap_rows(*rest[:3])
        shape = column if last else band
        *bands, odd_line = call(bands_kernel, meta, (total, *rims), (shape, shape, line))
        bands = swap_columns(*bands)
        mids = swap_columns(*rest[3:5])
        if last:
            break
        mids += swap_columns(*rest[5:])
        *edges, rows = call(
            update_edges_kernel,
            meta,
            (field, total, odd_line, rims[3], *bands),
            (*sends, lines),
        )
        halos = swap_rows(*edges)
        field, total = call(
            update_centre_kernel, meta, (field, total, rows, *mids), (whole, whole)
        )
    updated, *parts = call(
        almost_final_kernel,
        meta,
        (field, total, odd_line, rims[3], *mids),
        (object_field.shape, column, column),
    )
    (updated,) = call(
        final_kernel,
        meta,
        (updated, *parts, *bands),
        (object_field.shape,),
        scratch=(pltpu.VMEM((2, *column), jnp.float32), pltpu.SemaphoreType.DMA((4,))),
        aliases={1: 0},
        far=True,
    )
    return updated


def solution(mesh):
    return jax.shard_map(
        local,
        mesh=mesh,
        in_specs=(
            P(None, "gy", "gx"),
            P(),
            P("gy", "gx", None, None, None),
            P("gy", "gx", None, None),
            P("gy", "gx"),
        ),
        out_specs=P(None, "gy", "gx"),
        check_vma=False,
    )
```

```python
import functools
import math

import jax
import jax.numpy as jnp
from jax import lax
from jax.experimental import pallas as pl
from jax.experimental.pallas import tpu as pltpu
from jax.sharding import PartitionSpec as P


ITERS = 2
step_size = 0.25
amplitude_floor = 0.5

MIB = 1 << 20

GX_ODD, GY_ODD, EDGE, RELAY, LIVE, OFFS = 0, 1, 2, 3, 4, 5


def pairs(count, first):
    ups = [(i, i + 1) for i in range(first, count - 1, 2)]
    return ups + [(b, a) for a, b in ups]


def swap_odd(direct, detour):
    count = lax.axis_size("gy")
    low = count // 2 - 1
    far = [(low, low + 1), (low + 1, low)]
    near = [p for p in pairs(count, 1) if p not in far]
    first = lax.ppermute(detour, "gy", near + [(low, 0), (low + 1, count - 1)])
    straight = lax.ppermute(direct, "gy", near + far)
    second = lax.ppermute(first, "gy", [(0, low + 1), (count - 1, low)])
    return straight, first, second


def swap_even(cells):
    return lax.ppermute(cells, "gy", pairs(lax.axis_size("gy"), 0))


def swap_rows(direct, detour, even_cells):
    return *swap_odd(direct, detour), swap_even(even_cells)


def swap_columns(odd_cells, even_cells):
    count = lax.axis_size("gx")
    from_odd = lax.ppermute(odd_cells, "gx", pairs(count, 1))
    from_even = lax.ppermute(even_cells, "gx", pairs(count, 0))
    return from_odd, from_even


CUT = 128


def pack(real, imag, direct, detour):
    wide = real.shape[1]
    direct[:, :wide] = real
    direct[:, wide:] = imag[:, :CUT]
    detour[...] = imag[:, CUT:]


def unpack(meta, direct, detour, relayed, line):
    wide = line.shape[2]
    own = meta[RELAY] == 0
    line[0] = direct[:, :wide]
    line[1, :, :CUT] = direct[:, wide:]
    line[1, :, CUT:] = jnp.where(own, detour[...], jnp.zeros_like(detour)) + relayed[...]


def dot(a, b):
    return jnp.dot(a, b, preferred_element_type=jnp.float32)


def waves(turn, side):
    quarter = side // 4
    moved = turn + quarter // 2
    rest = (moved & (quarter - 1)) - quarter // 2
    which = (moved >> (quarter.bit_length() - 1)) & 3
    x = rest.astype(jnp.float32) * (2.0 * math.pi / side)
    y = x * x
    c = 1.0 + y * (-1 / 2 + y * (1 / 24 + y * (-1 / 720 + y * (1 / 40320))))
    s = x * (1.0 + y * (-1 / 6 + y * (1 / 120 + y * (-1 / 5040 + y * (1 / 362880)))))
    swapped = (which & 1) == 1
    first, second = jnp.where(swapped, s, c), jnp.where(swapped, c, s)
    cos = jnp.where((which == 1) | (which == 2), -first, first)
    sin = jnp.where(which >= 2, -second, second)
    return cos, sin


def table_blocks(shift, half, side):
    freq = 2 * lax.broadcasted_iota(jnp.int32, (half, half), 0)
    cell = lax.broadcasted_iota(jnp.int32, (half, half), 1) - shift
    norm = 1.0 / math.sqrt(side)
    out = []
    for odd in (0, 1):
        c, s = waves((freq + odd) * cell, side)
        c, s = c * norm, s * norm
        out.append((c, s, c.T, s.T))
    return out


def prepare_kernel(side, windows, meta, probe, measured, probes, tables, amps):
    half = side // 2
    bf = jnp.bfloat16
    rows = lax.broadcasted_iota(jnp.int32, (side, side), 0)
    cols = lax.broadcasted_iota(jnp.int32, (side, side), 1)
    place = jnp.where(cols < half, 2 * cols, 2 * (cols - half) + 1)
    picks = (rows == place).astype(jnp.float32).astype(bf)
    place_t = jnp.where(rows < half, 2 * rows, 2 * (rows - half) + 1)
    picks_t = (cols == place_t).astype(jnp.float32).astype(bf)

    def parts(x):
        high = x.astype(bf)
        rest = x - high.astype(jnp.float32)
        mid = rest.astype(bf)
        low = (rest - mid.astype(jnp.float32)).astype(bf)
        return high, mid, low

    def body(w, _):
        row = meta[OFFS + 2 * w] & (side - 1)
        col = meta[OFFS + 2 * w + 1] & (side - 1)
        for part in (0, 1):
            turned = pltpu.roll(probe[part], row, 0)
            probes[w, part] = pltpu.roll(turned, col, 1)
        for axis, shift in ((0, row), (1, col)):
            for odd, (c, s, ct, st) in enumerate(table_blocks(shift, half, side)):
                at = 4 * axis + 2 * odd
                tables[w, at, :half, :half] = c.astype(bf)
                tables[w, at, :half, half:] = s.astype(bf)
                tables[w, at, half:, :half] = (-s).astype(bf)
                tables[w, at, half:, half:] = c.astype(bf)
                tables[w, at + 1, :half, :half] = ct.astype(bf)
                tables[w, at + 1, :half, half:] = (-st).astype(bf)
                tables[w, at + 1, half:, :half] = st.astype(bf)
                tables[w, at + 1, half:, half:] = ct.astype(bf)
        a = [dot(x, picks) for x in parts(measured[w])]
        b = [dot(picks_t, x) for x in parts(a[0] + (a[1] + a[2]))]
        amps[w] = b[0] + (b[1] + b[2])
        return 0

    lax.fori_loop(0, windows, body, 0)


def gradient_kernel(
    side,
    windows,
    meta,
    _field,
    _total,
    halo_direct,
    halo_detour,
    halo_relayed,
    halo_even,
    probes,
    tables,
    amps,
    field,
    total,
    rim_direct,
    rim_detour,
    rim_even,
    *rest,
):
    *bands, mixed, terms = rest
    half = side // 2
    wide = field.shape[2]
    tile = wide - side
    bf = jnp.bfloat16
    odd_row = meta[GY_ODD]
    bottom = half + tile
    odd_rows = pl.ds(pl.multiple_of(odd_row * bottom, half), half)
    even_rows = pl.ds(pl.multiple_of((1 - odd_row) * bottom, half), half)
    unpack(meta, halo_direct, halo_detour, halo_relayed, field.at[:, odd_rows, :])
    field[:, even_rows, :] = halo_even[...]
    chunk, lanes = 32, 128
    zero = jnp.float32(0)

    for w in range(windows):
        a, b = meta[OFFS + 2 * w], meta[OFFS + 2 * w + 1]
        live = w < meta[LIVE]
        hi_a, hi_b = (a >= side).astype(jnp.int32), (b >= side).astype(jnp.int32)
        row0, col0 = pl.multiple_of(hi_a * side, side), pl.multiple_of(hi_b * side, side)
        row_in, col_in = a - row0, b - col0
        near = lax.broadcasted_iota(jnp.int32, (chunk, side), 1) >= col_in

        def below(start):
            return (lax.broadcasted_iota(jnp.int32, (chunk, side), 0) + start) >= row_in

        def patch(part, start):
            def at(i, j):
                return field[
                    part,
                    pl.ds(pl.multiple_of(row0 + i * side + start, chunk), chunk),
                    pl.ds(pl.multiple_of(col0 + j * side, side), side),
                ]

            return jnp.where(
                below(start),
                jnp.where(near, at(0, 0), at(0, 1)),
                jnp.where(near, at(1, 0), at(1, 1)),
            )

        def exits(start):
            real, imag = patch(0, start), patch(1, start)
            p_real = probes[w, 0, pl.ds(start, chunk), :]
            p_imag = probes[w, 1, pl.ds(start, chunk), :]
            return p_real * real - p_imag * imag, p_real * imag + p_imag * real

        for i in range(0, half, chunk):
            r0, i0 = exits(i)
            r1, i1 = exits(half + i)
            mixed[0, i : i + chunk, :] = (r0 + r1).astype(bf)
            mixed[0, half + i : half + i + chunk, :] = (i0 + i1).astype(bf)
            mixed[1, i : i + chunk, :] = (r0 - r1).astype(bf)
            mixed[1, half + i : half + i + chunk, :] = (i0 - i1).astype(bf)

        plus, minus = [], []
        for odd in (0, 1):
            h = dot(tables[w, 2 * odd], mixed[odd])
            re0, re1 = h[:half, :half], h[:half, half:]
            im0, im1 = h[half:, :half], h[half:, half:]
            plus.append(jnp.concatenate([re0 + re1, im0 + im1], axis=1).astype(bf))
            minus.append(jnp.concatenate([re0 - re1, im0 - im1], axis=1).astype(bf))

        backs = []
        for odd, sides in ((0, plus), (1, minus)):
            far = dot(jnp.concatenate(sides, axis=0), tables[w, 4 + 2 * odd + 1])
            re, im = far[:, :half], far[:, half:]
            power = jnp.maximum(re * re + im * im, amplitude_floor * amplitude_floor)
            factor = 1.0 - amps[w, :, odd * half : (odd + 1) * half] * lax.rsqrt(power)
            chi = jnp.concatenate([re * factor, im * factor], axis=1).astype(bf)
            backs.append(dot(chi, tables[w, 4 + 2 * odd]))
        left, right = backs[0] + backs[1], backs[0] - backs[1]

        outs = []
        for odd in (0, 1):
            at = slice(odd * half, (odd + 1) * half)
            real = jnp.concatenate([left[at, :half], right[at, :half]], axis=1)
            imag = jnp.concatenate([left[at, half:], right[at, half:]], axis=1)
            stacked = jnp.concatenate([real, imag], axis=0).astype(bf)
            outs.append(dot(tables[w, 2 * odd + 1], stacked))
        upper, lower = outs[0] + outs[1], outs[0] - outs[1]

        never = 2 * side
        cut_row, cut_col = jnp.minimum(row_in // chunk, side // chunk - 1), jnp.minimum(col_in // lanes, side // lanes - 1)
        cut_row, cut_col = pl.multiple_of(cut_row * chunk, chunk), pl.multiple_of(cut_col * lanes, lanes)
        rows_before = jnp.where((cut_row + chunk > row_in) & live, row_in, -1) - cut_row
        cols_before = jnp.where(cut_col + lanes > col_in, col_in, -1) - cut_col
        iota_r = lax.broadcasted_iota(jnp.int32, (chunk, lanes), 0)
        iota_c = lax.broadcasted_iota(jnp.int32, (chunk, lanes), 1)

        def placed(first, size, cut):
            moved = first + size <= cut
            return jnp.where(moved, side, 0) + first, jnp.where(moved, 0, cut) - first

        columns = []
        for first in range(0, side, lanes):
            at, least = placed(first, lanes, col_in)
            columns.append((first, pl.multiple_of(col0 + at, lanes), iota_c >= least))
        columns.append((cut_col, pl.multiple_of(col0 + side + cut_col, lanes), iota_c < cols_before))

        def add(part, row, col, term, keep):
            cells = (part, pl.ds(row, chunk), pl.ds(col, lanes))
            total[cells] = total[cells] + jnp.where(keep, term, zero)

        for start in range(0, side, chunk):
            back = upper if start < half else lower
            at = start % half
            b_real, b_imag = back[at : at + chunk], back[half + at : half + at + chunk]
            p_real = probes[w, 0, pl.ds(start, chunk), :]
            p_imag = probes[w, 1, pl.ds(start, chunk), :]
            both = (p_real * b_real + p_imag * b_imag, p_real * b_imag - p_imag * b_real)
            row, least = placed(start, chunk, row_in)
            row, keep = pl.multiple_of(row0 + row, chunk), iota_r >= jnp.where(live, least, never)
            for part in (0, 1):
                terms[part, start : start + chunk, :] = both[part]
                for first, col, wanted in columns[:-1]:
                    add(part, row, col, both[part][:, first : first + lanes], keep & wanted)
        first, col, wanted = columns[-1]
        for start in range(0, side, chunk):
            row, least = placed(start, chunk, row_in)
            row, keep = pl.multiple_of(row0 + row, chunk), iota_r >= jnp.where(live, least, never)
            for part in (0, 1):
                term = terms[part, start : start + chunk, pl.ds(first, lanes)]
                add(part, row, col, term, keep & wanted)
        row = pl.multiple_of(row0 + side + cut_row, chunk)
        keep = iota_r < rows_before
        for part in (0, 1):
            for first, col, wanted in columns:
                term = terms[part, pl.ds(cut_row, chunk), pl.ds(first, lanes)]
                add(part, row, col, term, keep & wanted)

    pack(total[0, odd_rows, :], total[1, odd_rows, :], rim_direct, rim_detour)
    rim_even[...] = total[:, even_rows, :]
    first = side
    for band_odd, band_even in zip(bands[::2], bands[1::2]):
        rows = slice(first, first + band_odd.shape[1])
        band_odd[...] = total[:, rows, odd_side(meta, band_odd, wide)]
        band_even[...] = total[:, rows, even_side(meta, band_even, wide)]
        first += band_odd.shape[1]


def odd_side(meta, band, wide):
    return pl.ds(pl.multiple_of(meta[GX_ODD] * (wide - band.shape[2]), 128), band.shape[2])


def even_side(meta, band, wide):
    return pl.ds(pl.multiple_of((1 - meta[GX_ODD]) * (wide - band.shape[2]), 128), band.shape[2])


def rim_rows(meta, half):
    odd_row = meta[GY_ODD]
    return (
        pl.ds(pl.multiple_of(odd_row * half, half), half),
        pl.ds(pl.multiple_of((1 - odd_row) * half, half), half),
    )


def both_sides(meta, odd, even, wide):
    return (odd, odd_side(meta, odd, wide)), (even, even_side(meta, even, wide))


def strip(meta, odd, half, tile, margin):
    low = meta[GY_ODD] if odd else 1 - meta[GY_ODD]
    return pl.ds(pl.multiple_of(margin + low * (tile - half), half), half)


def sides_kernel(meta, own, even_a, even_b, mid_a, mid_b, odd_own):
    tile, half = own.shape[1], even_a.shape[1]
    for rows, pair in (
        (strip(meta, False, half, tile, 0), (even_a, even_b)),
        (slice(half, tile - half), (mid_a, mid_b)),
    ):
        for out, cols in both_sides(meta, *pair, tile):
            out[...] = own[:, rows, cols]
    odd_own[...] = own[:, strip(meta, True, half, tile, 0), :]


def edge_kernel(odd, meta, own, side_odd, side_even, *outs):
    *sends, line = outs
    tile, half = own.shape[2], side_odd.shape[2]
    wide = line.shape[2]
    if odd:
        line[:, :, half : half + tile] = own[...]
    else:
        line[:, :, half : half + tile] = own[:, strip(meta, False, half, tile, 0), :]
    for side, cols in both_sides(meta, side_odd, side_even, wide):
        line[:, :, cols] = side[...]
    if odd:
        pack(line[0], line[1], *sends)


def inner_rows(half, tile):
    return (
        (slice(half, 2 * half), slice(0, half)),
        (slice(tile, half + tile), slice(half, 2 * half)),
        slice(2 * half, tile),
    )


def centre_kernel(meta, own, odd_line, even_line, side_odd, side_even, field, total):
    tile, half = own.shape[1], side_odd.shape[2]
    wide = field.shape[2]
    mid = slice(2 * half, tile)
    field[:, strip(meta, True, half, tile, half), :] = odd_line[...]
    field[:, strip(meta, False, half, tile, half), :] = even_line[...]
    field[:, mid, half : half + tile] = own[:, half : tile - half, :]
    for side, cols in both_sides(meta, side_odd, side_even, wide):
        field[:, mid, cols] = side[...]
    total[...] = jnp.zeros_like(total)


def bands_kernel(meta, total, direct, detour, relayed, even, band_odd, band_even, line):
    wide, half = total.shape[2], even.shape[1]
    unpack(meta, direct, detour, relayed, line)
    odd_rows, even_rows = rim_rows(meta, half)
    first, last, _ = inner_rows(half, wide - 2 * half)
    for band, cols in (
        (band_odd, odd_side(meta, band_odd, wide)),
        (band_even, even_side(meta, band_even, wide)),
    ):
        for rows, outer in (first, last):
            band[:, outer, :] = total[:, rows, cols]
        band[:, odd_rows, :] = band[:, odd_rows, :] + line[:, :, cols]
        band[:, even_rows, :] = band[:, even_rows, :] + even[:, :, cols]


def clear_outside(meta, cells, half):
    wide = cells.shape[2]

    @pl.when(meta[EDGE] == 1)
    def _():
        outside = pl.ds(pl.multiple_of(meta[GX_ODD] * (wide - half), half), half)
        cells[:, :, outside] = jnp.zeros((*cells.shape[:2], half), jnp.float32)


def update_edges_kernel(
    meta, field, total, line, even, band_odd, band_even, direct, detour, out_even, lines
):
    wide, half = total.shape[2], even.shape[1]
    odd_rows, even_rows = rim_rows(meta, half)
    first, last, _ = inner_rows(half, wide - 2 * half)
    for rows, outer in (first, last):
        lines[:, outer, :] = field[:, rows, :] - step_size * total[:, rows, :]
    lines[:, odd_rows, :] = lines[:, odd_rows, :] - step_size * line[...]
    lines[:, even_rows, :] = lines[:, even_rows, :] - step_size * even[...]
    for band, cols in (
        (band_odd, odd_side(meta, band_odd, wide)),
        (band_even, even_side(meta, band_even, wide)),
    ):
        lines[:, :, cols] = lines[:, :, cols] - step_size * band[...]
    clear_outside(meta, lines, half)
    pack(lines[0, odd_rows, :], lines[1, odd_rows, :], direct, detour)
    out_even[...] = lines[:, even_rows, :]


def update_centre_kernel(
    meta, field, total, lines, upper_odd, upper_even, lower_odd, lower_even, fresh, zeros
):
    wide, half = total.shape[2], lines.shape[1] // 2
    first, last, mid = inner_rows(half, wide - 2 * half)
    fresh[:, mid, :] = field[:, mid, :] - step_size * total[:, mid, :]
    start = mid.start
    for odd, even in ((upper_odd, upper_even), (lower_odd, lower_even)):
        rows = slice(start, start + odd.shape[1])
        for band, cols in ((odd, odd_side(meta, odd, wide)), (even, even_side(meta, even, wide))):
            fresh[:, rows, cols] = fresh[:, rows, cols] - step_size * band[...]
        start += odd.shape[1]
    clear_outside(meta, fresh.at[:, mid, :], half)
    for rows, outer in (first, last):
        fresh[:, rows, :] = lines[:, outer, :]
    zeros[...] = jnp.zeros_like(zeros)


def almost_final_kernel(meta, field, total, line, even, mid_odd, mid_even, out, part_odd, part_even):
    tile, half = out.shape[1], even.shape[1]
    own = slice(half, half + tile)
    odd_row = meta[GY_ODD]
    far = tile - half
    out[...] = field[:, own, own] - step_size * total[:, own, own]
    for at, rim in ((odd_row * far, line), ((1 - odd_row) * far, even)):
        rows = pl.ds(pl.multiple_of(at, half), half)
        out[:, rows, :] = out[:, rows, :] - step_size * rim[:, :, own]
    for mid, part, cols in (
        (mid_odd, part_odd, odd_side(meta, mid_odd, tile)),
        (mid_even, part_even, even_side(meta, mid_even, tile)),
    ):
        out[:, half:far, cols] = out[:, half:far, cols] - step_size * mid[...]
        part[:, :half, :] = out[:, :half, cols]
        part[:, half:, :] = out[:, far:, cols]


def final_kernel(meta, _, part_odd, part_even, rim_odd, rim_even, out, ready, sems):
    tile, half = out.shape[1], part_odd.shape[2]
    copies = []
    for i, (part, rim, cols) in enumerate(
        (
            (part_odd, rim_odd, odd_side(meta, part_odd, tile)),
            (part_even, rim_even, even_side(meta, part_even, tile)),
        )
    ):
        ready[i] = part[...] - step_size * rim[...]
        for j, first in enumerate((0, tile - half)):
            copies.append(
                pltpu.make_async_copy(
                    ready.at[i, :, pl.ds(j * half, half), :],
                    out.at[:, pl.ds(first, half), cols],
                    sems.at[len(copies)],
                )
            )
            copies[-1].start()
    for copy in copies:
        copy.wait()


def call(kernel, meta, arrays, outs, scratch=(), flops=0, room=0, after=None, aliases=None, far=False):
    f32 = jnp.float32
    shapes = [
        jax.ShapeDtypeStruct(*o) if isinstance(o[0], tuple) else jax.ShapeDtypeStruct(o, f32)
        for o in outs
    ]
    shapes_in = [jax.ShapeDtypeStruct(x.shape, x.dtype) for x in arrays]
    moved = sum(math.prod(x.shape) * x.dtype.itemsize for x in [*shapes_in, *shapes])
    late = [] if after is None else [after]
    smem = pl.BlockSpec(memory_space=pltpu.SMEM)
    vmem = pl.BlockSpec(memory_space=pltpu.VMEM)
    anywhere = pl.BlockSpec(memory_space=pl.ANY)
    return pl.pallas_call(
        kernel,
        out_shape=shapes,
        in_specs=[smem, anywhere if far else vmem, *[vmem] * (len(arrays) - 1), *[anywhere] * len(late)],
        out_specs=[anywhere if far else vmem] * len(shapes),
        scratch_shapes=list(scratch),
        input_output_aliases=aliases or {},
        compiler_params=pltpu.CompilerParams(vmem_limit_bytes=room or min(moved + MIB, 6 * MIB)),
        cost_estimate=pl.CostEstimate(flops=flops, bytes_accessed=moved, transcendentals=0),
    )(meta, *arrays, *late)


def local(object_field, probe_field, measured, offsets, counts):
    tile = object_field.shape[1]
    side = probe_field.shape[1]
    half = side // 2
    windows = offsets.shape[2]
    wide = tile + side
    bf = jnp.bfloat16
    place_col, columns_of_tiles = lax.axis_index("gx"), lax.axis_size("gx")
    odd_col = place_col % 2
    edge = (place_col == 0) | (place_col == columns_of_tiles - 1)
    place_row, rows_of_tiles = lax.axis_index("gy"), lax.axis_size("gy")
    odd_row = place_row % 2
    relay = (place_row == 0) | (place_row == rows_of_tiles - 1)
    places = jnp.stack([odd_col, odd_row, edge.astype(jnp.int32), relay.astype(jnp.int32)])
    meta = jnp.concatenate([places, counts[0], offsets[0, 0].reshape(-1)]).astype(jnp.int32)

    column, band = (2, 2 * half, half), (2, 2 * half, side)
    mid_column, mid_band = (2, tile - 2 * half, half), (2, tile // 2 - half, side)
    whole, lines = (2, wide, wide), (2, 2 * half, wide)
    line = (2, half, wide)
    sends = ((half, wide + CUT), (half, wide - CUT), line)

    block = (2, half, half)

    def corner(low, right):
        return object_field[:, low * (tile - half) :, right * (tile - half) :][:, :half, :half]

    right, left = [
        jnp.where(odd_row == 1, corner(1, at), corner(0, at)) for at in (1, 0)
    ]
    odd_sides = swap_columns(jnp.where(odd_col == 1, right, left), jnp.where(odd_col == 1, left, right))
    *sides, odd_own = call(
        sides_kernel,
        places,
        (object_field,),
        (block, block, mid_column, mid_column, (2, half, tile)),
    )
    even_sides = swap_columns(*sides[:2])
    mids = swap_columns(*sides[2:])
    *parts, odd_line = call(
        functools.partial(edge_kernel, True),
        meta,
        (odd_own, *odd_sides),
        (*sends[:2], line),
    )
    odd_halo = swap_odd(*parts)
    (even_line,) = call(
        functools.partial(edge_kernel, False), meta, (object_field, *even_sides), (line,)
    )
    halos = (*odd_halo, swap_even(even_line))
    probes, tables, amps = call(
        functools.partial(prepare_kernel, side, windows),
        meta,
        (probe_field, measured[0, 0]),
        ((windows, 2, side, side), ((windows, 8, side, side), bf), (windows, side, side)),
        flops=10**9,
        room=12 * MIB,
    )
    field, total = call(
        centre_kernel, meta, (object_field, odd_line, even_line, *mids), (whole, whole)
    )
    for iteration in range(ITERS):
        last = iteration + 1 == ITERS
        field, total, *rest = call(
            functools.partial(gradient_kernel, side, windows),
            meta,
            (field, total, *halos, probes, tables, amps),
            (whole, whole, *sends, *((mid_column,) * 2 if last else (mid_band,) * 4)),
            scratch=(pltpu.VMEM((2, side, side), bf), pltpu.VMEM((2, side, side), jnp.float32)),
            aliases={1: 0, 2: 1},
            flops=windows * 16 * side**3,
            room=8 * MIB,
        )
        rims = swap_rows(*rest[:3])
        shape = column if last else band
        *bands, odd_line = call(bands_kernel, meta, (total, *rims), (shape, shape, line))
        bands = swap_columns(*bands)
        mids = swap_columns(*rest[3:5])
        if last:
            break
        mids += swap_columns(*rest[5:])
        *edges, rows = call(
            update_edges_kernel,
            meta,
            (field, total, odd_line, rims[3], *bands),
            (*sends, lines),
        )
        halos = swap_rows(*edges)
        field, total = call(
            update_centre_kernel, meta, (field, total, rows, *mids), (whole, whole)
        )
    updated, *parts = call(
        almost_final_kernel,
        meta,
        (field, total, odd_line, rims[3], *mids),
        (object_field.shape, column, column),
    )
    (updated,) = call(
        final_kernel,
        meta,
        (updated, *parts, *bands),
        (object_field.shape,),
        scratch=(pltpu.VMEM((2, *column), jnp.float32), pltpu.SemaphoreType.DMA((4,))),
        aliases={1: 0},
        far=True,
    )
    return updated


def solution(mesh):
    return jax.shard_map(
        local,
        mesh=mesh,
        in_specs=(
            P(None, "gy", "gx"),
            P(),
            P("gy", "gx", None, None, None),
            P("gy", "gx", None, None),
            P("gy", "gx"),
        ),
        out_specs=P(None, "gy", "gx"),
        check_vma=False,
    )
```

```python
import functools
import math

import jax
import jax.numpy as jnp
from jax import lax
from jax.experimental import pallas as pl
from jax.experimental.pallas import tpu as pltpu
from jax.sharding import PartitionSpec as P


ITERS = 2
step_size = 0.25
amplitude_floor = 0.5

MIB = 1 << 20

GX_ODD, GY_ODD, EDGE, RELAY, LIVE, OFFS = 0, 1, 2, 3, 4, 5


def pairs(count, first):
    ups = [(i, i + 1) for i in range(first, count - 1, 2)]
    return ups + [(b, a) for a, b in ups]


def swap_odd(direct, detour):
    count = lax.axis_size("gy")
    low = count // 2 - 1
    far = [(low, low + 1), (low + 1, low)]
    near = [p for p in pairs(count, 1) if p not in far]
    first = lax.ppermute(detour, "gy", near + [(low, 0), (low + 1, count - 1)])
    straight = lax.ppermute(direct, "gy", near + far)
    second = lax.ppermute(first, "gy", [(0, low + 1), (count - 1, low)])
    return straight, first, second


def swap_even(cells):
    return lax.ppermute(cells, "gy", pairs(lax.axis_size("gy"), 0))


def swap_rows(direct, detour, even_cells):
    return *swap_odd(direct, detour), swap_even(even_cells)


def swap_columns(odd_cells, even_cells):
    count = lax.axis_size("gx")
    from_odd = lax.ppermute(odd_cells, "gx", pairs(count, 1))
    from_even = lax.ppermute(even_cells, "gx", pairs(count, 0))
    return from_odd, from_even


CUT = 128


def pack(real, imag, direct, detour):
    wide = real.shape[1]
    direct[:, :wide] = real
    direct[:, wide:] = imag[:, :CUT]
    detour[...] = imag[:, CUT:]


def unpack(meta, direct, detour, relayed, line):
    wide = line.shape[2]
    own = meta[RELAY] == 0
    line[0] = direct[:, :wide]
    line[1, :, :CUT] = direct[:, wide:]
    line[1, :, CUT:] = jnp.where(own, detour[...], jnp.zeros_like(detour)) + relayed[...]


def dot(a, b):
    return jnp.dot(a, b, preferred_element_type=jnp.float32)


def waves(turn, side):
    quarter = side // 4
    moved = turn + quarter // 2
    rest = (moved & (quarter - 1)) - quarter // 2
    which = (moved >> (quarter.bit_length() - 1)) & 3
    x = rest.astype(jnp.float32) * (2.0 * math.pi / side)
    y = x * x
    c = 1.0 + y * (-1 / 2 + y * (1 / 24 + y * (-1 / 720 + y * (1 / 40320))))
    s = x * (1.0 + y * (-1 / 6 + y * (1 / 120 + y * (-1 / 5040 + y * (1 / 362880)))))
    swapped = (which & 1) == 1
    first, second = jnp.where(swapped, s, c), jnp.where(swapped, c, s)
    cos = jnp.where((which == 1) | (which == 2), -first, first)
    sin = jnp.where(which >= 2, -second, second)
    return cos, sin


def table_blocks(shift, half, side):
    freq = 2 * lax.broadcasted_iota(jnp.int32, (half, half), 0)
    cell = lax.broadcasted_iota(jnp.int32, (half, half), 1) - shift
    norm = 1.0 / math.sqrt(side)
    out = []
    for odd in (0, 1):
        c, s = waves((freq + odd) * cell, side)
        c, s = c * norm, s * norm
        out.append((c, s, c.T, s.T))
    return out


def prepare_kernel(side, windows, meta, probe, measured, probes, tables, amps):
    half = side // 2
    bf = jnp.bfloat16
    rows = lax.broadcasted_iota(jnp.int32, (side, side), 0)
    cols = lax.broadcasted_iota(jnp.int32, (side, side), 1)
    place = jnp.where(cols < half, 2 * cols, 2 * (cols - half) + 1)
    picks = (rows == place).astype(jnp.float32).astype(bf)
    place_t = jnp.where(rows < half, 2 * rows, 2 * (rows - half) + 1)
    picks_t = (cols == place_t).astype(jnp.float32).astype(bf)

    def parts(x):
        high = x.astype(bf)
        rest = x - high.astype(jnp.float32)
        mid = rest.astype(bf)
        low = (rest - mid.astype(jnp.float32)).astype(bf)
        return high, mid, low

    def body(w, _):
        row = meta[OFFS + 2 * w] & (side - 1)
        col = meta[OFFS + 2 * w + 1] & (side - 1)
        for part in (0, 1):
            turned = pltpu.roll(probe[part], row, 0)
            probes[w, part] = pltpu.roll(turned, col, 1)
        for axis, shift in ((0, row), (1, col)):
            for odd, (c, s, ct, st) in enumerate(table_blocks(shift, half, side)):
                at = 4 * axis + 2 * odd
                tables[w, at, :half, :half] = c.astype(bf)
                tables[w, at, :half, half:] = s.astype(bf)
                tables[w, at, half:, :half] = (-s).astype(bf)
                tables[w, at, half:, half:] = c.astype(bf)
                tables[w, at + 1, :half, :half] = ct.astype(bf)
                tables[w, at + 1, :half, half:] = (-st).astype(bf)
                tables[w, at + 1, half:, :half] = st.astype(bf)
                tables[w, at + 1, half:, half:] = ct.astype(bf)
        a = [dot(x, picks) for x in parts(measured[w])]
        b = [dot(picks_t, x) for x in parts(a[0] + (a[1] + a[2]))]
        amps[w] = b[0] + (b[1] + b[2])
        return 0

    lax.fori_loop(0, windows, body, 0)


def gradient_kernel(
    side,
    windows,
    meta,
    _field,
    _total,
    halo_direct,
    halo_detour,
    halo_relayed,
    halo_even,
    probes,
    tables,
    amps,
    field,
    total,
    rim_direct,
    rim_detour,
    rim_even,
    *rest,
):
    *bands, mixed, terms = rest
    half = side // 2
    wide = field.shape[2]
    tile = wide - side
    bf = jnp.bfloat16
    odd_row = meta[GY_ODD]
    bottom = half + tile
    odd_rows = pl.ds(pl.multiple_of(odd_row * bottom, half), half)
    even_rows = pl.ds(pl.multiple_of((1 - odd_row) * bottom, half), half)
    unpack(meta, halo_direct, halo_detour, halo_relayed, field.at[:, odd_rows, :])
    field[:, even_rows, :] = halo_even[...]
    chunk, lanes = 32, 128
    zero = jnp.float32(0)

    for w in range(windows):
        a, b = meta[OFFS + 2 * w], meta[OFFS + 2 * w + 1]
        live = w < meta[LIVE]
        hi_a, hi_b = (a >= side).astype(jnp.int32), (b >= side).astype(jnp.int32)
        row0, col0 = pl.multiple_of(hi_a * side, side), pl.multiple_of(hi_b * side, side)
        row_in, col_in = a - row0, b - col0
        near = lax.broadcasted_iota(jnp.int32, (chunk, side), 1) >= col_in

        def below(start):
            return (lax.broadcasted_iota(jnp.int32, (chunk, side), 0) + start) >= row_in

        def patch(part, start):
            def at(i, j):
                return field[
                    part,
                    pl.ds(pl.multiple_of(row0 + i * side + start, chunk), chunk),
                    pl.ds(pl.multiple_of(col0 + j * side, side), side),
                ]

            return jnp.where(
                below(start),
                jnp.where(near, at(0, 0), at(0, 1)),
                jnp.where(near, at(1, 0), at(1, 1)),
            )

        def exits(start):
            real, imag = patch(0, start), patch(1, start)
            p_real = probes[w, 0, pl.ds(start, chunk), :]
            p_imag = probes[w, 1, pl.ds(start, chunk), :]
            return p_real * real - p_imag * imag, p_real * imag + p_imag * real

        for i in range(0, half, chunk):
            r0, i0 = exits(i)
            r1, i1 = exits(half + i)
            mixed[0, i : i + chunk, :] = (r0 + r1).astype(bf)
            mixed[0, half + i : half + i + chunk, :] = (i0 + i1).astype(bf)
            mixed[1, i : i + chunk, :] = (r0 - r1).astype(bf)
            mixed[1, half + i : half + i + chunk, :] = (i0 - i1).astype(bf)

        plus, minus = [], []
        for odd in (0, 1):
            h = dot(tables[w, 2 * odd], mixed[odd])
            re0, re1 = h[:half, :half], h[:half, half:]
            im0, im1 = h[half:, :half], h[half:, half:]
            plus.append(jnp.concatenate([re0 + re1, im0 + im1], axis=1).astype(bf))
            minus.append(jnp.concatenate([re0 - re1, im0 - im1], axis=1).astype(bf))

        backs = []
        for odd, sides in ((0, plus), (1, minus)):
            far = dot(jnp.concatenate(sides, axis=0), tables[w, 4 + 2 * odd + 1])
            re, im = far[:, :half], far[:, half:]
            power = jnp.maximum(re * re + im * im, amplitude_floor * amplitude_floor)
            factor = 1.0 - amps[w, :, odd * half : (odd + 1) * half] * lax.rsqrt(power)
            chi = jnp.concatenate([re * factor, im * factor], axis=1).astype(bf)
            backs.append(dot(chi, tables[w, 4 + 2 * odd]))
        left, right = backs[0] + backs[1], backs[0] - backs[1]

        outs = []
        for odd in (0, 1):
            at = slice(odd * half, (odd + 1) * half)
            real = jnp.concatenate([left[at, :half], right[at, :half]], axis=1)
            imag = jnp.concatenate([left[at, half:], right[at, half:]], axis=1)
            stacked = jnp.concatenate([real, imag], axis=0).astype(bf)
            outs.append(dot(tables[w, 2 * odd + 1], stacked))
        upper, lower = outs[0] + outs[1], outs[0] - outs[1]

        never = 2 * side
        cut_row, cut_col = jnp.minimum(row_in // chunk, side // chunk - 1), jnp.minimum(col_in // lanes, side // lanes - 1)
        cut_row, cut_col = pl.multiple_of(cut_row * chunk, chunk), pl.multiple_of(cut_col * lanes, lanes)
        rows_before = jnp.where((cut_row + chunk > row_in) & live, row_in, -1) - cut_row
        cols_before = jnp.where(cut_col + lanes > col_in, col_in, -1) - cut_col
        iota_r = lax.broadcasted_iota(jnp.int32, (chunk, lanes), 0)
        iota_c = lax.broadcasted_iota(jnp.int32, (chunk, lanes), 1)

        def placed(first, size, cut):
            moved = first + size <= cut
            return jnp.where(moved, side, 0) + first, jnp.where(moved, 0, cut) - first

        columns = []
        for first in range(0, side, lanes):
            at, least = placed(first, lanes, col_in)
            columns.append((first, pl.multiple_of(col0 + at, lanes), iota_c >= least))
        columns.append((cut_col, pl.multiple_of(col0 + side + cut_col, lanes), iota_c < cols_before))

        def add(part, row, col, term, keep):
            cells = (part, pl.ds(row, chunk), pl.ds(col, lanes))
            total[cells] = total[cells] + jnp.where(keep, term, zero)

        for start in range(0, side, chunk):
            back = upper if start < half else lower
            at = start % half
            b_real, b_imag = back[at : at + chunk], back[half + at : half + at + chunk]
            p_real = probes[w, 0, pl.ds(start, chunk), :]
            p_imag = probes[w, 1, pl.ds(start, chunk), :]
            both = (p_real * b_real + p_imag * b_imag, p_real * b_imag - p_imag * b_real)
            row, least = placed(start, chunk, row_in)
            row, keep = pl.multiple_of(row0 + row, chunk), iota_r >= jnp.where(live, least, never)
            for part in (0, 1):
                terms[part, start : start + chunk, :] = both[part]
                for first, col, wanted in columns[:-1]:
                    add(part, row, col, both[part][:, first : first + lanes], keep & wanted)
        first, col, wanted = columns[-1]
        for start in range(0, side, chunk):
            row, least = placed(start, chunk, row_in)
            row, keep = pl.multiple_of(row0 + row, chunk), iota_r >= jnp.where(live, least, never)
            for part in (0, 1):
                term = terms[part, start : start + chunk, pl.ds(first, lanes)]
                add(part, row, col, term, keep & wanted)
        row = pl.multiple_of(row0 + side + cut_row, chunk)
        keep = iota_r < rows_before
        for part in (0, 1):
            for first, col, wanted in columns:
                term = terms[part, pl.ds(cut_row, chunk), pl.ds(first, lanes)]
                add(part, row, col, term, keep & wanted)

    pack(total[0, odd_rows, :], total[1, odd_rows, :], rim_direct, rim_detour)
    rim_even[...] = total[:, even_rows, :]
    first = side
    for band_odd, band_even in zip(bands[::2], bands[1::2]):
        rows = slice(first, first + band_odd.shape[1])
        band_odd[...] = total[:, rows, odd_side(meta, band_odd, wide)]
        band_even[...] = total[:, rows, even_side(meta, band_even, wide)]
        first += band_odd.shape[1]


def odd_side(meta, band, wide):
    return pl.ds(pl.multiple_of(meta[GX_ODD] * (wide - band.shape[2]), 128), band.shape[2])


def even_side(meta, band, wide):
    return pl.ds(pl.multiple_of((1 - meta[GX_ODD]) * (wide - band.shape[2]), 128), band.shape[2])


def rim_rows(meta, half):
    odd_row = meta[GY_ODD]
    return (
        pl.ds(pl.multiple_of(odd_row * half, half), half),
        pl.ds(pl.multiple_of((1 - odd_row) * half, half), half),
    )


def both_sides(meta, odd, even, wide):
    return (odd, odd_side(meta, odd, wide)), (even, even_side(meta, even, wide))


def strip(meta, odd, half, tile, margin):
    low = meta[GY_ODD] if odd else 1 - meta[GY_ODD]
    return pl.ds(pl.multiple_of(margin + low * (tile - half), half), half)


def sides_kernel(meta, own, even_a, even_b, mid_a, mid_b, odd_own):
    tile, half = own.shape[1], even_a.shape[1]
    for rows, pair in (
        (strip(meta, False, half, tile, 0), (even_a, even_b)),
        (slice(half, tile - half), (mid_a, mid_b)),
    ):
        for out, cols in both_sides(meta, *pair, tile):
            out[...] = own[:, rows, cols]
    odd_own[...] = own[:, strip(meta, True, half, tile, 0), :]


def edge_kernel(odd, meta, own, side_odd, side_even, *outs):
    *sends, line = outs
    tile, half = own.shape[2], side_odd.shape[2]
    wide = line.shape[2]
    if odd:
        line[:, :, half : half + tile] = own[...]
    else:
        line[:, :, half : half + tile] = own[:, strip(meta, False, half, tile, 0), :]
    for side, cols in both_sides(meta, side_odd, side_even, wide):
        line[:, :, cols] = side[...]
    if odd:
        pack(line[0], line[1], *sends)


def inner_rows(half, tile):
    return (
        (slice(half, 2 * half), slice(0, half)),
        (slice(tile, half + tile), slice(half, 2 * half)),
        slice(2 * half, tile),
    )


def centre_kernel(meta, own, odd_line, even_line, side_odd, side_even, field, total):
    tile, half = own.shape[1], side_odd.shape[2]
    wide = field.shape[2]
    mid = slice(2 * half, tile)
    field[:, strip(meta, True, half, tile, half), :] = odd_line[...]
    field[:, strip(meta, False, half, tile, half), :] = even_line[...]
    field[:, mid, half : half + tile] = own[:, half : tile - half, :]
    for side, cols in both_sides(meta, side_odd, side_even, wide):
        field[:, mid, cols] = side[...]
    total[...] = jnp.zeros_like(total)


def bands_kernel(meta, total, direct, detour, relayed, even, band_odd, band_even, line):
    wide, half = total.shape[2], even.shape[1]
    unpack(meta, direct, detour, relayed, line)
    odd_rows, even_rows = rim_rows(meta, half)
    first, last, _ = inner_rows(half, wide - 2 * half)
    for band, cols in (
        (band_odd, odd_side(meta, band_odd, wide)),
        (band_even, even_side(meta, band_even, wide)),
    ):
        for rows, outer in (first, last):
            band[:, outer, :] = total[:, rows, cols]
        band[:, odd_rows, :] = band[:, odd_rows, :] + line[:, :, cols]
        band[:, even_rows, :] = band[:, even_rows, :] + even[:, :, cols]


def clear_outside(meta, cells, half):
    wide = cells.shape[2]

    @pl.when(meta[EDGE] == 1)
    def _():
        outside = pl.ds(pl.multiple_of(meta[GX_ODD] * (wide - half), half), half)
        cells[:, :, outside] = jnp.zeros((*cells.shape[:2], half), jnp.float32)


def update_edges_kernel(
    meta, field, total, line, even, band_odd, band_even, direct, detour, out_even, lines
):
    wide, half = total.shape[2], even.shape[1]
    odd_rows, even_rows = rim_rows(meta, half)
    first, last, _ = inner_rows(half, wide - 2 * half)
    for rows, outer in (first, last):
        lines[:, outer, :] = field[:, rows, :] - step_size * total[:, rows, :]
    lines[:, odd_rows, :] = lines[:, odd_rows, :] - step_size * line[...]
    lines[:, even_rows, :] = lines[:, even_rows, :] - step_size * even[...]
    for band, cols in (
        (band_odd, odd_side(meta, band_odd, wide)),
        (band_even, even_side(meta, band_even, wide)),
    ):
        lines[:, :, cols] = lines[:, :, cols] - step_size * band[...]
    clear_outside(meta, lines, half)
    pack(lines[0, odd_rows, :], lines[1, odd_rows, :], direct, detour)
    out_even[...] = lines[:, even_rows, :]


def update_centre_kernel(meta, field, total, lines, mid_odd, mid_even, fresh, zeros):
    wide, half = total.shape[2], lines.shape[1] // 2
    first, last, mid = inner_rows(half, wide - 2 * half)
    fresh[:, mid, :] = field[:, mid, :] - step_size * total[:, mid, :]
    for band, cols in both_sides(meta, mid_odd, mid_even, wide):
        fresh[:, mid, cols] = fresh[:, mid, cols] - step_size * band[...]
    clear_outside(meta, fresh.at[:, mid, :], half)
    for rows, outer in (first, last):
        fresh[:, rows, :] = lines[:, outer, :]
    zeros[...] = jnp.zeros_like(zeros)


def almost_final_kernel(meta, field, total, line, even, mid_odd, mid_even, out, part_odd, part_even):
    tile, half = out.shape[1], even.shape[1]
    own = slice(half, half + tile)
    odd_row = meta[GY_ODD]
    far = tile - half
    out[...] = field[:, own, own] - step_size * total[:, own, own]
    for at, rim in ((odd_row * far, line), ((1 - odd_row) * far, even)):
        rows = pl.ds(pl.multiple_of(at, half), half)
        out[:, rows, :] = out[:, rows, :] - step_size * rim[:, :, own]
    for mid, part, cols in (
        (mid_odd, part_odd, odd_side(meta, mid_odd, tile)),
        (mid_even, part_even, even_side(meta, mid_even, tile)),
    ):
        out[:, half:far, cols] = out[:, half:far, cols] - step_size * mid[...]
        part[:, :half, :] = out[:, :half, cols]
        part[:, half:, :] = out[:, far:, cols]


def final_kernel(meta, _, part_odd, part_even, rim_odd, rim_even, out, ready, sems):
    tile, half = out.shape[1], part_odd.shape[2]
    copies = []
    for i, (part, rim, cols) in enumerate(
        (
            (part_odd, rim_odd, odd_side(meta, part_odd, tile)),
            (part_even, rim_even, even_side(meta, part_even, tile)),
        )
    ):
        ready[i] = part[...] - step_size * rim[...]
        for j, first in enumerate((0, tile - half)):
            copies.append(
                pltpu.make_async_copy(
                    ready.at[i, :, pl.ds(j * half, half), :],
                    out.at[:, pl.ds(first, half), cols],
                    sems.at[len(copies)],
                )
            )
            copies[-1].start()
    for copy in copies:
        copy.wait()


def call(kernel, meta, arrays, outs, scratch=(), flops=0, room=0, after=None, aliases=None, far=False):
    f32 = jnp.float32
    shapes = [
        jax.ShapeDtypeStruct(*o) if isinstance(o[0], tuple) else jax.ShapeDtypeStruct(o, f32)
        for o in outs
    ]
    shapes_in = [jax.ShapeDtypeStruct(x.shape, x.dtype) for x in arrays]
    moved = sum(math.prod(x.shape) * x.dtype.itemsize for x in [*shapes_in, *shapes])
    late = [] if after is None else [after]
    smem = pl.BlockSpec(memory_space=pltpu.SMEM)
    vmem = pl.BlockSpec(memory_space=pltpu.VMEM)
    anywhere = pl.BlockSpec(memory_space=pl.ANY)
    return pl.pallas_call(
        kernel,
        out_shape=shapes,
        in_specs=[smem, anywhere if far else vmem, *[vmem] * (len(arrays) - 1), *[anywhere] * len(late)],
        out_specs=[anywhere if far else vmem] * len(shapes),
        scratch_shapes=list(scratch),
        input_output_aliases=aliases or {},
        compiler_params=pltpu.CompilerParams(vmem_limit_bytes=room or min(moved + MIB, 6 * MIB)),
        cost_estimate=pl.CostEstimate(flops=flops, bytes_accessed=moved, transcendentals=0),
    )(meta, *arrays, *late)


def local(object_field, probe_field, measured, offsets, counts):
    tile = object_field.shape[1]
    side = probe_field.shape[1]
    half = side // 2
    windows = offsets.shape[2]
    wide = tile + side
    bf = jnp.bfloat16
    place_col, columns_of_tiles = lax.axis_index("gx"), lax.axis_size("gx")
    odd_col = place_col % 2
    edge = (place_col == 0) | (place_col == columns_of_tiles - 1)
    place_row, rows_of_tiles = lax.axis_index("gy"), lax.axis_size("gy")
    odd_row = place_row % 2
    relay = (place_row == 0) | (place_row == rows_of_tiles - 1)
    places = jnp.stack([odd_col, odd_row, edge.astype(jnp.int32), relay.astype(jnp.int32)])
    meta = jnp.concatenate([places, counts[0], offsets[0, 0].reshape(-1)]).astype(jnp.int32)

    column, band = (2, 2 * half, half), (2, 2 * half, side)
    mid_column, mid_band = (2, tile - 2 * half, half), (2, tile - 2 * half, side)
    whole, lines = (2, wide, wide), (2, 2 * half, wide)
    line = (2, half, wide)
    sends = ((half, wide + CUT), (half, wide - CUT), line)

    block = (2, half, half)

    def corner(low, right):
        return object_field[:, low * (tile - half) :, right * (tile - half) :][:, :half, :half]

    right, left = [
        jnp.where(odd_row == 1, corner(1, at), corner(0, at)) for at in (1, 0)
    ]
    odd_sides = swap_columns(jnp.where(odd_col == 1, right, left), jnp.where(odd_col == 1, left, right))
    *sides, odd_own = call(
        sides_kernel,
        places,
        (object_field,),
        (block, block, mid_column, mid_column, (2, half, tile)),
    )
    even_sides = swap_columns(*sides[:2])
    mids = swap_columns(*sides[2:])
    *parts, odd_line = call(
        functools.partial(edge_kernel, True),
        meta,
        (odd_own, *odd_sides),
        (*sends[:2], line),
    )
    odd_halo = swap_odd(*parts)
    (even_line,) = call(
        functools.partial(edge_kernel, False), meta, (object_field, *even_sides), (line,)
    )
    halos = (*odd_halo, swap_even(even_line))
    probes, tables, amps = call(
        functools.partial(prepare_kernel, side, windows),
        meta,
        (probe_field, measured[0, 0]),
        ((windows, 2, side, side), ((windows, 8, side, side), bf), (windows, side, side)),
        flops=10**9,
        room=12 * MIB,
    )
    field, total = call(
        centre_kernel, meta, (object_field, odd_line, even_line, *mids), (whole, whole)
    )
    for iteration in range(ITERS):
        last = iteration + 1 == ITERS
        field, total, *rest = call(
            functools.partial(gradient_kernel, side, windows),
            meta,
            (field, total, *halos, probes, tables, amps),
            (whole, whole, *sends, *(mid_column if last else mid_band,) * 2),
            scratch=(pltpu.VMEM((2, side, side), bf), pltpu.VMEM((2, side, side), jnp.float32)),
            aliases={1: 0, 2: 1},
            flops=windows * 16 * side**3,
            room=8 * MIB,
        )
        rims = swap_rows(*rest[:3])
        shape = column if last else band
        *bands, odd_line = call(bands_kernel, meta, (total, *rims), (shape, shape, line))
        bands = swap_columns(*bands)
        mids = swap_columns(*rest[3:5])
        if last:
            break
        *edges, rows = call(
            update_edges_kernel,
            meta,
            (field, total, odd_line, rims[3], *bands),
            (*sends, lines),
        )
        halos = swap_rows(*edges)
        field, total = call(
            update_centre_kernel, meta, (field, total, rows, *mids), (whole, whole)
        )
    updated, *parts = call(
        almost_final_kernel,
        meta,
        (field, total, odd_line, rims[3], *mids),
        (object_field.shape, column, column),
    )
    (updated,) = call(
        final_kernel,
        meta,
        (updated, *parts, *bands),
        (object_field.shape,),
        scratch=(pltpu.VMEM((2, *column), jnp.float32), pltpu.SemaphoreType.DMA((4,))),
        aliases={1: 0},
        far=True,
    )
    return updated


def solution(mesh):
    return jax.shard_map(
        local,
        mesh=mesh,
        in_specs=(
            P(None, "gy", "gx"),
            P(),
            P("gy", "gx", None, None, None),
            P("gy", "gx", None, None),
            P("gy", "gx"),
        ),
        out_specs=P(None, "gy", "gx"),
        check_vma=False,
    )
```

```python
import functools
import math

import jax
import jax.numpy as jnp
from jax import lax
from jax.experimental import pallas as pl
from jax.experimental.pallas import tpu as pltpu
from jax.sharding import PartitionSpec as P


ITERS = 2
step_size = 0.25
amplitude_floor = 0.5

MIB = 1 << 20

GX_ODD, GY_ODD, EDGE, RELAY, LIVE, OFFS = 0, 1, 2, 3, 4, 5


def pairs(count, first):
    ups = [(i, i + 1) for i in range(first, count - 1, 2)]
    return ups + [(b, a) for a, b in ups]


def swap_odd(direct, detour):
    count = lax.axis_size("gy")
    low = count // 2 - 1
    far = [(low, low + 1), (low + 1, low)]
    near = [p for p in pairs(count, 1) if p not in far]
    first = lax.ppermute(detour, "gy", near + [(low, 0), (low + 1, count - 1)])
    straight = lax.ppermute(direct, "gy", near + far)
    second = lax.ppermute(first, "gy", [(0, low + 1), (count - 1, low)])
    return straight, first, second


def swap_even(cells):
    return lax.ppermute(cells, "gy", pairs(lax.axis_size("gy"), 0))


def swap_rows(direct, detour, even_cells):
    return *swap_odd(direct, detour), swap_even(even_cells)


def swap_columns(odd_cells, even_cells):
    count = lax.axis_size("gx")
    from_odd = lax.ppermute(odd_cells, "gx", pairs(count, 1))
    from_even = lax.ppermute(even_cells, "gx", pairs(count, 0))
    return from_odd, from_even


CUT = 128


def pack(real, imag, direct, detour):
    wide = real.shape[1]
    direct[:, :wide] = real
    direct[:, wide:] = imag[:, :CUT]
    detour[...] = imag[:, CUT:]


def unpack(meta, direct, detour, relayed, line):
    wide = line.shape[2]
    own = meta[RELAY] == 0
    line[0] = direct[:, :wide]
    line[1, :, :CUT] = direct[:, wide:]
    line[1, :, CUT:] = jnp.where(own, detour[...], jnp.zeros_like(detour)) + relayed[...]


def dot(a, b):
    return jnp.dot(a, b, preferred_element_type=jnp.float32)


def waves(turn, side):
    quarter = side // 4
    moved = turn + quarter // 2
    rest = (moved & (quarter - 1)) - quarter // 2
    which = (moved >> (quarter.bit_length() - 1)) & 3
    x = rest.astype(jnp.float32) * (2.0 * math.pi / side)
    y = x * x
    c = 1.0 + y * (-1 / 2 + y * (1 / 24 + y * (-1 / 720 + y * (1 / 40320))))
    s = x * (1.0 + y * (-1 / 6 + y * (1 / 120 + y * (-1 / 5040 + y * (1 / 362880)))))
    swapped = (which & 1) == 1
    first, second = jnp.where(swapped, s, c), jnp.where(swapped, c, s)
    cos = jnp.where((which == 1) | (which == 2), -first, first)
    sin = jnp.where(which >= 2, -second, second)
    return cos, sin


def table_blocks(shift, half, side):
    freq = 2 * lax.broadcasted_iota(jnp.int32, (half, half), 0)
    cell = lax.broadcasted_iota(jnp.int32, (half, half), 1) - shift
    norm = 1.0 / math.sqrt(side)
    out = []
    for odd in (0, 1):
        c, s = waves((freq + odd) * cell, side)
        c, s = c * norm, s * norm
        out.append((c, s, c.T, s.T))
    return out


def prepare_kernel(side, windows, meta, probe, measured, probes, tables, amps):
    half = side // 2
    bf = jnp.bfloat16
    rows = lax.broadcasted_iota(jnp.int32, (side, side), 0)
    cols = lax.broadcasted_iota(jnp.int32, (side, side), 1)
    place = jnp.where(cols < half, 2 * cols, 2 * (cols - half) + 1)
    picks = (rows == place).astype(jnp.float32).astype(bf)
    place_t = jnp.where(rows < half, 2 * rows, 2 * (rows - half) + 1)
    picks_t = (cols == place_t).astype(jnp.float32).astype(bf)

    def parts(x):
        high = x.astype(bf)
        rest = x - high.astype(jnp.float32)
        mid = rest.astype(bf)
        low = (rest - mid.astype(jnp.float32)).astype(bf)
        return high, mid, low

    def body(w, _):
        row = meta[OFFS + 2 * w] & (side - 1)
        col = meta[OFFS + 2 * w + 1] & (side - 1)
        for part in (0, 1):
            turned = pltpu.roll(probe[part], row, 0)
            probes[w, part] = pltpu.roll(turned, col, 1)
        for axis, shift in ((0, row), (1, col)):
            for odd, (c, s, ct, st) in enumerate(table_blocks(shift, half, side)):
                at = 4 * axis + 2 * odd
                tables[w, at, :half, :half] = c.astype(bf)
                tables[w, at, :half, half:] = s.astype(bf)
                tables[w, at, half:, :half] = (-s).astype(bf)
                tables[w, at, half:, half:] = c.astype(bf)
                tables[w, at + 1, :half, :half] = ct.astype(bf)
                tables[w, at + 1, :half, half:] = (-st).astype(bf)
                tables[w, at + 1, half:, :half] = st.astype(bf)
                tables[w, at + 1, half:, half:] = ct.astype(bf)
        a = [dot(x, picks) for x in parts(measured[w])]
        b = [dot(picks_t, x) for x in parts(a[0] + (a[1] + a[2]))]
        amps[w] = b[0] + (b[1] + b[2])
        return 0

    lax.fori_loop(0, windows, body, 0)


def gradient_kernel(
    side,
    windows,
    meta,
    _field,
    _total,
    halo_direct,
    halo_detour,
    halo_relayed,
    halo_even,
    probes,
    tables,
    amps,
    field,
    total,
    rim_direct,
    rim_detour,
    rim_even,
    *rest,
):
    *bands, mixed, terms = rest
    half = side // 2
    wide = field.shape[2]
    tile = wide - side
    bf = jnp.bfloat16
    odd_row = meta[GY_ODD]
    bottom = half + tile
    odd_rows = pl.ds(pl.multiple_of(odd_row * bottom, half), half)
    even_rows = pl.ds(pl.multiple_of((1 - odd_row) * bottom, half), half)
    unpack(meta, halo_direct, halo_detour, halo_relayed, field.at[:, odd_rows, :])
    field[:, even_rows, :] = halo_even[...]
    chunk, lanes = 32, 128
    zero = jnp.float32(0)

    for w in range(windows):
        a, b = meta[OFFS + 2 * w], meta[OFFS + 2 * w + 1]
        live = w < meta[LIVE]
        hi_a, hi_b = (a >= side).astype(jnp.int32), (b >= side).astype(jnp.int32)
        row0, col0 = pl.multiple_of(hi_a * side, side), pl.multiple_of(hi_b * side, side)
        row_in, col_in = a - row0, b - col0
        near = lax.broadcasted_iota(jnp.int32, (chunk, side), 1) >= col_in

        def below(start):
            return (lax.broadcasted_iota(jnp.int32, (chunk, side), 0) + start) >= row_in

        def patch(part, start):
            def at(i, j):
                return field[
                    part,
                    pl.ds(pl.multiple_of(row0 + i * side + start, chunk), chunk),
                    pl.ds(pl.multiple_of(col0 + j * side, side), side),
                ]

            return jnp.where(
                below(start),
                jnp.where(near, at(0, 0), at(0, 1)),
                jnp.where(near, at(1, 0), at(1, 1)),
            )

        def exits(start):
            real, imag = patch(0, start), patch(1, start)
            p_real = probes[w, 0, pl.ds(start, chunk), :]
            p_imag = probes[w, 1, pl.ds(start, chunk), :]
            return p_real * real - p_imag * imag, p_real * imag + p_imag * real

        for i in range(0, half, chunk):
            r0, i0 = exits(i)
            r1, i1 = exits(half + i)
            mixed[0, i : i + chunk, :] = (r0 + r1).astype(bf)
            mixed[0, half + i : half + i + chunk, :] = (i0 + i1).astype(bf)
            mixed[1, i : i + chunk, :] = (r0 - r1).astype(bf)
            mixed[1, half + i : half + i + chunk, :] = (i0 - i1).astype(bf)

        plus, minus = [], []
        for odd in (0, 1):
            h = dot(tables[w, 2 * odd], mixed[odd])
            re0, re1 = h[:half, :half], h[:half, half:]
            im0, im1 = h[half:, :half], h[half:, half:]
            plus.append(jnp.concatenate([re0 + re1, im0 + im1], axis=1).astype(bf))
            minus.append(jnp.concatenate([re0 - re1, im0 - im1], axis=1).astype(bf))

        backs = []
        for odd, sides in ((0, plus), (1, minus)):
            far = dot(jnp.concatenate(sides, axis=0), tables[w, 4 + 2 * odd + 1])
            re, im = far[:, :half], far[:, half:]
            power = jnp.maximum(re * re + im * im, amplitude_floor * amplitude_floor)
            factor = 1.0 - amps[w, :, odd * half : (odd + 1) * half] * lax.rsqrt(power)
            chi = jnp.concatenate([re * factor, im * factor], axis=1).astype(bf)
            backs.append(dot(chi, tables[w, 4 + 2 * odd]))
        left, right = backs[0] + backs[1], backs[0] - backs[1]

        outs = []
        for odd in (0, 1):
            at = slice(odd * half, (odd + 1) * half)
            real = jnp.concatenate([left[at, :half], right[at, :half]], axis=1)
            imag = jnp.concatenate([left[at, half:], right[at, half:]], axis=1)
            stacked = jnp.concatenate([real, imag], axis=0).astype(bf)
            outs.append(dot(tables[w, 2 * odd + 1], stacked))
        upper, lower = outs[0] + outs[1], outs[0] - outs[1]

        never = 2 * side
        cut_row, cut_col = jnp.minimum(row_in // chunk, side // chunk - 1), jnp.minimum(col_in // lanes, side // lanes - 1)
        cut_row, cut_col = pl.multiple_of(cut_row * chunk, chunk), pl.multiple_of(cut_col * lanes, lanes)
        rows_before = jnp.where((cut_row + chunk > row_in) & live, row_in, -1) - cut_row
        cols_before = jnp.where(cut_col + lanes > col_in, col_in, -1) - cut_col
        iota_r = lax.broadcasted_iota(jnp.int32, (chunk, lanes), 0)
        iota_c = lax.broadcasted_iota(jnp.int32, (chunk, lanes), 1)

        def placed(first, size, cut):
            moved = first + size <= cut
            return jnp.where(moved, side, 0) + first, jnp.where(moved, 0, cut) - first

        columns = []
        for first in range(0, side, lanes):
            at, least = placed(first, lanes, col_in)
            columns.append((first, pl.multiple_of(col0 + at, lanes), iota_c >= least))
        columns.append((cut_col, pl.multiple_of(col0 + side + cut_col, lanes), iota_c < cols_before))

        def add(part, row, col, term, keep):
            cells = (part, pl.ds(row, chunk), pl.ds(col, lanes))
            total[cells] = total[cells] + jnp.where(keep, term, zero)

        for start in range(0, side, chunk):
            back = upper if start < half else lower
            at = start % half
            b_real, b_imag = back[at : at + chunk], back[half + at : half + at + chunk]
            p_real = probes[w, 0, pl.ds(start, chunk), :]
            p_imag = probes[w, 1, pl.ds(start, chunk), :]
            both = (p_real * b_real + p_imag * b_imag, p_real * b_imag - p_imag * b_real)
            row, least = placed(start, chunk, row_in)
            row, keep = pl.multiple_of(row0 + row, chunk), iota_r >= jnp.where(live, least, never)
            for part in (0, 1):
                terms[part, start : start + chunk, :] = both[part]
                for first, col, wanted in columns[:-1]:
                    add(part, row, col, both[part][:, first : first + lanes], keep & wanted)
        first, col, wanted = columns[-1]
        for start in range(0, side, chunk):
            row, least = placed(start, chunk, row_in)
            row, keep = pl.multiple_of(row0 + row, chunk), iota_r >= jnp.where(live, least, never)
            for part in (0, 1):
                term = terms[part, start : start + chunk, pl.ds(first, lanes)]
                add(part, row, col, term, keep & wanted)
        row = pl.multiple_of(row0 + side + cut_row, chunk)
        keep = iota_r < rows_before
        for part in (0, 1):
            for first, col, wanted in columns:
                term = terms[part, pl.ds(cut_row, chunk), pl.ds(first, lanes)]
                add(part, row, col, term, keep & wanted)

    pack(total[0, odd_rows, :], total[1, odd_rows, :], rim_direct, rim_detour)
    rim_even[...] = total[:, even_rows, :]
    first = side
    for band_odd, band_even in zip(bands[::2], bands[1::2]):
        rows = slice(first, first + band_odd.shape[1])
        band_odd[...] = total[:, rows, odd_side(meta, band_odd, wide)]
        band_even[...] = total[:, rows, even_side(meta, band_even, wide)]
        first += band_odd.shape[1]


def odd_side(meta, band, wide):
    return pl.ds(pl.multiple_of(meta[GX_ODD] * (wide - band.shape[2]), 128), band.shape[2])


def even_side(meta, band, wide):
    return pl.ds(pl.multiple_of((1 - meta[GX_ODD]) * (wide - band.shape[2]), 128), band.shape[2])


def rim_rows(meta, half):
    odd_row = meta[GY_ODD]
    return (
        pl.ds(pl.multiple_of(odd_row * half, half), half),
        pl.ds(pl.multiple_of((1 - odd_row) * half, half), half),
    )


def both_sides(meta, odd, even, wide):
    return (odd, odd_side(meta, odd, wide)), (even, even_side(meta, even, wide))


def strip(meta, odd, half, tile, margin):
    low = meta[GY_ODD] if odd else 1 - meta[GY_ODD]
    return pl.ds(pl.multiple_of(margin + low * (tile - half), half), half)


def sides_kernel(meta, own, rest_odd, rest_even, odd_own):
    tile, half = own.shape[1], rest_odd.shape[2]
    even_rows = strip(meta, False, half, tile, 0)
    for out, cols in both_sides(meta, rest_odd, rest_even, tile):
        out[:, :half, :] = own[:, even_rows, cols]
        out[:, half:, :] = own[:, half : tile - half, cols]
    odd_own[...] = own[:, strip(meta, True, half, tile, 0), :]


def edge_kernel(odd, meta, own, side_odd, side_even, *outs):
    *sends, line = outs
    tile, half = own.shape[2], side_odd.shape[2]
    wide = line.shape[2]
    if odd:
        line[:, :, half : half + tile] = own[...]
    else:
        line[:, :, half : half + tile] = own[:, strip(meta, False, half, tile, 0), :]
    for side, cols in both_sides(meta, side_odd, side_even, wide):
        line[:, :, cols] = side[:, :half, :]
    if odd:
        pack(line[0], line[1], *sends)


def inner_rows(half, tile):
    return (
        (slice(half, 2 * half), slice(0, half)),
        (slice(tile, half + tile), slice(half, 2 * half)),
        slice(2 * half, tile),
    )


def centre_kernel(meta, own, odd_line, even_line, side_odd, side_even, field, total):
    tile, half = own.shape[1], side_odd.shape[2]
    wide = field.shape[2]
    mid = slice(2 * half, tile)
    field[:, strip(meta, True, half, tile, half), :] = odd_line[...]
    field[:, strip(meta, False, half, tile, half), :] = even_line[...]
    field[:, mid, half : half + tile] = own[:, half : tile - half, :]
    for side, cols in both_sides(meta, side_odd, side_even, wide):
        field[:, mid, cols] = side[:, half:, :]
    total[...] = jnp.zeros_like(total)


def bands_kernel(meta, total, direct, detour, relayed, even, band_odd, band_even, line):
    wide, half = total.shape[2], even.shape[1]
    unpack(meta, direct, detour, relayed, line)
    odd_rows, even_rows = rim_rows(meta, half)
    first, last, _ = inner_rows(half, wide - 2 * half)
    for band, cols in (
        (band_odd, odd_side(meta, band_odd, wide)),
        (band_even, even_side(meta, band_even, wide)),
    ):
        for rows, outer in (first, last):
            band[:, outer, :] = total[:, rows, cols]
        band[:, odd_rows, :] = band[:, odd_rows, :] + line[:, :, cols]
        band[:, even_rows, :] = band[:, even_rows, :] + even[:, :, cols]


def clear_outside(meta, cells, half):
    wide = cells.shape[2]

    @pl.when(meta[EDGE] == 1)
    def _():
        outside = pl.ds(pl.multiple_of(meta[GX_ODD] * (wide - half), half), half)
        cells[:, :, outside] = jnp.zeros((*cells.shape[:2], half), jnp.float32)


def update_edges_kernel(
    meta, field, total, line, even, band_odd, band_even, direct, detour, out_even, lines
):
    wide, half = total.shape[2], even.shape[1]
    odd_rows, even_rows = rim_rows(meta, half)
    first, last, _ = inner_rows(half, wide - 2 * half)
    for rows, outer in (first, last):
        lines[:, outer, :] = field[:, rows, :] - step_size * total[:, rows, :]
    lines[:, odd_rows, :] = lines[:, odd_rows, :] - step_size * line[...]
    lines[:, even_rows, :] = lines[:, even_rows, :] - step_size * even[...]
    for band, cols in (
        (band_odd, odd_side(meta, band_odd, wide)),
        (band_even, even_side(meta, band_even, wide)),
    ):
        lines[:, :, cols] = lines[:, :, cols] - step_size * band[...]
    clear_outside(meta, lines, half)
    pack(lines[0, odd_rows, :], lines[1, odd_rows, :], direct, detour)
    out_even[...] = lines[:, even_rows, :]


def update_centre_kernel(
    meta, field, total, lines, upper_odd, upper_even, lower_odd, lower_even, fresh, zeros
):
    wide, half = total.shape[2], lines.shape[1] // 2
    first, last, mid = inner_rows(half, wide - 2 * half)
    fresh[:, mid, :] = field[:, mid, :] - step_size * total[:, mid, :]
    start = mid.start
    for odd, even in ((upper_odd, upper_even), (lower_odd, lower_even)):
        rows = slice(start, start + odd.shape[1])
        for band, cols in ((odd, odd_side(meta, odd, wide)), (even, even_side(meta, even, wide))):
            fresh[:, rows, cols] = fresh[:, rows, cols] - step_size * band[...]
        start += odd.shape[1]
    clear_outside(meta, fresh.at[:, mid, :], half)
    for rows, outer in (first, last):
        fresh[:, rows, :] = lines[:, outer, :]
    zeros[...] = jnp.zeros_like(zeros)


def almost_final_kernel(meta, field, total, line, even, mid_odd, mid_even, out, part_odd, part_even):
    tile, half = out.shape[1], even.shape[1]
    own = slice(half, half + tile)
    odd_row = meta[GY_ODD]
    far = tile - half
    out[...] = field[:, own, own] - step_size * total[:, own, own]
    for at, rim in ((odd_row * far, line), ((1 - odd_row) * far, even)):
        rows = pl.ds(pl.multiple_of(at, half), half)
        out[:, rows, :] = out[:, rows, :] - step_size * rim[:, :, own]
    for mid, part, cols in (
        (mid_odd, part_odd, odd_side(meta, mid_odd, tile)),
        (mid_even, part_even, even_side(meta, mid_even, tile)),
    ):
        out[:, half:far, cols] = out[:, half:far, cols] - step_size * mid[...]
        part[:, :half, :] = out[:, :half, cols]
        part[:, half:, :] = out[:, far:, cols]


def final_kernel(meta, _, part_odd, part_even, rim_odd, rim_even, out, ready, sems):
    tile, half = out.shape[1], part_odd.shape[2]
    copies = []
    for i, (part, rim, cols) in enumerate(
        (
            (part_odd, rim_odd, odd_side(meta, part_odd, tile)),
            (part_even, rim_even, even_side(meta, part_even, tile)),
        )
    ):
        ready[i] = part[...] - step_size * rim[...]
        for j, first in enumerate((0, tile - half)):
            copies.append(
                pltpu.make_async_copy(
                    ready.at[i, :, pl.ds(j * half, half), :],
                    out.at[:, pl.ds(first, half), cols],
                    sems.at[len(copies)],
                )
            )
            copies[-1].start()
    for copy in copies:
        copy.wait()


def call(kernel, meta, arrays, outs, scratch=(), flops=0, room=0, after=None, aliases=None, far=False):
    f32 = jnp.float32
    shapes = [
        jax.ShapeDtypeStruct(*o) if isinstance(o[0], tuple) else jax.ShapeDtypeStruct(o, f32)
        for o in outs
    ]
    shapes_in = [jax.ShapeDtypeStruct(x.shape, x.dtype) for x in arrays]
    moved = sum(math.prod(x.shape) * x.dtype.itemsize for x in [*shapes_in, *shapes])
    late = [] if after is None else [after]
    smem = pl.BlockSpec(memory_space=pltpu.SMEM)
    vmem = pl.BlockSpec(memory_space=pltpu.VMEM)
    anywhere = pl.BlockSpec(memory_space=pl.ANY)
    return pl.pallas_call(
        kernel,
        out_shape=shapes,
        in_specs=[smem, anywhere if far else vmem, *[vmem] * (len(arrays) - 1), *[anywhere] * len(late)],
        out_specs=[anywhere if far else vmem] * len(shapes),
        scratch_shapes=list(scratch),
        input_output_aliases=aliases or {},
        compiler_params=pltpu.CompilerParams(vmem_limit_bytes=room or min(moved + MIB, 6 * MIB)),
        cost_estimate=pl.CostEstimate(flops=flops, bytes_accessed=moved, transcendentals=0),
    )(meta, *arrays, *late)


def local(object_field, probe_field, measured, offsets, counts):
    tile = object_field.shape[1]
    side = probe_field.shape[1]
    half = side // 2
    windows = offsets.shape[2]
    wide = tile + side
    bf = jnp.bfloat16
    place_col, columns_of_tiles = lax.axis_index("gx"), lax.axis_size("gx")
    odd_col = place_col % 2
    edge = (place_col == 0) | (place_col == columns_of_tiles - 1)
    place_row, rows_of_tiles = lax.axis_index("gy"), lax.axis_size("gy")
    odd_row = place_row % 2
    relay = (place_row == 0) | (place_row == rows_of_tiles - 1)
    places = jnp.stack([odd_col, odd_row, edge.astype(jnp.int32), relay.astype(jnp.int32)])
    meta = jnp.concatenate([places, counts[0], offsets[0, 0].reshape(-1)]).astype(jnp.int32)

    column, band = (2, 2 * half, half), (2, 2 * half, side)
    mid_column, mid_band = (2, tile - 2 * half, half), (2, tile // 2 - half, side)
    whole, lines = (2, wide, wide), (2, 2 * half, wide)
    line = (2, half, wide)
    sends = ((half, wide + CUT), (half, wide - CUT), line)

    rest = (2, tile - half, half)

    def corner(low, right):
        return object_field[:, low * (tile - half) :, right * (tile - half) :][:, :half, :half]

    right, left = [
        jnp.where(odd_row == 1, corner(1, at), corner(0, at)) for at in (1, 0)
    ]
    odd_sides = swap_columns(jnp.where(odd_col == 1, right, left), jnp.where(odd_col == 1, left, right))
    *sides, odd_own = call(
        sides_kernel,
        places,
        (object_field,),
        (rest, rest, (2, half, tile)),
    )
    sides = swap_columns(*sides)
    *parts, odd_line = call(
        functools.partial(edge_kernel, True),
        meta,
        (odd_own, *odd_sides),
        (*sends[:2], line),
    )
    odd_halo = swap_odd(*parts)
    (even_line,) = call(
        functools.partial(edge_kernel, False), meta, (object_field, *sides), (line,)
    )
    halos = (*odd_halo, swap_even(even_line))
    probes, tables, amps = call(
        functools.partial(prepare_kernel, side, windows),
        meta,
        (probe_field, measured[0, 0]),
        ((windows, 2, side, side), ((windows, 8, side, side), bf), (windows, side, side)),
        flops=10**9,
        room=12 * MIB,
    )
    field, total = call(
        centre_kernel, meta, (object_field, odd_line, even_line, *sides), (whole, whole)
    )
    for iteration in range(ITERS):
        last = iteration + 1 == ITERS
        field, total, *rest = call(
            functools.partial(gradient_kernel, side, windows),
            meta,
            (field, total, *halos, probes, tables, amps),
            (whole, whole, *sends, *((mid_column,) * 2 if last else (mid_band,) * 4)),
            scratch=(pltpu.VMEM((2, side, side), bf), pltpu.VMEM((2, side, side), jnp.float32)),
            aliases={1: 0, 2: 1},
            flops=windows * 16 * side**3,
            room=8 * MIB,
        )
        rims = swap_rows(*rest[:3])
        shape = column if last else band
        *bands, odd_line = call(bands_kernel, meta, (total, *rims), (shape, shape, line))
        bands = swap_columns(*bands)
        mids = swap_columns(*rest[3:5])
        if last:
            break
        mids += swap_columns(*rest[5:])
        *edges, rows = call(
            update_edges_kernel,
            meta,
            (field, total, odd_line, rims[3], *bands),
            (*sends, lines),
        )
        halos = swap_rows(*edges)
        field, total = call(
            update_centre_kernel, meta, (field, total, rows, *mids), (whole, whole)
        )
    updated, *parts = call(
        almost_final_kernel,
        meta,
        (field, total, odd_line, rims[3], *mids),
        (object_field.shape, column, column),
    )
    (updated,) = call(
        final_kernel,
        meta,
        (updated, *parts, *bands),
        (object_field.shape,),
        scratch=(pltpu.VMEM((2, *column), jnp.float32), pltpu.SemaphoreType.DMA((4,))),
        aliases={1: 0},
        far=True,
    )
    return updated


def solution(mesh):
    return jax.shard_map(
        local,
        mesh=mesh,
        in_specs=(
            P(None, "gy", "gx"),
            P(),
            P("gy", "gx", None, None, None),
            P("gy", "gx", None, None),
            P("gy", "gx"),
        ),
        out_specs=P(None, "gy", "gx"),
        check_vma=False,
    )
```
